32 devices in a mesh: gx: 2 (over core), gy: 4 (over y, x), gz: 4 (over z).
Axes of the slice: x: 2, y: 2, z: 4, core: 2. Of those that a mesh axis runs over, the one named last changes fastest.
Arguments:
- jacobian: bfloat16 [1024, 7, 135, 135], P(('gx', 'gy', 'gz')), may hold values from -6 to 6
- prolong: bfloat16 [1024, 135, 135], P(('gx', 'gy', 'gz')), may hold values from -0.5 to 0.5
- residual: bfloat16 [1024, 135], P(('gx', 'gy', 'gz')), may hold values from -6 to 6
- neighbours: int32 [1024, 6], P(('gx', 'gy', 'gz')), may hold values from -1 to 1023, as said below
- agg_map: int32 [1024], P(('gx', 'gy', 'gz')), may hold values from 0 to 127, as said below
- owners: int32 [128], P(('gx', 'gy', 'gz')), may hold values from 0 to 3, as said below
Outputs:
- coarse: bfloat16 [128, 7, 135, 135], P(('gx', 'gy', 'gz'))
- restricted: bfloat16 [128, 135], P(('gx', 'gy', 'gz'))
The draws below stay inside these ranges and needn't reach their ends.
Inputs may be any that keep to these rules, and one draw needn't show every extreme that they name: `neighbours`: elements form a structured grid of bricks of 4 x 4 x 2 per device, laid out by the device's gx, gy, gz index; inside a device their numbering is an arbitrary permutation. The neighbour in direction -x or +x lies on the same device or on the device one step along gx (likewise y with gy, z with gz); exactly 8, 8 and 16 elements of a device have their x, y and z neighbour of one side off the device or absent. `agg_map`: aggregates are cubes of 2 x 2 x 2 elements of one device's brick; device d holds aggregates d * 4 to (d + 1) * 4 - 1. `owners`: owners are multiples of 1; each device hands exactly 1 of its aggregates to each such owner.
All inputs are finite; a program needn't handle non-finite values.
Results may differ from the reference program's by a relative error of at most 0.0051.
Values may be sent and summed in bfloat16 or wider, within the bound.
A program may use at most 192 MiB of HBM per device.

```python
import jax
import jax.numpy as jnp
from jax import lax

B = 135
LX = 4
LY = 4
LZ = 2
E_DEV = 32
AGG_DEV = 4
SCAP = 1
ELEMS = 1024
CAPO = 4
N_GX = 2
N_GY = 4
N_GZ = 4


def cell_order(key):
    count = LX * LY * LZ
    devices = N_GX * N_GY * N_GZ
    keys = jax.random.split(jax.random.fold_in(key, 11), devices)
    return jax.vmap(lambda single: jax.random.permutation(single, count))(keys).astype(jnp.int32)


def cell_coords():
    count = LX * LY * LZ
    devices = N_GX * N_GY * N_GZ
    device = jnp.arange(devices, dtype=jnp.int32)[:, None]
    cell = jnp.arange(count, dtype=jnp.int32)[None, :]
    coord_x = device // (N_GY * N_GZ) * LX + cell // (LY * LZ)
    coord_y = device // N_GZ % N_GY * LY + cell // LZ % LY
    coord_z = device % N_GZ * LZ + cell % LZ
    return (coord_x, coord_y, coord_z)


def by_local(values, order):
    rows_index = jnp.arange(order.shape[0], dtype=jnp.int32)[:, None]
    return jnp.zeros(values.shape, jnp.int32).at[rows_index, order].set(values)


def draw_neighbours(key, part):
    count = LX * LY * LZ
    devices = N_GX * N_GY * N_GZ
    order = cell_order(key)
    coord_x, coord_y, coord_z = cell_coords()
    columns = []
    for step_x, step_y, step_z in ((-1, 0, 0), (1, 0, 0), (0, -1, 0), (0, 1, 0), (0, 0, -1), (0, 0, 1)):
        moved_x = coord_x + step_x
        moved_y = coord_y + step_y
        moved_z = coord_z + step_z
        inside = (moved_x >= 0) & (moved_x < LX * N_GX) & (moved_y >= 0) & (moved_y < LY * N_GY) & (moved_z >= 0) & (moved_z < LZ * N_GZ)
        moved_x = jnp.clip(moved_x, 0, LX * N_GX - 1)
        moved_y = jnp.clip(moved_y, 0, LY * N_GY - 1)
        moved_z = jnp.clip(moved_z, 0, LZ * N_GZ - 1)
        other_dev = (moved_x // LX * N_GY + moved_y // LY) * N_GZ + moved_z // LZ
        other_cell = (moved_x % LX * LY + moved_y % LY) * LZ + moved_z % LZ
        global_id = other_dev * count + order[other_dev, other_cell]
        columns.append(jnp.where(inside, global_id, -1))
    values = jnp.stack(columns, axis=-1).astype(jnp.int32)
    return by_local(values, order).reshape(devices * count, 6)


def draw_agg_map(key, part):
    count = LX * LY * LZ
    devices = N_GX * N_GY * N_GZ
    order = cell_order(key)
    coord_x, coord_y, coord_z = cell_coords()
    device = jnp.arange(devices, dtype=jnp.int32)[:, None]
    inner = (coord_x % LX // 2 * (LY // 2) + coord_y % LY // 2) * (LZ // 2) + coord_z % LZ // 2
    values = (device * (count // 8) + inner).astype(jnp.int32)
    return by_local(values, order).reshape(devices * count)


def draw_owners(key, part):
    devices = N_GX * N_GY * N_GZ
    keys = jax.random.split(jax.random.fold_in(key, 23), devices)
    listing = (jnp.arange(AGG_DEV, dtype=jnp.int32) // SCAP * (N_GZ // 4)).astype(jnp.int32)

    def single_device(single):
        return listing[jax.random.permutation(single, AGG_DEV)]
    return jax.vmap(single_device)(keys).reshape(-1).astype(jnp.int32)


def block_levels(key, shape, cuts, least, top_value):
    loudness, own = 1.0, jax.random.fold_in(key, 6)
    for dim, shards_of in cuts:
        draws = jnp.exp(jax.random.uniform(jax.random.fold_in(own, dim), (shards_of,), jnp.float32, least / len(cuts), top_value / len(cuts)))
        loudness = loudness * jnp.repeat(draws, shape[dim] // shards_of).reshape([-1 if axis == dim else 1 for axis in range(len(shape))])
    return loudness


def gaussian(key, shape, scale, reach, cuts=(), kind=jnp.bfloat16):
    array = scale * jax.random.normal(key, shape, jnp.float32)
    if cuts:
        array = array * block_levels(key, shape, cuts, -0.22, 0.18)
    return jnp.clip(array, -reach, reach).astype(kind)


def setup_inputs(seed: int = 0) -> dict:
    streams_of = jax.random.split(jax.random.key(seed), 7)
    return {
        "jacobian": gaussian(streams_of[0], (ELEMS, 7, B, B), 1.0, 6.0, ((0, 32),)),
        "prolong": gaussian(streams_of[1], (ELEMS, B, B), B ** -0.5, 0.5, ((0, 32),)),
        "residual": gaussian(streams_of[2], (ELEMS, B), 1.0, 6.0, ((0, 32),)),
        "neighbours": draw_neighbours(jax.random.fold_in(streams_of[6], 71), 0),
        "agg_map": draw_agg_map(jax.random.fold_in(streams_of[6], 71), 0),
        "owners": draw_owners(jax.random.fold_in(streams_of[6], 71), 0),
    }


def device_rows(device, jacobian, prolong, residual, neighbours, agg_map):
    first = (device * E_DEV).astype(jnp.int32)
    jac_dev = lax.dynamic_slice_in_dim(jacobian, first, E_DEV, 0)
    pro_dev = lax.dynamic_slice_in_dim(prolong, first, E_DEV, 0)
    res_dev = lax.dynamic_slice_in_dim(residual, first, E_DEV, 0)
    nbr_dev = lax.dynamic_slice_in_dim(neighbours, first, E_DEV, 0)
    agg_dev = lax.dynamic_slice_in_dim(agg_map, first, E_DEV, 0)
    is_valid = nbr_dev >= 0
    safe_ids = jnp.maximum(nbr_dev, 0)
    beside = jnp.where(is_valid[:, :, None, None], prolong[safe_ids], jnp.zeros((), jnp.bfloat16))
    gathered = jnp.concatenate([pro_dev[:, None], beside], axis=1)
    products = jnp.einsum("edij,edjk->edik", jac_dev.astype(jnp.float32), gathered.astype(jnp.float32)).astype(jnp.bfloat16)
    triple = jnp.einsum("eji,edjk->edik", pro_dev.astype(jnp.float32), products.astype(jnp.float32))
    same_agg = is_valid & (agg_map[safe_ids] == agg_dev[:, None])
    slot_ids = jnp.where(same_agg, 0, jnp.arange(1, 7, dtype=jnp.int32)[None, :])
    slot_ids = jnp.concatenate([jnp.zeros((E_DEV, 1), jnp.int32), slot_ids], axis=1)
    present = jnp.concatenate([jnp.ones((E_DEV, 1), bool), is_valid], axis=1)
    slot_hot = ((slot_ids[:, :, None] == jnp.arange(7, dtype=jnp.int32)) & present[:, :, None]).astype(jnp.float32)
    agg_hot = ((agg_dev - device * AGG_DEV)[:, None] == jnp.arange(AGG_DEV, dtype=jnp.int32)).astype(jnp.float32)
    coarse_rows = jnp.einsum("ea,eds,edik->asik", agg_hot, slot_hot, triple, precision=lax.Precision.HIGHEST)
    per_element = jnp.einsum("eji,ej->ei", pro_dev.astype(jnp.float32), res_dev.astype(jnp.float32))
    restr = jnp.dot(agg_hot.T, per_element, precision=lax.Precision.HIGHEST)
    return coarse_rows.astype(jnp.bfloat16), restr.astype(jnp.bfloat16)


def reference(jacobian, prolong, residual, neighbours, agg_map, owners):
    devices = N_GX * N_GY * N_GZ
    rows_all, restr_all = lax.map(lambda device: device_rows(device, jacobian, prolong, residual, neighbours, agg_map), jnp.arange(devices, dtype=jnp.int32))
    rows_all = rows_all.reshape(devices * AGG_DEV, 7, B, B)
    restr_all = restr_all.reshape(devices * AGG_DEV, B)
    owner_dev = owners.reshape(devices, AGG_DEV)
    counter = jnp.arange(AGG_DEV, dtype=jnp.int32)
    earlier = (owner_dev[:, None, :] == owner_dev[:, :, None]) & (counter[None, None, :] < counter[None, :, None])
    within = jnp.sum(earlier.astype(jnp.int32), axis=-1).reshape(-1)
    source = jnp.arange(devices * AGG_DEV, dtype=jnp.int32) // AGG_DEV
    target = (source // N_GZ) * N_GZ + owners
    row_ids = target * CAPO + (source % N_GZ) * SCAP + within
    coarse = jnp.zeros((devices * CAPO, 7, B, B), jnp.bfloat16).at[row_ids].set(rows_all)
    restricted = jnp.zeros((devices * CAPO, B), jnp.bfloat16).at[row_ids].set(restr_all)
    return coarse, restricted
```

```python
import jax
import jax.numpy as jnp
from jax import lax
from jax.experimental import pallas as pl
from jax.experimental.pallas import tpu as pltpu
from jax.sharding import PartitionSpec as P

LX = 4
LY = 4
LZ = 2
GROUPS = 4
LANES = 128
CHUNK = 4
MESH = pl.DeviceIdType.MESH


def mul(a, b):
    return jnp.dot(a, b, preferred_element_type=jnp.float32)


def lane_ids(shape):
    return lax.broadcasted_iota(jnp.int32, shape, 1)


def channels_of(size_x):
    z = [("gz", 1, LX * LY, 5), ("gz", -1, LX * LY, 4)]
    y = [("gy", 1, LX * LZ, 3), ("gy", -1, LX * LZ, 2)]
    if size_x == 2:
        x = [("gx", 0, LY * LZ, None)]
    else:
        x = [("gx", 1, LY * LZ, 1), ("gx", -1, LY * LZ, 0)]
    return z + y + x


def channel_offsets(channels, elems):
    offsets, at = [], elems
    for _, _, count, _ in channels:
        offsets.append(at)
        at += count
    return offsets, at


def face_rows(count, tall):
    return count * LANES + count * 8 + tall


def partner_bits(me, r):
    high, low = me // 2, me % 2
    high = high + (1 - r // 2) * (1 - 2 * high)
    low = low + (1 - r % 2) * (1 - 2 * low)
    return high * 2 + low


def fused_kernel(table, prolong, jac, residual, sizes, aggs_here):
    width, elems, _ = prolong.shape
    sides = jac.shape[0]
    size_x, size_y, size_z = sizes
    rest = width - LANES
    tall = pl.cdiv(width + 1, 8) * 8
    full = pl.cdiv(width + 1, 16) * 16
    pitch = elems + 1
    per_owner = aggs_here // GROUPS
    stride_z = size_z // GROUPS
    out_slots = size_z * per_owner
    members = elems // aggs_here
    on_face = members // 2
    channels = channels_of(size_x)
    offsets, zero_block = channel_offsets(channels, elems)
    nch = len(channels)
    tail = sides * LANES
    msg_rows = tail + LANES
    half = LANES // 2
    most = max(count for _, _, count, _ in channels)
    pieces = sides + 1
    step_rows = 5 if width % 5 == 0 else 1

    def kernel(table_ref, p_hbm, j_hbm, res_ref, rows_ref, *refs):
        praw, jraw, near, far, pool, pt, jm = refs[:7]
        sends, recvs = refs[7 : 7 + nch], refs[7 + nch : 7 + 2 * nch]
        remf, farf, msg, msg_rem, msg_far, racc, acc = refs[7 + 2 * nch : 14 + 2 * nch]
        p_sem, j_sem, f_send, f_recv, r_send, r_recv, self_sem = refs[14 + 2 * nch :]
        me = {"gx": lax.axis_index("gx"), "gy": lax.axis_index("gy"), "gz": lax.axis_index("gz")}
        size = {"gx": size_x, "gy": size_y, "gz": size_z}
        me_z = me["gz"]

        p_copy = pltpu.make_async_copy(p_hbm, praw, p_sem)
        p_copy.start()

        def j_copy(k):
            return pltpu.make_async_copy(j_hbm.at[k], jraw.at[k], j_sem.at[k])

        for k in range(sides):
            j_copy(k).start()

        barrier = pltpu.get_barrier_semaphore()
        for step in range(1, size_z):
            to = lax.rem(me_z + step, size_z)
            pl.semaphore_signal(barrier, inc=1, device_id={"gz": to}, device_id_type=MESH)
        expected = size_z - 1
        if size_x == 2:
            pl.semaphore_signal(
                barrier, inc=1, device_id={"gx": 1 - me["gx"]}, device_id_type=MESH
            )
            expected = expected + 1
        for axis in ["gy"] + (["gx"] if size_x > 2 else []):
            for step in (1, -1):
                there = me[axis] + step
                exists = (there >= 0) & (there < size[axis])

                @pl.when(exists)
                def _(axis=axis, there=there):
                    pl.semaphore_signal(
                        barrier, inc=1, device_id={axis: there}, device_id_type=MESH
                    )

                expected = expected + exists.astype(jnp.int32)

        msg_far[...] = jnp.zeros_like(msg_far)
        pool[zero_block] = jnp.zeros(pool.shape[1:], pool.dtype)

        def spread(load, last):
            @pl.loop(0, width // step_rows)
            def _(c):
                part = load(c).astype(jnp.float32)
                for i in range(step_rows):
                    rows = pl.ds((c * step_rows + i) * pitch, elems)
                    near[rows, :] = part[i, :, :LANES]
                    far[rows, :rest] = part[i, :, LANES:]

            near[pl.ds(width * pitch, elems), :] = last[:, :LANES]
            far[pl.ds(width * pitch, elems), :rest] = last[:, LANES:]

        def block(e):
            rows = pl.ds(e, width + 1, stride=pitch)
            right = far[rows, :]
            right = jnp.where(lane_ids(right.shape) < rest, right, 0.0)
            both = jnp.concatenate([near[rows, :], right], axis=1)[:, :full]
            below = jnp.zeros((full - width - 1, full), jnp.float32)
            return jnp.concatenate([both, below], axis=0)

        p_copy.wait()
        spread(
            lambda c: praw[pl.ds(c * step_rows, step_rows)],
            jnp.zeros((elems, width), jnp.float32),
        )

        @pl.loop(0, elems // 4)
        def _(group):
            for u in range(4):
                e = group * 4 + u
                whole = block(e)
                pool[e] = whole[:, :width].astype(pool.dtype)
                pt[e] = whole.T[:tall].astype(pt.dtype)

        pl.semaphore_wait(barrier, expected)

        def face_target(c):
            axis, step, _, _ = channels[c]
            return {axis: 1 - me[axis] if step == 0 else me[axis] + step}

        def when_sent(c):
            axis, step, _, _ = channels[c]
            if step == 0:
                return lambda f: f()
            there = me[axis] + step
            return pl.when((there >= 0) & (there < size[axis]))

        def when_received(c):
            axis, step, _, _ = channels[c]
            if step == 0:
                return lambda f: f()
            there = me[axis] - step
            return pl.when((there >= 0) & (there < size[axis]))

        def face_parts(c):
            count = channels[c][2]
            parts = [(n * LANES, CHUNK * LANES) for n in range(0, count, CHUNK)]
            return parts + [(count * LANES, count * 8 + full)]

        def face_copy(c, part):
            start, rows = face_parts(c)[part]
            return pltpu.make_async_remote_copy(
                src_ref=sends[c].at[pl.ds(start, rows)],
                dst_ref=recvs[c].at[pl.ds(start, rows)],
                send_sem=f_send.at[c, part],
                recv_sem=f_recv.at[c, part],
                device_id=face_target(c),
                device_id_type=MESH,
            )

        def pack(c, n):
            whole = pool[table_ref[c, n]]
            sends[c][n * LANES : (n + 1) * LANES, :] = whole[:LANES, :LANES]
            remf[c, n * 8 : (n + 1) * 8, :] = whole[LANES:tall, :LANES].astype(jnp.float32)
            farf[c, :, n * rest : (n + 1) * rest] = whole[:, LANES:width].astype(jnp.float32)

        def pack_tail(c):
            count = channels[c][2]
            at = count * LANES
            sends[c][at : at + count * 8, :] = remf[c, : count * 8, :].astype(jnp.bfloat16)
            sends[c][at + count * 8 : at + count * 8 + full, :] = farf[c].astype(jnp.bfloat16)

        def send_faces(group):
            parts = max(len(face_parts(c)) for c in group)
            for part in range(parts):
                for c in group:
                    if part < len(face_parts(c)):
                        if part < len(face_parts(c)) - 1:
                            for n in range(part * CHUNK, (part + 1) * CHUNK):
                                pack(c, n)
                        else:
                            pack_tail(c)

                        @when_sent(c)
                        def _(c=c, part=part):
                            face_copy(c, part).start()

        def take_faces(group):
            for c in group:

                @when_received(c)
                def _(c=c):
                    for part in range(len(face_parts(c))):
                        face_copy(c, part).wait_recv()
                    count = channels[c][2]
                    at = count * LANES
                    remf[c, : count * 8, :] = recvs[c][at : at + count * 8, :].astype(jnp.float32)
                    farf[c] = recvs[c][at + count * 8 : at + count * 8 + full, :].astype(
                        jnp.float32
                    )
                    for n in range(count):
                        to = offsets[c] + n
                        pool[to, :LANES, :LANES] = recvs[c][n * LANES : (n + 1) * LANES, :]
                        below = remf[c, n * 8 : (n + 1) * 8, :]
                        below = jnp.concatenate([below, jnp.zeros_like(below)], axis=0)
                        pool[to, LANES:full, :LANES] = below.astype(pool.dtype)
                        pool[to, :, LANES:width] = farf[
                            c, :, n * rest : (n + 1) * rest
                        ].astype(pool.dtype)

        send_faces([0, 1])
        send_faces(list(range(2, nch)))

        @pl.loop(0, sides)
        def _(k):
            j_copy(k).wait()
            own = (k == 0).astype(jnp.float32)
            spread(
                lambda c: jraw[k, pl.ds(c * step_rows, step_rows)],
                res_ref[...].astype(jnp.float32) * own,
            )

            @pl.loop(0, elems // 4)
            def _(group):
                for u in range(4):
                    e = group * 4 + u
                    jm[k, e] = block(e).astype(jm.dtype)

        my_group = me_z // stride_z

        def target_of(r):
            return partner_bits(my_group, r // per_owner) * stride_z

        def slot_of(z, r):
            return z * per_owner + r % per_owner

        def row_copy(r, piece):
            at = pl.ds(pl.multiple_of(piece * LANES, LANES), LANES)
            slot = slot_of(me_z, r)
            return pltpu.make_async_remote_copy(
                src_ref=msg.at[r, at],
                dst_ref=rows_ref.at[slot, at],
                send_sem=r_send.at[r, piece],
                recv_sem=r_recv.at[slot, piece],
                device_id={"gz": target_of(r)},
                device_id_type=MESH,
            )

        def send_row(r, piece):
            @pl.when(target_of(r) != me_z)
            def _():
                row_copy(r, piece).start()

        def emit(r, s, value):
            msg[r, s * LANES : (s + 1) * LANES, :] = value[:LANES, :LANES].astype(msg.dtype)
            msg_rem[r, s * 8 : (s + 1) * 8, :] = value[LANES:tall, :LANES]
            msg_far[r, :, s * rest : (s + 1) * rest] = value[:, LANES:width]
            send_row(r, s)

        def side_sum(r, d):
            total = None
            for m in range(on_face):
                code = table_ref[nch + 1 + d, r * on_face + m]
                e, n = code % elems, code // elems
                product = mul(jm[1 + d, e], pool[n]).astype(jnp.bfloat16)
                triple = mul(pt[e], product)
                total = triple if total is None else total + triple
            return total

        @pl.loop(0, aggs_here)
        def _(r):
            acc[...] = jnp.zeros_like(acc)
            racc[...] = jnp.zeros_like(racc)

            @pl.loop(0, members // 2)
            def _(pair):
                total = None
                for u in range(2):
                    code = table_ref[nch, r * members + pair * 2 + u]
                    e, code = code % elems, code // elems
                    product = mul(jm[0, e], pool[e])
                    for axis in range(3):
                        x, code = code % (2 * elems), code // (2 * elems)
                        k = 1 + 2 * axis + x // elems
                        product = product + mul(jm[k, e], pool[x % elems])
                    racc[...] += product[LANES:tall]
                    triple = mul(pt[e], product.astype(jnp.bfloat16))
                    total = triple if total is None else total + triple
                acc[...] += total

            below = racc[...]
            spare = lax.broadcasted_iota(jnp.int32, below.shape, 0) == width - LANES
            acc[LANES:tall, :] += jnp.where(spare, below, 0.0)
            emit(r, 0, acc[...])

        take_faces(list(range(2, nch)))

        @pl.loop(0, aggs_here)
        def _(r):
            for d in range(sides - 3):
                emit(r, 1 + d, side_sum(r, d))

        take_faces([0, 1])

        @pl.loop(0, aggs_here)
        def _(r):
            for d in range(sides - 3, sides - 1):
                emit(r, 1 + d, side_sum(r, d))
            msg_rem[r, sides * 8 : (sides + 1) * 8, :] = msg_far[r, LANES:tall, :]
            msg[r, tail : tail + half, :] = msg_rem[r].astype(msg.dtype)
            right = pltpu.roll(msg_far[r, half:LANES, :], half, 1)
            left = msg_far[r, :half, :]
            folded = jnp.where(lane_ids(left.shape) < half, left, right)
            msg[r, tail + half : msg_rows, :] = folded.astype(msg.dtype)
            send_row(r, sides)

        def self_copy(r):
            return pltpu.make_async_copy(
                msg.at[r], rows_ref.at[slot_of(me_z, r)], self_sem.at[r % per_owner]
            )

        for sub in range(per_owner):
            r = aggs_here - per_owner + sub

            @pl.when(target_of(r) == me_z)
            def _(r=r):
                self_copy(r).start()

        for c in range(nch):

            @when_sent(c)
            def _(c=c):
                for part in range(len(face_parts(c))):
                    face_copy(c, part).wait_send()

        @pl.loop(0, aggs_here)
        def _(r):
            @pl.when(target_of(r) != me_z)
            def _():
                for piece in range(pieces):
                    row_copy(r, piece).wait_send()

        def row_arrival(slot, piece):
            at = pl.ds(piece * LANES, LANES)
            return pltpu.make_async_remote_copy(
                src_ref=msg.at[0, at],
                dst_ref=rows_ref.at[slot, at],
                send_sem=r_send.at[0, piece],
                recv_sem=r_recv.at[slot, piece],
                device_id={"gz": me_z},
                device_id_type=MESH,
            )

        owner = me_z % stride_z == 0

        @pl.when(owner)
        def _():
            @pl.loop(0, out_slots)
            def _(slot):
                @pl.when(slot // per_owner != me_z)
                def _():
                    for piece in range(pieces):
                        row_arrival(slot, piece).wait_recv()

        if stride_z > 1:

            @pl.when(jnp.logical_not(owner))
            def _():
                rows_ref[...] = jnp.zeros_like(rows_ref)

        for sub in range(per_owner):
            r = aggs_here - per_owner + sub

            @pl.when(target_of(r) == me_z)
            def _(r=r):
                self_copy(r).wait()

    bf16, f32 = jnp.bfloat16, jnp.float32
    spread_rows = (width + 1) * pitch
    faces = [pltpu.VMEM((face_rows(count, full), LANES), bf16) for _, _, count, _ in channels]
    parts = most // CHUNK + 1
    scratch = [
        pltpu.VMEM((width, elems, width), bf16),
        pltpu.VMEM((sides, width, elems, width), bf16),
        pltpu.VMEM((spread_rows, LANES), f32),
        pltpu.VMEM((spread_rows, LANES), f32),
        pltpu.VMEM((zero_block + 1, full, width), bf16),
        pltpu.VMEM((elems, tall, full), bf16),
        pltpu.VMEM((sides, elems, full, full), bf16),
        *faces,
        *faces,
        pltpu.VMEM((nch, most * 8, LANES), f32),
        pltpu.VMEM((nch, full, LANES), f32),
        pltpu.VMEM((aggs_here, msg_rows, LANES), bf16),
        pltpu.VMEM((aggs_here, (sides + 1) * 8, LANES), f32),
        pltpu.VMEM((aggs_here, tall, LANES), f32),
        pltpu.VMEM((8, width), f32),
        pltpu.VMEM((tall, width), f32),
        pltpu.SemaphoreType.DMA,
        pltpu.SemaphoreType.DMA((sides,)),
        pltpu.SemaphoreType.DMA((nch, parts)),
        pltpu.SemaphoreType.DMA((nch, parts)),
        pltpu.SemaphoreType.DMA((aggs_here, pieces)),
        pltpu.SemaphoreType.DMA((out_slots, pieces)),
        pltpu.SemaphoreType.DMA((per_owner,)),
    ]
    return pl.pallas_call(
        kernel,
        in_specs=[
            pl.BlockSpec(memory_space=pltpu.SMEM),
            pl.BlockSpec(memory_space=pl.ANY),
            pl.BlockSpec(memory_space=pl.ANY),
            pl.BlockSpec(memory_space=pltpu.VMEM),
        ],
        out_specs=pl.BlockSpec(memory_space=pltpu.VMEM),
        out_shape=jax.ShapeDtypeStruct((out_slots, msg_rows, LANES), bf16),
        scratch_shapes=scratch,
        compiler_params=pltpu.CompilerParams(
            collective_id=0, has_side_effects=True, vmem_limit_bytes=62 << 20
        ),
    )(table, prolong, jac, residual)


def tables(neighbours, agg_map, owners, device, elems, sizes):
    size_x, _, size_z = sizes
    aggs_here = owners.shape[0]
    per_owner = aggs_here // GROUPS
    stride_z = size_z // GROUPS
    members = elems // aggs_here
    on_face = members // 2
    channels = channels_of(size_x)
    offsets, zero_block = channel_offsets(channels, elems)
    most = max(count for _, _, count, _ in channels)
    nbr = neighbours.T
    local = nbr - device * elems
    here = (local >= 0) & (local < elems)
    valid = nbr >= 0
    ids = jnp.arange(elems, dtype=jnp.int32)
    agg = agg_map - device * aggs_here
    before = ids[None, :] < ids[:, None]

    away = jnp.logical_not(here)
    rank = jnp.sum((away[:, None, :] & before[None]).astype(jnp.int32), axis=2)
    places = jnp.arange(most, dtype=jnp.int32)
    chosen = away[:, None, :] & (rank[:, None, :] == places[None, :, None])
    by_side = jnp.sum(jnp.where(chosen, ids, 0), axis=2)

    away_valid = away & valid
    lower = away_valid[:, None, :] & (nbr[:, None, :] < nbr[:, :, None])
    position = jnp.sum(lower.astype(jnp.int32), axis=2)
    x_from = [4, 4] if size_x == 2 else [4, 5]
    source = jnp.array([offsets[c] for c in x_from + [2, 3, 0, 1]], jnp.int32)[:, None]
    index = jnp.where(here, local, source + position)
    index = jnp.where(valid, index, zero_block)
    near_agg = jnp.sum(jnp.where(local[:, :, None] == ids, agg, 0), axis=2)
    same = here & (near_agg == agg[None, :])

    count = jnp.arange(aggs_here, dtype=jnp.int32)
    earlier = (owners[None, :] == owners[:, None]) & (count[None, :] < count[:, None])
    within = jnp.sum(earlier.astype(jnp.int32), axis=1)
    mine = lax.axis_index("gz") // stride_z
    to = owners // stride_z
    turn = 3 - (2 * jnp.abs(to // 2 - mine // 2) + jnp.abs(to % 2 - mine % 2))
    order = turn * per_owner + within
    order_e = jnp.sum(jnp.where(agg[:, None] == count, order, 0), axis=1)

    together = before & (order_e[None, :] == order_e[:, None])
    m_place = order_e * members + jnp.sum(together.astype(jnp.int32), axis=1)
    inner = [
        jnp.where(same[2 * a + 1], elems + local[2 * a + 1], local[2 * a]) for a in range(3)
    ]
    wide = 2 * elems
    m_code = ids + elems * (inner[0] + wide * (inner[1] + wide * inner[2]))
    m_row = jnp.sum(jnp.where(m_place[None, :] == ids[:, None], m_code, 0), axis=1)

    outer = jnp.logical_not(same)
    s_rank = jnp.sum((outer[:, None, :] & together[None]).astype(jnp.int32), axis=2)
    s_place = jnp.where(outer, order_e * on_face + s_rank, -1)
    slots = jnp.arange(aggs_here * on_face, dtype=jnp.int32)
    s_code = ids + elems * index
    s_hit = s_place[:, None, :] == slots[None, :, None]
    s_rows = jnp.sum(jnp.where(s_hit, s_code[:, None, :], 0), axis=2)

    if size_x == 2:
        swap = jnp.where(lax.axis_index("gx") == 0, by_side[1], by_side[0])
        picks = jnp.stack([by_side[5], by_side[4], by_side[3], by_side[2], swap])
    else:
        picks = by_side[::-1][jnp.array([0, 1, 2, 3, 4, 5])]

    def padded(rows):
        return jnp.pad(rows, ((0, 0), (0, elems - rows.shape[1])))

    return jnp.concatenate([padded(picks), m_row[None], padded(s_rows)], axis=0)


def body(jacobian, prolong, residual, neighbours, agg_map, owners):
    elems = jacobian.shape[0]
    sides = jacobian.shape[1]
    width = prolong.shape[1]
    aggs_here = owners.shape[0]
    rest = width - LANES
    half = LANES // 2
    sizes = tuple(lax.axis_size(a) for a in ("gx", "gy", "gz"))
    place = tuple(lax.axis_index(a) for a in ("gx", "gy", "gz"))
    device = (place[0] * sizes[1] + place[1]) * sizes[2] + place[2]
    table = tables(neighbours, agg_map, owners, device, elems, sizes)
    jac = jnp.transpose(jacobian, (1, 2, 0, 3))
    pro = jnp.transpose(prolong, (1, 0, 2))
    rows = fused_kernel(table, pro, jac, residual, sizes, aggs_here)

    tail = sides * LANES
    slots = rows.shape[0]
    head = rows[:, :tail].reshape(slots, sides, LANES, LANES)
    below = rows[:, tail : tail + sides * 8].reshape(slots, sides, 8, LANES)
    last = rows[:, tail + sides * 8 : tail + half]
    folded = rows[:, tail + half :]
    used = sides * rest
    far = jnp.concatenate(
        [folded[:, :, :used], folded[:, :, half : half + used], last[:, :rest, :used]], axis=1
    )
    far = far.reshape(slots, width, sides, rest).transpose(0, 2, 1, 3)
    heads = jnp.concatenate([head, below[:, :, :rest]], axis=2)
    coarse = jnp.concatenate([heads, far], axis=3)
    restricted = jnp.concatenate([below[:, 0, rest], last[:, rest, :rest]], axis=1)
    return coarse, restricted


def solution(mesh):
    spec = P(("gx", "gy", "gz"))
    return jax.shard_map(
        body,
        mesh=mesh,
        in_specs=(spec,) * 6,
        out_specs=(spec, spec),
        check_vma=False,
    )
```

```python
import jax
import jax.numpy as jnp
from jax import lax
from jax.experimental import pallas as pl
from jax.experimental.pallas import tpu as pltpu
from jax.sharding import PartitionSpec as P

LX = 4
LY = 4
LZ = 2
GROUPS = 4
LANES = 128
CHUNK = 4
AHEAD = 4
MESH = pl.DeviceIdType.MESH


def mul(a, b):
    return jnp.dot(a, b, preferred_element_type=jnp.float32)


def lane_ids(shape):
    return lax.broadcasted_iota(jnp.int32, shape, 1)


def channels_of(size_x):
    z = [("gz", 1, LX * LY, 5), ("gz", -1, LX * LY, 4)]
    y = [("gy", 1, LX * LZ, 3), ("gy", -1, LX * LZ, 2)]
    if size_x == 2:
        x = [("gx", 0, LY * LZ, None)]
    else:
        x = [("gx", 1, LY * LZ, 1), ("gx", -1, LY * LZ, 0)]
    return z + y + x


def channel_offsets(channels, elems):
    offsets, at = [], elems
    for _, _, count, _ in channels:
        offsets.append(at)
        at += count
    return offsets, at


def face_rows(count, tall):
    return count * LANES + count * 8 + tall


def partner_bits(me, r):
    high, low = me // 2, me % 2
    high = high + (1 - r // 2) * (1 - 2 * high)
    low = low + (1 - r % 2) * (1 - 2 * low)
    return high * 2 + low


def fused_kernel(neighbours, agg_map, owners, prolong, jac, residual, sizes):
    width, elems, _ = prolong.shape
    sides = jac.shape[0]
    aggs_here = owners.shape[1]
    size_x, size_y, size_z = sizes
    rest = width - LANES
    tall = pl.cdiv(width + 1, 8) * 8
    full = pl.cdiv(width + 1, 16) * 16
    pitch = elems + 1
    per_owner = aggs_here // GROUPS
    stride_z = size_z // GROUPS
    out_slots = size_z * per_owner
    members = elems // aggs_here
    on_face = members // 2
    channels = channels_of(size_x)
    offsets, zero_block = channel_offsets(channels, elems)
    nch = len(channels)
    tail = sides * LANES
    msg_rows = tail + LANES
    half = LANES // 2
    most = max(count for _, _, count, _ in channels)
    pieces = sides + 1
    early = aggs_here // 2
    step_rows = 5 if width % 5 == 0 else 1

    def kernel(nbr_ref, agg_ref, own_ref, p_hbm, j_hbm, res_ref, out_ref, rest_ref, *refs):
        tab, table_ref, praw, jraw, near, far, pool, pt, jm = refs[:9]
        sends, recvs = refs[9 : 9 + nch], refs[9 + nch : 9 + 2 * nch]
        refs = refs[9 + 2 * nch :]
        remf, farf, msg, msg_rem, msg_far, racc, acc = refs[:7]
        rows_ref, mixed, mixed_rem, mixed_rest = refs[7:11]
        t_sem, p_sem, j_sem, f_send, f_recv, r_send, r_recv, self_sem = refs[11:]
        me = {"gx": lax.axis_index("gx"), "gy": lax.axis_index("gy"), "gz": lax.axis_index("gz")}
        size = {"gx": size_x, "gy": size_y, "gz": size_z}
        me_z = me["gz"]

        p_copy = pltpu.make_async_copy(p_hbm, praw, p_sem)
        p_copy.start()

        def j_copy(k):
            slot = k % AHEAD
            return pltpu.make_async_copy(j_hbm.at[k], jraw.at[slot], j_sem.at[slot])

        barrier = pltpu.get_barrier_semaphore()
        for step in range(1, size_z):
            to = lax.rem(me_z + step, size_z)
            pl.semaphore_signal(barrier, inc=1, device_id={"gz": to}, device_id_type=MESH)
        expected = size_z - 1
        if size_x == 2:
            pl.semaphore_signal(
                barrier, inc=1, device_id={"gx": 1 - me["gx"]}, device_id_type=MESH
            )
            expected = expected + 1
        for axis in ["gy"] + (["gx"] if size_x > 2 else []):
            for step in (1, -1):
                there = me[axis] + step
                exists = (there >= 0) & (there < size[axis])

                @pl.when(exists)
                def _(axis=axis, there=there):
                    pl.semaphore_signal(
                        barrier, inc=1, device_id={axis: there}, device_id_type=MESH
                    )

                expected = expected + exists.astype(jnp.int32)

        msg_far[...] = jnp.zeros_like(msg_far)
        pool[zero_block] = jnp.zeros(pool.shape[1:], pool.dtype)

        def spread(load, last):
            @pl.loop(0, width // step_rows)
            def _(c):
                part = load(c).astype(jnp.float32)
                for i in range(step_rows):
                    rows = pl.ds((c * step_rows + i) * pitch, elems)
                    near[rows, :] = part[i, :, :LANES]
                    far[rows, :rest] = part[i, :, LANES:]

            near[pl.ds(width * pitch, elems), :] = last[:, :LANES]
            far[pl.ds(width * pitch, elems), :rest] = last[:, LANES:]

        def block(e):
            rows = pl.ds(e, width + 1, stride=pitch)
            right = far[rows, :]
            right = jnp.where(lane_ids(right.shape) < rest, right, 0.0)
            both = jnp.concatenate([near[rows, :], right], axis=1)[:, :full]
            below = jnp.zeros((full - width - 1, full), jnp.float32)
            return jnp.concatenate([both, below], axis=0)

        device = (me["gx"] * size_y + me["gy"]) * size_z + me_z
        write_table(
            tab,
            nbr_ref[...],
            agg_ref[...] - device * aggs_here,
            own_ref[...],
            device * elems,
            me_z // stride_z,
            me["gx"],
            sizes,
        )
        t_copy = pltpu.make_async_copy(tab, table_ref, t_sem)
        t_copy.start()
        p_copy.wait()
        for k in range(AHEAD):
            j_copy(k).start()
        spread(
            lambda c: praw[pl.ds(c * step_rows, step_rows)],
            jnp.zeros((elems, width), jnp.float32),
        )

        @pl.loop(0, elems // 4)
        def _(group):
            for u in range(4):
                e = group * 4 + u
                pool[e] = block(e)[:, :width].astype(pool.dtype)

        t_copy.wait()
        pl.semaphore_wait(barrier, expected)

        def face_target(c):
            axis, step, _, _ = channels[c]
            return {axis: 1 - me[axis] if step == 0 else me[axis] + step}

        def when_sent(c):
            axis, step, _, _ = channels[c]
            if step == 0:
                return lambda f: f()
            there = me[axis] + step
            return pl.when((there >= 0) & (there < size[axis]))

        def when_received(c):
            axis, step, _, _ = channels[c]
            if step == 0:
                return lambda f: f()
            there = me[axis] - step
            return pl.when((there >= 0) & (there < size[axis]))

        def face_parts(c):
            count = channels[c][2]
            parts = [(n * LANES, CHUNK * LANES) for n in range(0, count, CHUNK)]
            return parts + [(count * LANES, count * 8 + full)]

        def face_copy(c, part):
            start, rows = face_parts(c)[part]
            return pltpu.make_async_remote_copy(
                src_ref=sends[c].at[pl.ds(start, rows)],
                dst_ref=recvs[c].at[pl.ds(start, rows)],
                send_sem=f_send.at[c, part],
                recv_sem=f_recv.at[c, part],
                device_id=face_target(c),
                device_id_type=MESH,
            )

        def pack(c, n):
            whole = pool[table_ref[c, n] % elems]
            sends[c][n * LANES : (n + 1) * LANES, :] = whole[:LANES, :LANES]
            remf[c, n * 8 : (n + 1) * 8, :] = whole[LANES:tall, :LANES].astype(jnp.float32)
            farf[c, :, n * rest : (n + 1) * rest] = whole[:, LANES:width].astype(jnp.float32)

        def pack_tail(c):
            count = channels[c][2]
            at = count * LANES
            sends[c][at : at + count * 8, :] = remf[c, : count * 8, :].astype(jnp.bfloat16)
            sends[c][at + count * 8 : at + count * 8 + full, :] = farf[c].astype(jnp.bfloat16)

        def send_faces(group):
            parts = max(len(face_parts(c)) for c in group)
            for part in range(parts):
                for c in group:
                    if part < len(face_parts(c)):
                        if part < len(face_parts(c)) - 1:
                            for n in range(part * CHUNK, (part + 1) * CHUNK):
                                pack(c, n)
                        else:
                            pack_tail(c)

                        @when_sent(c)
                        def _(c=c, part=part):
                            face_copy(c, part).start()

        def take_faces(group):
            for c in group:

                @when_received(c)
                def _(c=c):
                    for part in range(len(face_parts(c))):
                        face_copy(c, part).wait_recv()
                    count = channels[c][2]
                    at = count * LANES
                    remf[c, : count * 8, :] = recvs[c][at : at + count * 8, :].astype(jnp.float32)
                    farf[c] = recvs[c][at + count * 8 : at + count * 8 + full, :].astype(
                        jnp.float32
                    )
                    for n in range(count):
                        to = offsets[c] + n
                        pool[to, :LANES, :LANES] = recvs[c][n * LANES : (n + 1) * LANES, :]
                        below = remf[c, n * 8 : (n + 1) * 8, :]
                        below = jnp.concatenate([below, jnp.zeros_like(below)], axis=0)
                        pool[to, LANES:full, :LANES] = below.astype(pool.dtype)
                        pool[to, :, LANES:width] = farf[
                            c, :, n * rest : (n + 1) * rest
                        ].astype(pool.dtype)

        send_faces([0, 1])
        send_faces(list(range(2, nch)))

        @pl.loop(0, elems // 4)
        def _(group):
            for u in range(4):
                e = group * 4 + u
                pt[e] = block(e).T[:tall].astype(pt.dtype)

        @pl.loop(0, sides)
        def _(k):
            j_copy(k).wait()
            own = (k == 0).astype(jnp.float32)
            spread(
                lambda c: jraw[k % AHEAD, pl.ds(c * step_rows, step_rows)],
                res_ref[...].astype(jnp.float32) * own,
            )

            @pl.when(k + AHEAD < sides)
            def _():
                j_copy(k + AHEAD).start()

            @pl.loop(0, elems // 4)
            def _(group):
                for u in range(4):
                    e = group * 4 + u
                    jm[k, e] = block(e).astype(jm.dtype)

        my_group = me_z // stride_z

        def target_of(r):
            return partner_bits(my_group, r // per_owner) * stride_z

        def slot_of(z, r):
            return z * per_owner + r % per_owner

        def row_copy(r, piece):
            at = pl.ds(pl.multiple_of(piece * LANES, LANES), LANES)
            slot = slot_of(me_z, r)
            return pltpu.make_async_remote_copy(
                src_ref=msg.at[r, at],
                dst_ref=rows_ref.at[slot, at],
                send_sem=r_send.at[r, piece],
                recv_sem=r_recv.at[slot, piece],
                device_id={"gz": target_of(r)},
                device_id_type=MESH,
            )

        def self_copy(r, piece):
            at = pl.ds(pl.multiple_of(piece * LANES, LANES), LANES)
            return pltpu.make_async_copy(
                msg.at[r, at],
                rows_ref.at[slot_of(me_z, r), at],
                self_sem.at[r % per_owner, piece],
            )

        def send_row(r, piece):
            @pl.when(target_of(r) != me_z)
            def _():
                row_copy(r, piece).start()

            @pl.when(target_of(r) == me_z)
            def _():
                self_copy(r, piece).start()

        def emit(r, s, value):
            msg[r, s * LANES : (s + 1) * LANES, :] = value[:LANES, :LANES].astype(msg.dtype)
            msg_rem[r, s * 8 : (s + 1) * 8, :] = value[LANES:tall, :LANES]
            msg_far[r, :, s * rest : (s + 1) * rest] = value[:, LANES:width]
            send_row(r, s)

        def side_sum(r, d):
            total = None
            for m in range(on_face):
                code = table_ref[nch + 1 + d, r * on_face + m]
                e, n = code % elems, jnp.clip(code // elems, 0, zero_block)
                product = mul(jm[1 + d, e], pool[n]).astype(jnp.bfloat16)
                triple = mul(pt[e], product)
                total = triple if total is None else total + triple
            return total

        def own_slot(r):
            acc[...] = jnp.zeros_like(acc)
            racc[...] = jnp.zeros_like(racc)

            @pl.loop(0, members // 2)
            def _(pair):
                total = None
                for u in range(2):
                    code = table_ref[nch, r * members + pair * 2 + u]
                    e, code = code % elems, code // elems
                    product = mul(jm[0, e], pool[e])
                    for axis in range(3):
                        x, code = code % (2 * elems), code // (2 * elems)
                        k = 1 + 2 * axis + x // elems
                        product = product + mul(jm[k, e], pool[x % elems])
                    racc[...] += product[LANES:tall]
                    triple = mul(pt[e], product.astype(jnp.bfloat16))
                    total = triple if total is None else total + triple
                acc[...] += total

            below = racc[...]
            spare = lax.broadcasted_iota(jnp.int32, below.shape, 0) == width - LANES
            acc[LANES:tall, :] += jnp.where(spare, below, 0.0)
            emit(r, 0, acc[...])

        def send_tail(r):
            msg_rem[r, sides * 8 : (sides + 1) * 8, :] = msg_far[r, LANES:tall, :]
            msg[r, tail : tail + half, :] = msg_rem[r].astype(msg.dtype)
            right = pltpu.roll(msg_far[r, half:LANES, :], half, 1)
            left = msg_far[r, :half, :]
            folded = jnp.where(lane_ids(left.shape) < half, left, right)
            msg[r, tail + half : msg_rows, :] = folded.astype(msg.dtype)
            send_row(r, sides)

        @pl.loop(0, 2)
        def _(part):
            first, last = part * early, part * early + early
            pl.loop(first, last)(own_slot)
            axis_faces = [list(range(4, nch)), [2, 3], [0, 1]]
            for axis in range(3):

                @pl.when(part == 0)
                def _(axis=axis):
                    take_faces(axis_faces[axis])

                @pl.loop(first, last)
                def _(r, axis=axis):
                    for d in (2 * axis, 2 * axis + 1):
                        emit(r, 1 + d, side_sum(r, d))
                    if axis == 2:
                        send_tail(r)

        owner = me_z % stride_z == 0

        def row_arrival(slot, piece):
            at = pl.ds(piece * LANES, LANES)
            return pltpu.make_async_remote_copy(
                src_ref=msg.at[0, at],
                dst_ref=rows_ref.at[slot, at],
                send_sem=r_send.at[0, piece],
                recv_sem=r_recv.at[slot, piece],
                device_id={"gz": me_z},
                device_id_type=MESH,
            )

        def arrive(piece):
            for slot in range(out_slots):
                mine = slot // per_owner == me_z

                @pl.when(mine)
                def _(slot=slot):
                    self_copy(aggs_here - per_owner + slot % per_owner, piece).wait()

                @pl.when(jnp.logical_not(mine))
                def _(slot=slot):
                    row_arrival(slot, piece).wait_recv()

        def scatter(ref, slot, start, value):
            count = value.shape[0]
            ref[pl.ds(start * out_slots + slot, count, stride=out_slots), :] = value

        def gathered(ref, count):
            value = ref[: count * out_slots, :].astype(jnp.bfloat16)
            return value.reshape(count, out_slots, LANES)

        def unpack():
            for s in range(sides):
                arrive(s)
                for slot in range(out_slots):
                    block_of = rows_ref[slot, s * LANES : (s + 1) * LANES, :]
                    scatter(mixed, slot, 0, block_of.astype(jnp.float32))
                out_ref[s, :LANES, :, :LANES] = gathered(mixed, LANES)

            arrive(sides)
            for slot in range(out_slots):
                below = rows_ref[slot, tail : tail + half, :].astype(jnp.float32)
                folded = rows_ref[slot, tail + half : msg_rows, :].astype(jnp.float32)
                scatter(mixed, slot, 0, folded)
                scatter(mixed, slot, half, pltpu.roll(folded, half, 1))
                scatter(mixed, slot, LANES, below[sides * 8 :])
                for s in range(sides):
                    scatter(mixed_rem.at[s], slot, 0, below[s * 8 : (s + 1) * 8])
                mixed_rest[slot : slot + 1, :LANES] = below[rest : rest + 1]
                at = sides * 8 + rest
                mixed_rest[slot : slot + 1, LANES:] = below[at : at + 1, :rest]
            rest_ref[...] = mixed_rest[:out_slots].astype(rest_ref.dtype)
            right = gathered(mixed, tall)
            for s in range(sides):
                low = gathered(mixed_rem.at[s], 8)
                out_ref[s, LANES:, :, :LANES] = low[:rest]
                out_ref[s, :, :, LANES:] = right[:width, :, s * rest : (s + 1) * rest]

        if stride_z == 1:
            unpack()
        else:
            pl.when(owner)(unpack)

            @pl.when(jnp.logical_not(owner))
            def _():
                out_ref[...] = jnp.zeros_like(out_ref)
                rest_ref[...] = jnp.zeros_like(rest_ref)

        for c in range(nch):

            @when_sent(c)
            def _(c=c):
                for part in range(len(face_parts(c))):
                    face_copy(c, part).wait_send()

        @pl.loop(0, aggs_here)
        def _(r):
            @pl.when(target_of(r) != me_z)
            def _():
                for piece in range(pieces):
                    row_copy(r, piece).wait_send()

    bf16, f32 = jnp.bfloat16, jnp.float32
    spread_rows = (width + 1) * pitch
    faces = [pltpu.VMEM((face_rows(count, full), LANES), bf16) for _, _, count, _ in channels]
    parts = most // CHUNK + 1
    table_rows = pl.cdiv(nch + sides, 8) * 8
    scratch = [
        pltpu.VMEM((table_rows, LANES), jnp.int32),
        pltpu.SMEM((table_rows, LANES), jnp.int32),
        pltpu.VMEM((width, elems, width), bf16),
        pltpu.VMEM((AHEAD, width, elems, width), bf16),
        pltpu.VMEM((spread_rows, LANES), f32),
        pltpu.VMEM((spread_rows, LANES), f32),
        pltpu.VMEM((zero_block + 1, full, width), bf16),
        pltpu.VMEM((elems, tall, full), bf16),
        pltpu.VMEM((sides, elems, full, full), bf16),
        *faces,
        *faces,
        pltpu.VMEM((nch, most * 8, LANES), f32),
        pltpu.VMEM((nch, full, LANES), f32),
        pltpu.VMEM((aggs_here, msg_rows, LANES), bf16),
        pltpu.VMEM((aggs_here, (sides + 1) * 8, LANES), f32),
        pltpu.VMEM((aggs_here, tall, LANES), f32),
        pltpu.VMEM((8, width), f32),
        pltpu.VMEM((tall, width), f32),
        pltpu.VMEM((out_slots, msg_rows, LANES), bf16),
        pltpu.VMEM((tall * out_slots, LANES), f32),
        pltpu.VMEM((sides, 8 * out_slots, LANES), f32),
        pltpu.VMEM((pl.cdiv(out_slots, 8) * 8, width), f32),
        pltpu.SemaphoreType.DMA,
        pltpu.SemaphoreType.DMA,
        pltpu.SemaphoreType.DMA((AHEAD,)),
        pltpu.SemaphoreType.DMA((nch, parts)),
        pltpu.SemaphoreType.DMA((nch, parts)),
        pltpu.SemaphoreType.DMA((aggs_here, pieces)),
        pltpu.SemaphoreType.DMA((out_slots, pieces)),
        pltpu.SemaphoreType.DMA((per_owner, pieces)),
    ]
    return pl.pallas_call(
        kernel,
        in_specs=[pl.BlockSpec(memory_space=pltpu.VMEM)] * 3
        + [pl.BlockSpec(memory_space=pl.ANY)] * 2
        + [pl.BlockSpec(memory_space=pltpu.VMEM)],
        out_specs=[pl.BlockSpec(memory_space=pltpu.VMEM)] * 2,
        out_shape=[
            jax.ShapeDtypeStruct((sides, width, out_slots, width), bf16),
            jax.ShapeDtypeStruct((out_slots, width), bf16),
        ],
        scratch_shapes=scratch,
        compiler_params=pltpu.CompilerParams(
            collective_id=0, has_side_effects=True, vmem_limit_bytes=62 << 20
        ),
    )(neighbours, agg_map, owners, prolong, jac, residual)


def write_table(tab, nbr, agg, owners, base, mine, x, sizes):
    size_x, _, size_z = sizes
    elems, aggs_here = nbr.shape[1], owners.shape[1]
    per_owner = aggs_here // GROUPS
    stride_z = size_z // GROUPS
    members = elems // aggs_here
    on_face = members // 2
    channels = channels_of(size_x)
    offsets, zero_block = channel_offsets(channels, elems)
    nch = len(channels)
    square = (elems, elems)
    down = lax.broadcasted_iota(jnp.int32, square, 0)
    along = lax.broadcasted_iota(jnp.int32, square, 1)
    ids = down[:, :1]

    def flag(mask):
        return jnp.where(mask, 1, 0)

    eye = flag(down == along)
    before = flag(along < down)

    def by_row(value):
        return jnp.sum(value, axis=1, keepdims=True)

    def by_column(value):
        return jnp.sum(value, axis=0, keepdims=True)

    def column(row):
        return by_row(eye * row)

    def row(col):
        return by_column(eye * col)

    def listed(place, value):
        return by_column(flag(place == along) * value)

    def put(at, value):
        tab[at : at + 1, :elems] = value

    a_down = lax.broadcasted_iota(jnp.int32, (aggs_here, aggs_here), 0)
    a_along = lax.broadcasted_iota(jnp.int32, (aggs_here, aggs_here), 1)
    to = owners // stride_z
    turn = 3 - (2 * jnp.abs(to // 2 - mine // 2) + jnp.abs(to % 2 - mine % 2))
    turn = jnp.broadcast_to(turn, a_down.shape)
    turn = by_row(jnp.where(a_down == a_along, turn, 0))
    if per_owner > 1:
        turn_row = by_column(jnp.where(a_down == a_along, turn, 0))
        equal = flag(turn_row == turn) * flag(a_along < a_down)
        turn = turn * per_owner + by_row(equal)
    a_ids = lax.broadcasted_iota(jnp.int32, (aggs_here, elems), 0)
    order_row = by_column(flag(agg == a_ids) * turn)
    order = column(order_row)
    agg_col = column(agg)
    together = before * flag(order_row == order)
    m_place = order * members + by_row(together)

    if size_x == 2:
        listing = [(5, 0), (4, 1), (3, 2), (2, 3)]
        sources = [4, 4, 2, 3, 0, 1]
    else:
        listing = [(5, 0), (4, 1), (3, 2), (2, 3), (1, 4), (0, 5)]
        sources = [4, 5, 2, 3, 0, 1]
    sides_of, local_of, same_of = [], [], []
    for d in range(6):
        nbr_row = nbr[d : d + 1]
        nbr_col = column(nbr_row)
        local_row, local = nbr_row - base, nbr_col - base
        away_row = 1 - flag(local_row >= 0) * flag(local_row < elems)
        here = flag(local >= 0) * flag(local < elems)
        rank = by_row(before * away_row)
        place = jnp.where(here > 0, -1, rank)
        sides_of.append(listed(place, ids))
        crossing = away_row * flag(nbr_row >= 0)
        position = by_row(crossing * flag(nbr_row < nbr_col))
        index = jnp.where(here > 0, local, position + offsets[sources[d]])
        index = jnp.where(nbr_col >= 0, index, zero_block)
        near_agg = by_row(flag(local == along) * agg)
        same = here * flag(near_agg == agg_col)
        local_of.append(local)
        same_of.append(same)
        s_rank = by_row(together * (1 - row(same)))
        s_place = jnp.where(same > 0, -1, order * on_face + s_rank)
        put(nch + 1 + d, listed(s_place, ids + elems * index))
    for d, c in listing:
        put(c, sides_of[d])
    if size_x == 2:
        put(4, jnp.where(x == 0, sides_of[1], sides_of[0]))
    code = jnp.zeros_like(ids)
    for axis in (2, 1, 0):
        after = same_of[2 * axis + 1] > 0
        inner = jnp.where(after, local_of[2 * axis + 1] + elems, local_of[2 * axis])
        code = code * (2 * elems) + inner
    put(nch, listed(m_place, code * elems + ids))


def body(jacobian, prolong, residual, neighbours, agg_map, owners):
    sizes = tuple(lax.axis_size(a) for a in ("gx", "gy", "gz"))
    coarse, restricted = fused_kernel(
        neighbours.T,
        agg_map[None],
        owners[None],
        jnp.transpose(prolong, (1, 0, 2)),
        jnp.transpose(jacobian, (1, 2, 0, 3)),
        residual,
        sizes,
    )
    return jnp.transpose(coarse, (2, 0, 1, 3)), restricted


def solution(mesh):
    spec = P(("gx", "gy", "gz"))
    return jax.shard_map(
        body,
        mesh=mesh,
        in_specs=(spec,) * 6,
        out_specs=(spec, spec),
        check_vma=False,
    )
```

```python
import jax
import jax.numpy as jnp
from jax import lax
from jax.experimental import pallas as pl
from jax.experimental.pallas import tpu as pltpu
from jax.sharding import PartitionSpec as P

LX = 4
LY = 4
LZ = 2
GROUPS = 4
LANES = 128
CHUNK = 4
AHEAD = 4
MESH = pl.DeviceIdType.MESH


def mul(a, b):
    return jnp.dot(a, b, preferred_element_type=jnp.float32)


def lane_ids(shape):
    return lax.broadcasted_iota(jnp.int32, shape, 1)


def channels_of(size_x):
    z = [("gz", 1, LX * LY, 5), ("gz", -1, LX * LY, 4)]
    y = [("gy", 1, LX * LZ, 3), ("gy", -1, LX * LZ, 2)]
    if size_x == 2:
        x = [("gx", 0, LY * LZ, None)]
    else:
        x = [("gx", 1, LY * LZ, 1), ("gx", -1, LY * LZ, 0)]
    return z + y + x


def channel_offsets(channels, elems):
    offsets, at = [], elems
    for _, _, count, _ in channels:
        offsets.append(at)
        at += count
    return offsets, at


def face_rows(count, tall):
    return count * LANES + count * 8 + tall


def partner_bits(me, r):
    high, low = me // 2, me % 2
    high = high + (1 - r // 2) * (1 - 2 * high)
    low = low + (1 - r % 2) * (1 - 2 * low)
    return high * 2 + low


def fused_kernel(neighbours, agg_map, owners, prolong, jac, residual, sizes):
    width, elems, _ = prolong.shape
    sides = jac.shape[0]
    aggs_here = owners.shape[1]
    size_x, size_y, size_z = sizes
    rest = width - LANES
    tall = pl.cdiv(width + 1, 8) * 8
    full = pl.cdiv(width + 1, 16) * 16
    pitch = elems + 1
    per_owner = aggs_here // GROUPS
    stride_z = size_z // GROUPS
    out_slots = size_z * per_owner
    members = elems // aggs_here
    on_face = members // 2
    channels = channels_of(size_x)
    offsets, zero_block = channel_offsets(channels, elems)
    nch = len(channels)
    tail = sides * LANES
    msg_rows = tail + LANES
    half = LANES // 2
    most = max(count for _, _, count, _ in channels)
    pieces = sides + 1
    early = aggs_here // 2
    step_rows = 5 if width % 5 == 0 else 1

    def kernel(nbr_ref, agg_ref, own_ref, p_hbm, j_hbm, res_ref, out_ref, rest_ref, *refs):
        tab, table_ref, praw, jraw, near, far, pool, pt, jm = refs[:9]
        sends, recvs = refs[9 : 9 + nch], refs[9 + nch : 9 + 2 * nch]
        refs = refs[9 + 2 * nch :]
        remf, farf, msg, msg_rem, msg_far, racc, acc = refs[:7]
        rows_ref, mixed, mixed_rem, mixed_rest = refs[7:11]
        t_sem, p_sem, j_sem, f_send, f_recv, r_send, r_recv, self_sem = refs[11:]
        me = {"gx": lax.axis_index("gx"), "gy": lax.axis_index("gy"), "gz": lax.axis_index("gz")}
        size = {"gx": size_x, "gy": size_y, "gz": size_z}
        me_z = me["gz"]

        p_copy = pltpu.make_async_copy(p_hbm, praw, p_sem)
        p_copy.start()

        def j_copy(k):
            slot = k % AHEAD
            return pltpu.make_async_copy(j_hbm.at[k], jraw.at[slot], j_sem.at[slot])

        barrier = pltpu.get_barrier_semaphore()
        for step in range(1, size_z):
            to = lax.rem(me_z + step, size_z)
            pl.semaphore_signal(barrier, inc=1, device_id={"gz": to}, device_id_type=MESH)
        expected = size_z - 1
        if size_x == 2:
            pl.semaphore_signal(
                barrier, inc=1, device_id={"gx": 1 - me["gx"]}, device_id_type=MESH
            )
            expected = expected + 1
        for axis in ["gy"] + (["gx"] if size_x > 2 else []):
            for step in (1, -1):
                there = me[axis] + step
                exists = (there >= 0) & (there < size[axis])

                @pl.when(exists)
                def _(axis=axis, there=there):
                    pl.semaphore_signal(
                        barrier, inc=1, device_id={axis: there}, device_id_type=MESH
                    )

                expected = expected + exists.astype(jnp.int32)

        msg_far[...] = jnp.zeros_like(msg_far)
        for sub in range(per_owner):
            for piece, slot in ((5, sub), (6, out_slots - per_owner + sub)):
                rows_ref[slot, piece * LANES : (piece + 1) * LANES, :] = jnp.zeros(
                    (LANES, LANES), rows_ref.dtype
                )
        pool[zero_block] = jnp.zeros(pool.shape[1:], pool.dtype)

        def spread(load, last):
            @pl.loop(0, width // step_rows)
            def _(c):
                part = load(c).astype(jnp.float32)
                for i in range(step_rows):
                    rows = pl.ds((c * step_rows + i) * pitch, elems)
                    near[rows, :] = part[i, :, :LANES]
                    far[rows, :rest] = part[i, :, LANES:]

            near[pl.ds(width * pitch, elems), :] = last[:, :LANES]
            far[pl.ds(width * pitch, elems), :rest] = last[:, LANES:]

        def block(e):
            rows = pl.ds(e, width + 1, stride=pitch)
            right = far[rows, :]
            right = jnp.where(lane_ids(right.shape) < rest, right, 0.0)
            both = jnp.concatenate([near[rows, :], right], axis=1)[:, :full]
            below = jnp.zeros((full - width - 1, full), jnp.float32)
            return jnp.concatenate([both, below], axis=0)

        device = (me["gx"] * size_y + me["gy"]) * size_z + me_z
        write_table(
            tab,
            nbr_ref[...],
            agg_ref[...] - device * aggs_here,
            own_ref[...],
            device * elems,
            me_z // stride_z,
            me["gx"],
            sizes,
        )
        t_copy = pltpu.make_async_copy(tab, table_ref, t_sem)
        t_copy.start()
        p_copy.wait()
        for k in range(AHEAD):
            j_copy(k).start()
        spread(
            lambda c: praw[pl.ds(c * step_rows, step_rows)],
            jnp.zeros((elems, width), jnp.float32),
        )

        @pl.loop(0, elems // 4)
        def _(group):
            for u in range(4):
                e = group * 4 + u
                pool[e] = block(e)[:, :width].astype(pool.dtype)

        t_copy.wait()
        pl.semaphore_wait(barrier, expected)

        def face_target(c):
            axis, step, _, _ = channels[c]
            return {axis: 1 - me[axis] if step == 0 else me[axis] + step}

        def when_sent(c):
            axis, step, _, _ = channels[c]
            if step == 0:
                return lambda f: f()
            there = me[axis] + step
            return pl.when((there >= 0) & (there < size[axis]))

        def when_received(c):
            axis, step, _, _ = channels[c]
            if step == 0:
                return lambda f: f()
            there = me[axis] - step
            return pl.when((there >= 0) & (there < size[axis]))

        def face_parts(c):
            count = channels[c][2]
            parts = [(n * LANES, CHUNK * LANES) for n in range(0, count, CHUNK)]
            return parts + [(count * LANES, count * 8 + full)]

        def face_copy(c, part):
            start, rows = face_parts(c)[part]
            return pltpu.make_async_remote_copy(
                src_ref=sends[c].at[pl.ds(start, rows)],
                dst_ref=recvs[c].at[pl.ds(start, rows)],
                send_sem=f_send.at[c, part],
                recv_sem=f_recv.at[c, part],
                device_id=face_target(c),
                device_id_type=MESH,
            )

        def pack(c, n):
            whole = pool[table_ref[c, n] % elems]
            sends[c][n * LANES : (n + 1) * LANES, :] = whole[:LANES, :LANES]
            remf[c, n * 8 : (n + 1) * 8, :] = whole[LANES:tall, :LANES].astype(jnp.float32)
            farf[c, :, n * rest : (n + 1) * rest] = whole[:, LANES:width].astype(jnp.float32)

        def pack_tail(c):
            count = channels[c][2]
            at = count * LANES
            sends[c][at : at + count * 8, :] = remf[c, : count * 8, :].astype(jnp.bfloat16)
            sends[c][at + count * 8 : at + count * 8 + full, :] = farf[c].astype(jnp.bfloat16)

        def send_faces(group):
            parts = max(len(face_parts(c)) for c in group)
            for part in range(parts):
                for c in group:
                    if part < len(face_parts(c)):
                        if part < len(face_parts(c)) - 1:
                            for n in range(part * CHUNK, (part + 1) * CHUNK):
                                pack(c, n)
                        else:
                            pack_tail(c)

                        @when_sent(c)
                        def _(c=c, part=part):
                            face_copy(c, part).start()

        def take_faces(group):
            for c in group:

                @when_received(c)
                def _(c=c):
                    for part in range(len(face_parts(c))):
                        face_copy(c, part).wait_recv()
                    count = channels[c][2]
                    at = count * LANES
                    remf[c, : count * 8, :] = recvs[c][at : at + count * 8, :].astype(jnp.float32)
                    farf[c] = recvs[c][at + count * 8 : at + count * 8 + full, :].astype(
                        jnp.float32
                    )
                    for n in range(count):
                        to = offsets[c] + n
                        pool[to, :LANES, :LANES] = recvs[c][n * LANES : (n + 1) * LANES, :]
                        below = remf[c, n * 8 : (n + 1) * 8, :]
                        below = jnp.concatenate([below, jnp.zeros_like(below)], axis=0)
                        pool[to, LANES:full, :LANES] = below.astype(pool.dtype)
                        pool[to, :, LANES:width] = farf[
                            c, :, n * rest : (n + 1) * rest
                        ].astype(pool.dtype)

        send_faces([0, 1])
        send_faces(list(range(2, nch)))

        @pl.loop(0, elems // 4)
        def _(group):
            for u in range(4):
                e = group * 4 + u
                pt[e] = block(e).T[:tall].astype(pt.dtype)

        @pl.loop(0, sides)
        def _(k):
            j_copy(k).wait()
            own = (k == 0).astype(jnp.float32)
            spread(
                lambda c: jraw[k % AHEAD, pl.ds(c * step_rows, step_rows)],
                res_ref[...].astype(jnp.float32) * own,
            )

            @pl.when(k + AHEAD < sides)
            def _():
                j_copy(k + AHEAD).start()

            @pl.loop(0, elems // 4)
            def _(group):
                for u in range(4):
                    e = group * 4 + u
                    jm[k, e] = block(e).astype(jm.dtype)

        my_group = me_z // stride_z

        def target_of(r):
            return partner_bits(my_group, r // per_owner) * stride_z

        def slot_of(z, r):
            return z * per_owner + r % per_owner

        def row_copy(r, piece):
            at = pl.ds(pl.multiple_of(piece * LANES, LANES), LANES)
            slot = slot_of(me_z, r)
            return pltpu.make_async_remote_copy(
                src_ref=msg.at[r, at],
                dst_ref=rows_ref.at[slot, at],
                send_sem=r_send.at[r, piece],
                recv_sem=r_recv.at[slot, piece],
                device_id={"gz": target_of(r)},
                device_id_type=MESH,
            )

        def self_copy(r, piece):
            at = pl.ds(pl.multiple_of(piece * LANES, LANES), LANES)
            return pltpu.make_async_copy(
                msg.at[r, at],
                rows_ref.at[slot_of(me_z, r), at],
                self_sem.at[r % per_owner, piece],
            )

        def send_row(r, piece):
            sent = present(piece, me_z)

            @pl.when((target_of(r) != me_z) & sent)
            def _():
                row_copy(r, piece).start()

            @pl.when((target_of(r) == me_z) & sent)
            def _():
                self_copy(r, piece).start()

        def emit(r, s, value):
            msg[r, s * LANES : (s + 1) * LANES, :] = value[:LANES, :LANES].astype(msg.dtype)
            msg_rem[r, s * 8 : (s + 1) * 8, :] = value[LANES:tall, :LANES]
            msg_far[r, :, s * rest : (s + 1) * rest] = value[:, LANES:width]

        def present(piece, z):
            if piece == 5:
                return z > 0
            if piece == 6:
                return z < size_z - 1
            return True

        def side_sum(r, d):
            total = None
            for m in range(on_face):
                code = table_ref[nch + 1 + d, r * on_face + m]
                e, n = code % elems, jnp.clip(code // elems, 0, zero_block)
                product = mul(jm[1 + d, e], pool[n]).astype(jnp.bfloat16)
                triple = mul(pt[e], product)
                total = triple if total is None else total + triple
            return total

        def own_slot(r):
            acc[...] = jnp.zeros_like(acc)
            racc[...] = jnp.zeros_like(racc)

            @pl.loop(0, members // 4)
            def _(pair):
                total = None
                for u in range(4):
                    code = table_ref[nch, r * members + pair * 4 + u]
                    e, code = code % elems, code // elems
                    product = mul(jm[0, e], pool[e])
                    for axis in range(3):
                        x, code = code % (2 * elems), code // (2 * elems)
                        k = 1 + 2 * axis + x // elems
                        product = product + mul(jm[k, e], pool[x % elems])
                    racc[...] += product[LANES:tall]
                    triple = mul(pt[e], product.astype(jnp.bfloat16))
                    total = triple if total is None else total + triple
                acc[...] += total

            below = racc[...]
            spare = lax.broadcasted_iota(jnp.int32, below.shape, 0) == width - LANES
            acc[LANES:tall, :] += jnp.where(spare, below, 0.0)
            emit(r, 0, acc[...])
            send_row(r, 0)

        def pack_row_tail(r):
            msg_rem[r, sides * 8 : (sides + 1) * 8, :] = msg_far[r, LANES:tall, :]
            msg[r, tail : tail + half, :] = msg_rem[r].astype(msg.dtype)
            right = pltpu.roll(msg_far[r, half:LANES, :], half, 1)
            left = msg_far[r, :half, :]
            folded = jnp.where(lane_ids(left.shape) < half, left, right)
            msg[r, tail + half : msg_rows, :] = folded.astype(msg.dtype)

        @pl.loop(0, 2)
        def _(part):
            first, last = part * early, part * early + early
            pl.loop(first, last)(own_slot)
            axis_faces = [list(range(4, nch)), [2, 3], [0, 1]]
            for axis in range(3):

                @pl.when(part == 0)
                def _(axis=axis):
                    take_faces(axis_faces[axis])

                @pl.loop(first, last)
                def _(r, axis=axis):
                    pair = (2 * axis, 2 * axis + 1)
                    for d, total in [(d, side_sum(r, d)) for d in pair]:
                        emit(r, 1 + d, total)
                    if axis == 2:
                        pack_row_tail(r)
                    for d in pair:
                        send_row(r, 1 + d)
                    if axis == 2:
                        send_row(r, sides)

        owner = me_z % stride_z == 0

        def row_arrival(slot, piece):
            at = pl.ds(piece * LANES, LANES)
            return pltpu.make_async_remote_copy(
                src_ref=msg.at[0, at],
                dst_ref=rows_ref.at[slot, at],
                send_sem=r_send.at[0, piece],
                recv_sem=r_recv.at[slot, piece],
                device_id={"gz": me_z},
                device_id_type=MESH,
            )

        def arrive(piece):
            for slot in range(out_slots):
                sent = present(piece, slot // per_owner)
                if sent is False:
                    continue
                mine = slot // per_owner == me_z

                @pl.when(mine)
                def _(slot=slot):
                    self_copy(aggs_here - per_owner + slot % per_owner, piece).wait()

                @pl.when(jnp.logical_not(mine))
                def _(slot=slot):
                    row_arrival(slot, piece).wait_recv()

        def scatter(ref, slot, start, value):
            count = value.shape[0]
            ref[pl.ds(start * out_slots + slot, count, stride=out_slots), :] = value

        def gathered(ref, count):
            value = ref[: count * out_slots, :].astype(jnp.bfloat16)
            return value.reshape(count, out_slots, LANES)

        def unpack():
            for s in range(sides):
                arrive(s)
                for slot in range(out_slots):
                    block_of = rows_ref[slot, s * LANES : (s + 1) * LANES, :]
                    scatter(mixed, slot, 0, block_of.astype(jnp.float32))
                out_ref[s, :LANES, :, :LANES] = gathered(mixed, LANES)

            arrive(sides)
            for slot in range(out_slots):
                below = rows_ref[slot, tail : tail + half, :].astype(jnp.float32)
                folded = rows_ref[slot, tail + half : msg_rows, :].astype(jnp.float32)
                scatter(mixed, slot, 0, folded)
                scatter(mixed, slot, half, pltpu.roll(folded, half, 1))
                scatter(mixed, slot, LANES, below[sides * 8 :])
                for s in range(sides):
                    scatter(mixed_rem.at[s], slot, 0, below[s * 8 : (s + 1) * 8])
                mixed_rest[slot : slot + 1, :LANES] = below[rest : rest + 1]
                at = sides * 8 + rest
                mixed_rest[slot : slot + 1, LANES:] = below[at : at + 1, :rest]
            rest_ref[...] = mixed_rest[:out_slots].astype(rest_ref.dtype)
            for s in range(sides):
                low = gathered(mixed_rem.at[s], 8)
                out_ref[s, LANES:, :, :LANES] = low[:rest]
                right = mixed[...]
                if s > 0:
                    right = pltpu.roll(right, LANES - s * rest, 1)
                right = right.astype(jnp.bfloat16).reshape(tall, out_slots, LANES)
                out_ref[s, :, :, LANES:] = right[:width, :, :rest]

        if stride_z == 1:
            unpack()
        else:
            pl.when(owner)(unpack)

            @pl.when(jnp.logical_not(owner))
            def _():
                out_ref[...] = jnp.zeros_like(out_ref)
                rest_ref[...] = jnp.zeros_like(rest_ref)

        for c in range(nch):

            @when_sent(c)
            def _(c=c):
                for part in range(len(face_parts(c))):
                    face_copy(c, part).wait_send()

        @pl.loop(0, aggs_here)
        def _(r):
            @pl.when(target_of(r) != me_z)
            def _():
                for piece in range(pieces):

                    @pl.when(present(piece, me_z))
                    def _(piece=piece):
                        row_copy(r, piece).wait_send()

    bf16, f32 = jnp.bfloat16, jnp.float32
    spread_rows = (width + 1) * pitch
    faces = [pltpu.VMEM((face_rows(count, full), LANES), bf16) for _, _, count, _ in channels]
    parts = most // CHUNK + 1
    table_rows = pl.cdiv(nch + sides, 8) * 8
    scratch = [
        pltpu.VMEM((table_rows, LANES), jnp.int32),
        pltpu.SMEM((table_rows, LANES), jnp.int32),
        pltpu.VMEM((width, elems, width), bf16),
        pltpu.VMEM((AHEAD, width, elems, width), bf16),
        pltpu.VMEM((spread_rows, LANES), f32),
        pltpu.VMEM((spread_rows, LANES), f32),
        pltpu.VMEM((zero_block + 1, full, width), bf16),
        pltpu.VMEM((elems, tall, full), bf16),
        pltpu.VMEM((sides, elems, full, full), bf16),
        *faces,
        *faces,
        pltpu.VMEM((nch, most * 8, LANES), f32),
        pltpu.VMEM((nch, full, LANES), f32),
        pltpu.VMEM((aggs_here, msg_rows, LANES), bf16),
        pltpu.VMEM((aggs_here, (sides + 1) * 8, LANES), f32),
        pltpu.VMEM((aggs_here, tall, LANES), f32),
        pltpu.VMEM((8, width), f32),
        pltpu.VMEM((tall, width), f32),
        pltpu.VMEM((out_slots, msg_rows, LANES), bf16),
        pltpu.VMEM((tall * out_slots, LANES), f32),
        pltpu.VMEM((sides, 8 * out_slots, LANES), f32),
        pltpu.VMEM((pl.cdiv(out_slots, 8) * 8, width), f32),
        pltpu.SemaphoreType.DMA,
        pltpu.SemaphoreType.DMA,
        pltpu.SemaphoreType.DMA((AHEAD,)),
        pltpu.SemaphoreType.DMA((nch, parts)),
        pltpu.SemaphoreType.DMA((nch, parts)),
        pltpu.SemaphoreType.DMA((aggs_here, pieces)),
        pltpu.SemaphoreType.DMA((out_slots, pieces)),
        pltpu.SemaphoreType.DMA((per_owner, pieces)),
    ]
    return pl.pallas_call(
        kernel,
        in_specs=[pl.BlockSpec(memory_space=pltpu.VMEM)] * 3
        + [pl.BlockSpec(memory_space=pl.ANY)] * 2
        + [pl.BlockSpec(memory_space=pltpu.VMEM)],
        out_specs=[pl.BlockSpec(memory_space=pltpu.VMEM)] * 2,
        out_shape=[
            pltpu.VMEM((sides, width, out_slots, width), bf16),
            pltpu.VMEM((out_slots, width), bf16),
        ],
        scratch_shapes=scratch,
        compiler_params=pltpu.CompilerParams(
            collective_id=0, has_side_effects=True, vmem_limit_bytes=54 << 20
        ),
    )(neighbours, agg_map, owners, prolong, jac, residual)


def stored(coarse, restricted):
    pieces = coarse.shape[0]

    def kernel(coarse_ref, small_ref, out_hbm, small_hbm, sems):
        copies = [
            pltpu.make_async_copy(coarse_ref.at[k], out_hbm.at[k], sems.at[k])
            for k in range(pieces)
        ]
        copies.append(pltpu.make_async_copy(small_ref, small_hbm, sems.at[pieces]))
        for copy in copies:
            copy.start()
        for copy in copies:
            copy.wait()

    return pl.pallas_call(
        kernel,
        in_specs=[pl.BlockSpec(memory_space=pltpu.VMEM)] * 2,
        out_specs=[pl.BlockSpec(memory_space=pl.ANY)] * 2,
        out_shape=[jax.ShapeDtypeStruct(a.shape, a.dtype) for a in (coarse, restricted)],
        scratch_shapes=[pltpu.SemaphoreType.DMA((pieces + 1,))],
        compiler_params=pltpu.CompilerParams(vmem_limit_bytes=1 << 20),
    )(coarse, restricted)


def write_table(tab, nbr, agg, owners, base, mine, x, sizes):
    size_x, _, size_z = sizes
    elems, aggs_here = nbr.shape[1], owners.shape[1]
    per_owner = aggs_here // GROUPS
    stride_z = size_z // GROUPS
    members = elems // aggs_here
    on_face = members // 2
    channels = channels_of(size_x)
    offsets, zero_block = channel_offsets(channels, elems)
    nch = len(channels)
    square = (elems, elems)
    down = lax.broadcasted_iota(jnp.int32, square, 0)
    along = lax.broadcasted_iota(jnp.int32, square, 1)
    ids = down[:, :1]

    def flag(mask):
        return jnp.where(mask, 1, 0)

    eye = flag(down == along)
    before = flag(along < down)

    def by_row(value):
        return jnp.sum(value, axis=1, keepdims=True)

    def by_column(value):
        return jnp.sum(value, axis=0, keepdims=True)

    def column(row):
        return by_row(eye * row)

    def row(col):
        return by_column(eye * col)

    def listed(place, value):
        return by_column(flag(place == along) * value)

    def put(at, value):
        tab[at : at + 1, :elems] = value

    a_down = lax.broadcasted_iota(jnp.int32, (aggs_here, aggs_here), 0)
    a_along = lax.broadcasted_iota(jnp.int32, (aggs_here, aggs_here), 1)
    to = owners // stride_z
    turn = 3 - (2 * jnp.abs(to // 2 - mine // 2) + jnp.abs(to % 2 - mine % 2))
    turn = jnp.broadcast_to(turn, a_down.shape)
    turn = by_row(jnp.where(a_down == a_along, turn, 0))
    if per_owner > 1:
        turn_row = by_column(jnp.where(a_down == a_along, turn, 0))
        equal = flag(turn_row == turn) * flag(a_along < a_down)
        turn = turn * per_owner + by_row(equal)
    a_ids = lax.broadcasted_iota(jnp.int32, (aggs_here, elems), 0)
    order_row = by_column(flag(agg == a_ids) * turn)
    order = column(order_row)
    agg_col = column(agg)
    together = before * flag(order_row == order)
    m_place = order * members + by_row(together)

    if size_x == 2:
        listing = [(5, 0), (4, 1), (3, 2), (2, 3)]
        sources = [4, 4, 2, 3, 0, 1]
    else:
        listing = [(5, 0), (4, 1), (3, 2), (2, 3), (1, 4), (0, 5)]
        sources = [4, 5, 2, 3, 0, 1]
    sides_of, local_of, same_of = [], [], []
    for d in range(6):
        nbr_row = nbr[d : d + 1]
        nbr_col = column(nbr_row)
        local_row, local = nbr_row - base, nbr_col - base
        away_row = 1 - flag(local_row >= 0) * flag(local_row < elems)
        here = flag(local >= 0) * flag(local < elems)
        rank = by_row(before * away_row)
        place = jnp.where(here > 0, -1, rank)
        sides_of.append(listed(place, ids))
        crossing = away_row * flag(nbr_row >= 0)
        position = by_row(crossing * flag(nbr_row < nbr_col))
        index = jnp.where(here > 0, local, position + offsets[sources[d]])
        index = jnp.where(nbr_col >= 0, index, zero_block)
        near_agg = by_row(flag(local == along) * agg)
        same = here * flag(near_agg == agg_col)
        local_of.append(local)
        same_of.append(same)
        s_rank = by_row(together * (1 - row(same)))
        s_place = jnp.where(same > 0, -1, order * on_face + s_rank)
        put(nch + 1 + d, listed(s_place, ids + elems * index))
    for d, c in listing:
        put(c, sides_of[d])
    if size_x == 2:
        put(4, jnp.where(x == 0, sides_of[1], sides_of[0]))
    code = jnp.zeros_like(ids)
    for axis in (2, 1, 0):
        after = same_of[2 * axis + 1] > 0
        inner = jnp.where(after, local_of[2 * axis + 1] + elems, local_of[2 * axis])
        code = code * (2 * elems) + inner
    put(nch, listed(m_place, code * elems + ids))


def body(jacobian, prolong, residual, neighbours, agg_map, owners):
    sizes = tuple(lax.axis_size(a) for a in ("gx", "gy", "gz"))
    coarse, restricted = fused_kernel(
        neighbours.T,
        agg_map[None],
        owners[None],
        jnp.transpose(prolong, (1, 0, 2)),
        jnp.transpose(jacobian, (1, 2, 0, 3)),
        residual,
        sizes,
    )
    coarse, restricted = stored(coarse, restricted)
    return jnp.transpose(coarse, (2, 0, 1, 3)), restricted


def solution(mesh):
    spec = P(("gx", "gy", "gz"))
    return jax.shard_map(
        body,
        mesh=mesh,
        in_specs=(spec,) * 6,
        out_specs=(spec, spec),
        check_vma=False,
    )
```

```python
import jax
import jax.numpy as jnp
from jax import lax
from jax.experimental import pallas as pl
from jax.experimental.pallas import tpu as pltpu
from jax.sharding import PartitionSpec as P

LX = 4
LY = 4
LZ = 2
GROUPS = 4
LANES = 128
CHUNK = 4
AHEAD = 4
MESH = pl.DeviceIdType.MESH


def mul(a, b):
    return jnp.dot(a, b, preferred_element_type=jnp.float32)


def lane_ids(shape):
    return lax.broadcasted_iota(jnp.int32, shape, 1)


def channels_of(size_x):
    z = [("gz", 1, LX * LY, 5), ("gz", -1, LX * LY, 4)]
    y = [("gy", 1, LX * LZ, 3), ("gy", -1, LX * LZ, 2)]
    if size_x == 2:
        x = [("gx", 0, LY * LZ, None)]
    else:
        x = [("gx", 1, LY * LZ, 1), ("gx", -1, LY * LZ, 0)]
    return z + y + x


def channel_offsets(channels, elems):
    offsets, at = [], elems
    for _, _, count, _ in channels:
        offsets.append(at)
        at += count
    return offsets, at


def face_rows(count, tall):
    return count * LANES + count * 8 + tall


def partner_bits(me, r):
    high, low = me // 2, me % 2
    inner = (high + low) % 2
    cross = 1 - r // 2
    turn = (1 + r + inner * cross) % 2
    high = high + cross * (1 - 2 * high)
    low = low + turn * (1 - 2 * low)
    return high * 2 + low


def fused_kernel(neighbours, agg_map, owners, prolong, jac, residual, sizes):
    width, elems, _ = prolong.shape
    sides = jac.shape[0]
    aggs_here = owners.shape[1]
    size_x, size_y, size_z = sizes
    rest = width - LANES
    tall = pl.cdiv(width + 1, 8) * 8
    full = pl.cdiv(width + 1, 16) * 16
    pitch = elems + 1
    per_owner = aggs_here // GROUPS
    stride_z = size_z // GROUPS
    out_slots = size_z * per_owner
    members = elems // aggs_here
    on_face = members // 2
    channels = channels_of(size_x)
    offsets, zero_block = channel_offsets(channels, elems)
    nch = len(channels)
    tail = sides * LANES
    msg_rows = tail + LANES
    half = LANES // 2
    most = max(count for _, _, count, _ in channels)
    pieces = sides + 1
    early = aggs_here // 2
    step_rows = 5 if width % 5 == 0 else 1

    def kernel(nbr_ref, agg_ref, own_ref, p_hbm, j_hbm, res_ref, out_ref, rest_ref, *refs):
        tab, table_ref, praw, jraw, near, far, pool, pt, jm = refs[:9]
        sends, recvs = refs[9 : 9 + nch], refs[9 + nch : 9 + 2 * nch]
        refs = refs[9 + 2 * nch :]
        remf, farf, msg, msg_rem, msg_far, racc, acc = refs[:7]
        rows_ref, mixed, mixed_rem, mixed_rest = refs[7:11]
        t_sem, p_sem, j_sem, f_send, f_recv, r_send, r_recv, self_sem = refs[11:]
        me = {"gx": lax.axis_index("gx"), "gy": lax.axis_index("gy"), "gz": lax.axis_index("gz")}
        size = {"gx": size_x, "gy": size_y, "gz": size_z}
        me_z = me["gz"]

        p_copy = pltpu.make_async_copy(p_hbm, praw, p_sem)
        p_copy.start()

        def block_at(i):
            return (i + 1) * (i < 2) + i * (i > 2)

        def j_copy(i):
            slot = i % AHEAD
            return pltpu.make_async_copy(
                j_hbm.at[block_at(i)], jraw.at[slot], j_sem.at[slot]
            )

        barrier = pltpu.get_barrier_semaphore()
        for step in range(1, size_z):
            to = lax.rem(me_z + step, size_z)
            pl.semaphore_signal(barrier, inc=1, device_id={"gz": to}, device_id_type=MESH)
        expected = size_z - 1
        if size_x == 2:
            pl.semaphore_signal(
                barrier, inc=1, device_id={"gx": 1 - me["gx"]}, device_id_type=MESH
            )
            expected = expected + 1
        for axis in ["gy"] + (["gx"] if size_x > 2 else []):
            for step in (1, -1):
                there = me[axis] + step
                exists = (there >= 0) & (there < size[axis])

                @pl.when(exists)
                def _(axis=axis, there=there):
                    pl.semaphore_signal(
                        barrier, inc=1, device_id={axis: there}, device_id_type=MESH
                    )

                expected = expected + exists.astype(jnp.int32)

        msg_far[...] = jnp.zeros_like(msg_far)
        for sub in range(per_owner):
            for piece, slot in ((5, sub), (6, out_slots - per_owner + sub)):
                rows_ref[slot, piece * LANES : (piece + 1) * LANES, :] = jnp.zeros(
                    (LANES, LANES), rows_ref.dtype
                )
        pool[zero_block] = jnp.zeros(pool.shape[1:], pool.dtype)

        def spread(load, last):
            @pl.loop(0, width // step_rows)
            def _(c):
                part = load(c).astype(jnp.float32)
                for i in range(step_rows):
                    rows = pl.ds((c * step_rows + i) * pitch, elems)
                    near[rows, :] = part[i, :, :LANES]
                    far[rows, :rest] = part[i, :, LANES:]

            near[pl.ds(width * pitch, elems), :] = last[:, :LANES]
            far[pl.ds(width * pitch, elems), :rest] = last[:, LANES:]

        def block(e):
            rows = pl.ds(e, width + 1, stride=pitch)
            right = far[rows, :]
            right = jnp.where(lane_ids(right.shape) < rest, right, 0.0)
            both = jnp.concatenate([near[rows, :], right], axis=1)[:, :full]
            below = jnp.zeros((full - width - 1, full), jnp.float32)
            return jnp.concatenate([both, below], axis=0)

        device = (me["gx"] * size_y + me["gy"]) * size_z + me_z
        write_table(
            tab,
            nbr_ref[...],
            agg_ref[...] - device * aggs_here,
            own_ref[...],
            device * elems,
            me_z // stride_z,
            me["gx"],
            sizes,
        )
        t_copy = pltpu.make_async_copy(tab, table_ref, t_sem)
        t_copy.start()
        p_copy.wait()
        for k in range(AHEAD):
            j_copy(k).start()
        spread(
            lambda c: praw[pl.ds(c * step_rows, step_rows)],
            jnp.zeros((elems, width), jnp.float32),
        )

        @pl.loop(0, elems // 4)
        def _(group):
            for u in range(4):
                e = group * 4 + u
                pool[e] = block(e)[:, :width].astype(pool.dtype)

        t_copy.wait()
        pl.semaphore_wait(barrier, expected)

        def face_target(c):
            axis, step, _, _ = channels[c]
            return {axis: 1 - me[axis] if step == 0 else me[axis] + step}

        def when_sent(c):
            axis, step, _, _ = channels[c]
            if step == 0:
                return lambda f: f()
            there = me[axis] + step
            return pl.when((there >= 0) & (there < size[axis]))

        def when_received(c):
            axis, step, _, _ = channels[c]
            if step == 0:
                return lambda f: f()
            there = me[axis] - step
            return pl.when((there >= 0) & (there < size[axis]))

        def face_parts(c):
            count = channels[c][2]
            parts = [(n * LANES, CHUNK * LANES) for n in range(0, count, CHUNK)]
            return parts + [(count * LANES, count * 8 + full)]

        def face_copy(c, part):
            start, rows = face_parts(c)[part]
            return pltpu.make_async_remote_copy(
                src_ref=sends[c].at[pl.ds(start, rows)],
                dst_ref=recvs[c].at[pl.ds(start, rows)],
                send_sem=f_send.at[c, part],
                recv_sem=f_recv.at[c, part],
                device_id=face_target(c),
                device_id_type=MESH,
            )

        def pack(c, n):
            whole = pool[table_ref[c, n] % elems]
            sends[c][n * LANES : (n + 1) * LANES, :] = whole[:LANES, :LANES]
            remf[c, n * 8 : (n + 1) * 8, :] = whole[LANES:tall, :LANES].astype(jnp.float32)
            farf[c, :, n * rest : (n + 1) * rest] = whole[:, LANES:width].astype(jnp.float32)

        def pack_tail(c):
            count = channels[c][2]
            at = count * LANES
            sends[c][at : at + count * 8, :] = remf[c, : count * 8, :].astype(jnp.bfloat16)
            sends[c][at + count * 8 : at + count * 8 + full, :] = farf[c].astype(jnp.bfloat16)

        def send_faces(group):
            parts = max(len(face_parts(c)) for c in group)
            for part in range(parts):
                for c in group:
                    if part < len(face_parts(c)):
                        if part < len(face_parts(c)) - 1:
                            for n in range(part * CHUNK, (part + 1) * CHUNK):
                                pack(c, n)
                        else:
                            pack_tail(c)

                        @when_sent(c)
                        def _(c=c, part=part):
                            face_copy(c, part).start()

        def take_faces(group):
            for c in group:

                @when_received(c)
                def _(c=c):
                    for part in range(len(face_parts(c))):
                        face_copy(c, part).wait_recv()
                    count = channels[c][2]
                    at = count * LANES
                    remf[c, : count * 8, :] = recvs[c][at : at + count * 8, :].astype(jnp.float32)
                    farf[c] = recvs[c][at + count * 8 : at + count * 8 + full, :].astype(
                        jnp.float32
                    )
                    for n in range(count):
                        to = offsets[c] + n
                        pool[to, :LANES, :LANES] = recvs[c][n * LANES : (n + 1) * LANES, :]
                        below = remf[c, n * 8 : (n + 1) * 8, :]
                        below = jnp.concatenate([below, jnp.zeros_like(below)], axis=0)
                        pool[to, LANES:full, :LANES] = below.astype(pool.dtype)
                        pool[to, :, LANES:width] = farf[
                            c, :, n * rest : (n + 1) * rest
                        ].astype(pool.dtype)

        send_faces([0, 1])
        send_faces(list(range(2, nch)))

        @pl.loop(0, elems // 4)
        def _(group):
            for u in range(4):
                e = group * 4 + u
                pt[e] = block(e).T[:tall].astype(pt.dtype)

        def lay_out(i):
            k = block_at(i)
            j_copy(i).wait()
            own = (k == 0).astype(jnp.float32)
            spread(
                lambda c: jraw[i % AHEAD, pl.ds(c * step_rows, step_rows)],
                res_ref[...].astype(jnp.float32) * own,
            )

            @pl.when(i + AHEAD < sides)
            def _():
                j_copy(i + AHEAD).start()

            @pl.loop(0, elems // 4)
            def _(group):
                for u in range(4):
                    e = group * 4 + u
                    jm[k, e] = block(e).astype(jm.dtype)

        my_group = me_z // stride_z

        def target_of(r):
            return partner_bits(my_group, r // per_owner) * stride_z

        def slot_of(z, r):
            return z * per_owner + r % per_owner

        def row_copy(r, piece):
            at = pl.ds(pl.multiple_of(piece * LANES, LANES), LANES)
            slot = slot_of(me_z, r)
            return pltpu.make_async_remote_copy(
                src_ref=msg.at[r, at],
                dst_ref=rows_ref.at[slot, at],
                send_sem=r_send.at[r, piece],
                recv_sem=r_recv.at[slot, piece],
                device_id={"gz": target_of(r)},
                device_id_type=MESH,
            )

        def self_copy(r, piece):
            at = pl.ds(pl.multiple_of(piece * LANES, LANES), LANES)
            return pltpu.make_async_copy(
                msg.at[r, at],
                rows_ref.at[slot_of(me_z, r), at],
                self_sem.at[r % per_owner, piece],
            )

        def send_row(r, piece):
            sent = present(piece, me_z)

            @pl.when((target_of(r) != me_z) & sent)
            def _():
                row_copy(r, piece).start()

            @pl.when((target_of(r) == me_z) & sent)
            def _():
                self_copy(r, piece).start()

        def emit(r, s, value):
            msg[r, s * LANES : (s + 1) * LANES, :] = value[:LANES, :LANES].astype(msg.dtype)
            msg_rem[r, s * 8 : (s + 1) * 8, :] = value[LANES:tall, :LANES]
            msg_far[r, :, s * rest : (s + 1) * rest] = value[:, LANES:width]

        def present(piece, z):
            if piece == 5:
                return z > 0
            if piece == 6:
                return z < size_z - 1
            return True

        def side_sum(r, d):
            total = None
            for m in range(on_face):
                code = table_ref[nch + 1 + d, r * on_face + m]
                e, n = code % elems, jnp.clip(code // elems, 0, zero_block)
                product = mul(jm[1 + d, e], pool[n]).astype(jnp.bfloat16)
                triple = mul(pt[e], product)
                total = triple if total is None else total + triple
            return total

        def own_slot(r):
            acc[...] = jnp.zeros_like(acc)
            racc[...] = jnp.zeros_like(racc)

            @pl.loop(0, members // 4)
            def _(pair):
                total = None
                for u in range(4):
                    code = table_ref[nch, r * members + pair * 4 + u]
                    e, code = code % elems, code // elems
                    product = mul(jm[0, e], pool[e])
                    for axis in range(3):
                        x, code = code % (2 * elems), code // (2 * elems)
                        k = 1 + 2 * axis + x // elems
                        product = product + mul(jm[k, e], pool[x % elems])
                    racc[...] += product[LANES:tall]
                    triple = mul(pt[e], product.astype(jnp.bfloat16))
                    total = triple if total is None else total + triple
                acc[...] += total

            below = racc[...]
            spare = lax.broadcasted_iota(jnp.int32, below.shape, 0) == width - LANES
            acc[LANES:tall, :] += jnp.where(spare, below, 0.0)
            emit(r, 0, acc[...])
            send_row(r, 0)

        def pack_row_tail(r):
            msg_rem[r, sides * 8 : (sides + 1) * 8, :] = msg_far[r, LANES:tall, :]
            msg[r, tail : tail + half, :] = msg_rem[r].astype(msg.dtype)
            right = pltpu.roll(msg_far[r, half:LANES, :], half, 1)
            left = msg_far[r, :half, :]
            folded = jnp.where(lane_ids(left.shape) < half, left, right)
            msg[r, tail + half : msg_rows, :] = folded.astype(msg.dtype)

        def side_slots(r, axis):
            pair = (2 * axis, 2 * axis + 1)
            for d, total in [(d, side_sum(r, d)) for d in pair]:
                emit(r, 1 + d, total)
            if axis == 2:
                pack_row_tail(r)
            for d in pair:
                send_row(r, 1 + d)
            if axis == 2:
                send_row(r, sides)

        axis_faces = [list(range(4, nch)), [2, 3], [0, 1]]

        @pl.loop(0, 2)
        def _(part):
            first, last = part * early, part * early + early

            @pl.when(part == 0)
            def _():
                pl.loop(0, 2)(lay_out)
                take_faces(axis_faces[0])

            pl.loop(first, last)(lambda r: side_slots(r, 0))

            @pl.when(part == 0)
            def _():
                pl.loop(2, sides)(lay_out)

            pl.loop(first, last)(own_slot)
            for axis in (1, 2):

                @pl.when(part == 0)
                def _(axis=axis):
                    take_faces(axis_faces[axis])

                pl.loop(first, last)(lambda r, axis=axis: side_slots(r, axis))

        owner = me_z % stride_z == 0

        def row_arrival(slot, piece):
            at = pl.ds(piece * LANES, LANES)
            return pltpu.make_async_remote_copy(
                src_ref=msg.at[0, at],
                dst_ref=rows_ref.at[slot, at],
                send_sem=r_send.at[0, piece],
                recv_sem=r_recv.at[slot, piece],
                device_id={"gz": me_z},
                device_id_type=MESH,
            )

        def arrive(piece):
            for slot in range(out_slots):
                sent = present(piece, slot // per_owner)
                if sent is False:
                    continue
                mine = slot // per_owner == me_z

                @pl.when(mine)
                def _(slot=slot):
                    self_copy(aggs_here - per_owner + slot % per_owner, piece).wait()

                @pl.when(jnp.logical_not(mine))
                def _(slot=slot):
                    row_arrival(slot, piece).wait_recv()

        def scatter(ref, slot, start, value):
            count = value.shape[0]
            ref[pl.ds(start * out_slots + slot, count, stride=out_slots), :] = value

        def gathered(ref, count):
            value = ref[: count * out_slots, :].astype(jnp.bfloat16)
            return value.reshape(count, out_slots, LANES)

        def unpack():
            for s in [1, 2, 0, *range(3, sides)]:
                arrive(s)
                for slot in range(out_slots):
                    block_of = rows_ref[slot, s * LANES : (s + 1) * LANES, :]
                    scatter(mixed, slot, 0, block_of.astype(jnp.float32))
                out_ref[s, :LANES, :, :LANES] = gathered(mixed, LANES)

            arrive(sides)
            for slot in range(out_slots):
                below = rows_ref[slot, tail : tail + half, :].astype(jnp.float32)
                folded = rows_ref[slot, tail + half : msg_rows, :].astype(jnp.float32)
                scatter(mixed, slot, 0, folded)
                scatter(mixed, slot, half, pltpu.roll(folded, half, 1))
                scatter(mixed, slot, LANES, below[sides * 8 :])
                for s in range(sides):
                    scatter(mixed_rem.at[s], slot, 0, below[s * 8 : (s + 1) * 8])
                mixed_rest[slot : slot + 1, :LANES] = below[rest : rest + 1]
                at = sides * 8 + rest
                mixed_rest[slot : slot + 1, LANES:] = below[at : at + 1, :rest]
            rest_ref[...] = mixed_rest[:out_slots].astype(rest_ref.dtype)
            for s in range(sides):
                low = gathered(mixed_rem.at[s], 8)
                out_ref[s, LANES:, :, :LANES] = low[:rest]
                right = mixed[...]
                if s > 0:
                    right = pltpu.roll(right, LANES - s * rest, 1)
                right = right.astype(jnp.bfloat16).reshape(tall, out_slots, LANES)
                out_ref[s, :, :, LANES:] = right[:width, :, :rest]

        if stride_z == 1:
            unpack()
        else:
            pl.when(owner)(unpack)

            @pl.when(jnp.logical_not(owner))
            def _():
                out_ref[...] = jnp.zeros_like(out_ref)
                rest_ref[...] = jnp.zeros_like(rest_ref)

        for c in range(nch):

            @when_sent(c)
            def _(c=c):
                for part in range(len(face_parts(c))):
                    face_copy(c, part).wait_send()

        @pl.loop(0, aggs_here)
        def _(r):
            @pl.when(target_of(r) != me_z)
            def _():
                for piece in range(pieces):

                    @pl.when(present(piece, me_z))
                    def _(piece=piece):
                        row_copy(r, piece).wait_send()

    bf16, f32 = jnp.bfloat16, jnp.float32
    spread_rows = (width + 1) * pitch
    faces = [pltpu.VMEM((face_rows(count, full), LANES), bf16) for _, _, count, _ in channels]
    parts = most // CHUNK + 1
    table_rows = pl.cdiv(nch + sides, 8) * 8
    scratch = [
        pltpu.VMEM((table_rows, LANES), jnp.int32),
        pltpu.SMEM((table_rows, LANES), jnp.int32),
        pltpu.VMEM((width, elems, width), bf16),
        pltpu.VMEM((AHEAD, width, elems, width), bf16),
        pltpu.VMEM((spread_rows, LANES), f32),
        pltpu.VMEM((spread_rows, LANES), f32),
        pltpu.VMEM((zero_block + 1, full, width), bf16),
        pltpu.VMEM((elems, tall, full), bf16),
        pltpu.VMEM((sides, elems, full, full), bf16),
        *faces,
        *faces,
        pltpu.VMEM((nch, most * 8, LANES), f32),
        pltpu.VMEM((nch, full, LANES), f32),
        pltpu.VMEM((aggs_here, msg_rows, LANES), bf16),
        pltpu.VMEM((aggs_here, (sides + 1) * 8, LANES), f32),
        pltpu.VMEM((aggs_here, tall, LANES), f32),
        pltpu.VMEM((8, width), f32),
        pltpu.VMEM((tall, width), f32),
        pltpu.VMEM((out_slots, msg_rows, LANES), bf16),
        pltpu.VMEM((tall * out_slots, LANES), f32),
        pltpu.VMEM((sides, 8 * out_slots, LANES), f32),
        pltpu.VMEM((pl.cdiv(out_slots, 8) * 8, width), f32),
        pltpu.SemaphoreType.DMA,
        pltpu.SemaphoreType.DMA,
        pltpu.SemaphoreType.DMA((AHEAD,)),
        pltpu.SemaphoreType.DMA((nch, parts)),
        pltpu.SemaphoreType.DMA((nch, parts)),
        pltpu.SemaphoreType.DMA((aggs_here, pieces)),
        pltpu.SemaphoreType.DMA((out_slots, pieces)),
        pltpu.SemaphoreType.DMA((per_owner, pieces)),
    ]
    return pl.pallas_call(
        kernel,
        in_specs=[pl.BlockSpec(memory_space=pltpu.VMEM)] * 3
        + [pl.BlockSpec(memory_space=pl.ANY)] * 2
        + [pl.BlockSpec(memory_space=pltpu.VMEM)],
        out_specs=[pl.BlockSpec(memory_space=pltpu.VMEM)] * 2,
        out_shape=[
            pltpu.VMEM((sides, width, out_slots, width), bf16),
            pltpu.VMEM((out_slots, width), bf16),
        ],
        scratch_shapes=scratch,
        compiler_params=pltpu.CompilerParams(
            collective_id=0, has_side_effects=True, vmem_limit_bytes=54 << 20
        ),
    )(neighbours, agg_map, owners, prolong, jac, residual)


def stored(coarse, restricted):
    pieces = coarse.shape[0]

    def kernel(coarse_ref, small_ref, out_hbm, small_hbm, sems):
        copies = [
            pltpu.make_async_copy(coarse_ref.at[k], out_hbm.at[k], sems.at[k])
            for k in range(pieces)
        ]
        copies.append(pltpu.make_async_copy(small_ref, small_hbm, sems.at[pieces]))
        for copy in copies:
            copy.start()
        for copy in copies:
            copy.wait()

    return pl.pallas_call(
        kernel,
        in_specs=[pl.BlockSpec(memory_space=pltpu.VMEM)] * 2,
        out_specs=[pl.BlockSpec(memory_space=pl.ANY)] * 2,
        out_shape=[jax.ShapeDtypeStruct(a.shape, a.dtype) for a in (coarse, restricted)],
        scratch_shapes=[pltpu.SemaphoreType.DMA((pieces + 1,))],
        compiler_params=pltpu.CompilerParams(vmem_limit_bytes=1 << 20),
    )(coarse, restricted)


def write_table(tab, nbr, agg, owners, base, mine, x, sizes):
    size_x, _, size_z = sizes
    elems, aggs_here = nbr.shape[1], owners.shape[1]
    per_owner = aggs_here // GROUPS
    stride_z = size_z // GROUPS
    members = elems // aggs_here
    on_face = members // 2
    channels = channels_of(size_x)
    offsets, zero_block = channel_offsets(channels, elems)
    nch = len(channels)
    square = (elems, elems)
    down = lax.broadcasted_iota(jnp.int32, square, 0)
    along = lax.broadcasted_iota(jnp.int32, square, 1)
    ids = down[:, :1]

    def flag(mask):
        return jnp.where(mask, 1, 0)

    eye = flag(down == along)
    before = flag(along < down)

    def by_row(value):
        return jnp.sum(value, axis=1, keepdims=True)

    def by_column(value):
        return jnp.sum(value, axis=0, keepdims=True)

    def column(row):
        return by_row(eye * row)

    def row(col):
        return by_column(eye * col)

    def listed(place, value):
        return by_column(flag(place == along) * value)

    def put(at, value):
        tab[at : at + 1, :elems] = value

    a_down = lax.broadcasted_iota(jnp.int32, (aggs_here, aggs_here), 0)
    a_along = lax.broadcasted_iota(jnp.int32, (aggs_here, aggs_here), 1)
    to = owners // stride_z
    crosses = jnp.abs(to // 2 - mine // 2)
    flips = jnp.abs(to % 2 - mine % 2)
    turn = 2 * (1 - crosses) + (1 + flips + crosses * ((mine // 2 + mine % 2) % 2)) % 2
    turn = jnp.broadcast_to(turn, a_down.shape)
    turn = by_row(jnp.where(a_down == a_along, turn, 0))
    if per_owner > 1:
        turn_row = by_column(jnp.where(a_down == a_along, turn, 0))
        equal = flag(turn_row == turn) * flag(a_along < a_down)
        turn = turn * per_owner + by_row(equal)
    a_ids = lax.broadcasted_iota(jnp.int32, (aggs_here, elems), 0)
    order_row = by_column(flag(agg == a_ids) * turn)
    order = column(order_row)
    agg_col = column(agg)
    together = before * flag(order_row == order)
    m_place = order * members + by_row(together)

    if size_x == 2:
        listing = [(5, 0), (4, 1), (3, 2), (2, 3)]
        sources = [4, 4, 2, 3, 0, 1]
    else:
        listing = [(5, 0), (4, 1), (3, 2), (2, 3), (1, 4), (0, 5)]
        sources = [4, 5, 2, 3, 0, 1]
    sides_of, local_of, same_of = [], [], []
    for d in range(6):
        nbr_row = nbr[d : d + 1]
        nbr_col = column(nbr_row)
        local_row, local = nbr_row - base, nbr_col - base
        away_row = 1 - flag(local_row >= 0) * flag(local_row < elems)
        here = flag(local >= 0) * flag(local < elems)
        rank = by_row(before * away_row)
        place = jnp.where(here > 0, -1, rank)
        sides_of.append(listed(place, ids))
        crossing = away_row * flag(nbr_row >= 0)
        position = by_row(crossing * flag(nbr_row < nbr_col))
        index = jnp.where(here > 0, local, position + offsets[sources[d]])
        index = jnp.where(nbr_col >= 0, index, zero_block)
        near_agg = by_row(flag(local == along) * agg)
        same = here * flag(near_agg == agg_col)
        local_of.append(local)
        same_of.append(same)
        s_rank = by_row(together * (1 - row(same)))
        s_place = jnp.where(same > 0, -1, order * on_face + s_rank)
        put(nch + 1 + d, listed(s_place, ids + elems * index))
    for d, c in listing:
        put(c, sides_of[d])
    if size_x == 2:
        put(4, jnp.where(x == 0, sides_of[1], sides_of[0]))
    code = jnp.zeros_like(ids)
    for axis in (2, 1, 0):
        after = same_of[2 * axis + 1] > 0
        inner = jnp.where(after, local_of[2 * axis + 1] + elems, local_of[2 * axis])
        code = code * (2 * elems) + inner
    put(nch, listed(m_place, code * elems + ids))


def body(jacobian, prolong, residual, neighbours, agg_map, owners):
    sizes = tuple(lax.axis_size(a) for a in ("gx", "gy", "gz"))
    coarse, restricted = fused_kernel(
        neighbours.T,
        agg_map[None],
        owners[None],
        jnp.transpose(prolong, (1, 0, 2)),
        jnp.transpose(jacobian, (1, 2, 0, 3)),
        residual,
        sizes,
    )
    coarse, restricted = stored(coarse, restricted)
    return jnp.transpose(coarse, (2, 0, 1, 3)), restricted


def solution(mesh):
    spec = P(("gx", "gy", "gz"))
    return jax.shard_map(
        body,
        mesh=mesh,
        in_specs=(spec,) * 6,
        out_specs=(spec, spec),
        check_vma=False,
    )
```

```python
import jax
import jax.numpy as jnp
from jax import lax
from jax.experimental import pallas as pl
from jax.experimental.pallas import tpu as pltpu
from jax.sharding import PartitionSpec as P

LX = 4
LY = 4
LZ = 2
GROUPS = 4
LANES = 128
CHUNK = 4
AHEAD = 4
MESH = pl.DeviceIdType.MESH


def mul(a, b):
    return jnp.dot(a, b, preferred_element_type=jnp.float32)


def lane_ids(shape):
    return lax.broadcasted_iota(jnp.int32, shape, 1)


def channels_of(size_x):
    z = [("gz", 1, LX * LY, 5), ("gz", -1, LX * LY, 4)]
    y = [("gy", 1, LX * LZ, 3), ("gy", -1, LX * LZ, 2)]
    if size_x == 2:
        x = [("gx", 0, LY * LZ, None)]
    else:
        x = [("gx", 1, LY * LZ, 1), ("gx", -1, LY * LZ, 0)]
    return z + y + x


def channel_offsets(channels, elems):
    offsets, at = [], elems
    for _, _, count, _ in channels:
        offsets.append(at)
        at += count
    return offsets, at


def face_rows(count, tall):
    return count * LANES + count * 8 + tall


def partner_bits(me, r):
    high, low = me // 2, me % 2
    inner = (high + low) % 2
    cross = 1 - r // 2
    turn = (1 + r + inner * cross) % 2
    high = high + cross * (1 - 2 * high)
    low = low + turn * (1 - 2 * low)
    return high * 2 + low


def fused_kernel(neighbours, agg_map, owners, prolong, jac, residual, sizes):
    width, elems, _ = prolong.shape
    sides = jac.shape[0]
    aggs_here = owners.shape[1]
    size_x, size_y, size_z = sizes
    rest = width - LANES
    tall = pl.cdiv(width + 1, 8) * 8
    full = pl.cdiv(width + 1, 16) * 16
    pitch = elems + 1
    per_owner = aggs_here // GROUPS
    stride_z = size_z // GROUPS
    out_slots = size_z * per_owner
    members = elems // aggs_here
    on_face = members // 2
    channels = channels_of(size_x)
    offsets, zero_block = channel_offsets(channels, elems)
    nch = len(channels)
    tail = sides * LANES
    msg_rows = tail + LANES
    half = LANES // 2
    most = max(count for _, _, count, _ in channels)
    pieces = sides + 1
    early = aggs_here // 2
    step_rows = 5 if width % 5 == 0 else 1

    def kernel(nbr_ref, agg_ref, own_ref, p_hbm, j_hbm, res_ref, out_ref, rest_ref, *refs):
        tab, table_ref, praw, jraw, near, far, pool, pt, jm = refs[:9]
        sends, recvs = refs[9 : 9 + nch], refs[9 + nch : 9 + 2 * nch]
        refs = refs[9 + 2 * nch :]
        remf, farf, msg, msg_rem, msg_far, racc, acc = refs[:7]
        rows_ref, mixed, mixed_rem, mixed_rest = refs[7:11]
        t_sem, p_sem, j_sem, f_send, f_recv, r_send, r_recv, self_sem, relay_sem = refs[11:]
        me = {"gx": lax.axis_index("gx"), "gy": lax.axis_index("gy"), "gz": lax.axis_index("gz")}
        size = {"gx": size_x, "gy": size_y, "gz": size_z}
        me_z = me["gz"]

        p_copy = pltpu.make_async_copy(p_hbm, praw, p_sem)
        p_copy.start()

        def block_at(i):
            return (i + 1) * (i < 2) + i * (i > 2)

        def j_copy(i):
            slot = i % AHEAD
            return pltpu.make_async_copy(
                j_hbm.at[block_at(i)], jraw.at[slot], j_sem.at[slot]
            )

        barrier = pltpu.get_barrier_semaphore()
        expected = 0
        if size_x == 2:
            pl.semaphore_signal(
                barrier, inc=1, device_id={"gx": 1 - me["gx"]}, device_id_type=MESH
            )
            expected = expected + 1
        for axis in ["gz", "gy"] + (["gx"] if size_x > 2 else []):
            for step in (1, -1):
                there = me[axis] + step
                exists = (there >= 0) & (there < size[axis])

                @pl.when(exists)
                def _(axis=axis, there=there):
                    pl.semaphore_signal(
                        barrier, inc=1, device_id={axis: there}, device_id_type=MESH
                    )

                expected = expected + exists.astype(jnp.int32)

        msg_far[...] = jnp.zeros_like(msg_far)
        for sub in range(per_owner):
            for piece, slot in ((5, sub), (6, out_slots - per_owner + sub)):
                rows_ref[slot, piece * LANES : (piece + 1) * LANES, :] = jnp.zeros(
                    (LANES, LANES), rows_ref.dtype
                )
        pool[zero_block] = jnp.zeros(pool.shape[1:], pool.dtype)

        def spread(load, last):
            @pl.loop(0, width // step_rows)
            def _(c):
                part = load(c).astype(jnp.float32)
                for i in range(step_rows):
                    rows = pl.ds((c * step_rows + i) * pitch, elems)
                    near[rows, :] = part[i, :, :LANES]
                    far[rows, :rest] = part[i, :, LANES:]

            near[pl.ds(width * pitch, elems), :] = last[:, :LANES]
            far[pl.ds(width * pitch, elems), :rest] = last[:, LANES:]

        def block(e):
            rows = pl.ds(e, width + 1, stride=pitch)
            right = far[rows, :]
            right = jnp.where(lane_ids(right.shape) < rest, right, 0.0)
            both = jnp.concatenate([near[rows, :], right], axis=1)[:, :full]
            below = jnp.zeros((full - width - 1, full), jnp.float32)
            return jnp.concatenate([both, below], axis=0)

        device = (me["gx"] * size_y + me["gy"]) * size_z + me_z
        write_table(
            tab,
            nbr_ref[...],
            agg_ref[...] - device * aggs_here,
            own_ref[...],
            device * elems,
            me_z // stride_z,
            me["gx"],
            sizes,
        )
        t_copy = pltpu.make_async_copy(tab, table_ref, t_sem)
        t_copy.start()
        p_copy.wait()
        for k in range(AHEAD):
            j_copy(k).start()
        spread(
            lambda c: praw[pl.ds(c * step_rows, step_rows)],
            jnp.zeros((elems, width), jnp.float32),
        )

        @pl.loop(0, elems // 4)
        def _(group):
            for u in range(4):
                e = group * 4 + u
                pool[e] = block(e)[:, :width].astype(pool.dtype)

        t_copy.wait()

        def face_target(c):
            axis, step, _, _ = channels[c]
            return {axis: 1 - me[axis] if step == 0 else me[axis] + step}

        def when_sent(c):
            axis, step, _, _ = channels[c]
            if step == 0:
                return lambda f: f()
            there = me[axis] + step
            return pl.when((there >= 0) & (there < size[axis]))

        def when_received(c):
            axis, step, _, _ = channels[c]
            if step == 0:
                return lambda f: f()
            there = me[axis] - step
            return pl.when((there >= 0) & (there < size[axis]))

        def face_parts(c):
            count = channels[c][2]
            parts = [(n * LANES, CHUNK * LANES) for n in range(0, count, CHUNK)]
            return parts + [(count * LANES, count * 8 + full)]

        def face_copy(c, part):
            start, rows = face_parts(c)[part]
            return pltpu.make_async_remote_copy(
                src_ref=sends[c].at[pl.ds(start, rows)],
                dst_ref=recvs[c].at[pl.ds(start, rows)],
                send_sem=f_send.at[c, part],
                recv_sem=f_recv.at[c, part],
                device_id=face_target(c),
                device_id_type=MESH,
            )

        def pack(c, n):
            whole = pool[table_ref[c, n] % elems]
            sends[c][n * LANES : (n + 1) * LANES, :] = whole[:LANES, :LANES]
            remf[c, n * 8 : (n + 1) * 8, :] = whole[LANES:tall, :LANES].astype(jnp.float32)
            farf[c, :, n * rest : (n + 1) * rest] = whole[:, LANES:width].astype(jnp.float32)

        def pack_tail(c):
            count = channels[c][2]
            at = count * LANES
            sends[c][at : at + count * 8, :] = remf[c, : count * 8, :].astype(jnp.bfloat16)
            sends[c][at + count * 8 : at + count * 8 + full, :] = farf[c].astype(jnp.bfloat16)

        def pack_faces(group):
            for c in group:
                for n in range(channels[c][2]):
                    pack(c, n)
                pack_tail(c)

        def send_faces(group):
            for part in range(max(len(face_parts(c)) for c in group)):
                for c in group:
                    if part < len(face_parts(c)):

                        @when_sent(c)
                        def _(c=c, part=part):
                            face_copy(c, part).start()

        def take_faces(group):
            for c in group:

                @when_received(c)
                def _(c=c):
                    for part in range(len(face_parts(c))):
                        face_copy(c, part).wait_recv()
                    count = channels[c][2]
                    at = count * LANES
                    remf[c, : count * 8, :] = recvs[c][at : at + count * 8, :].astype(jnp.float32)
                    farf[c] = recvs[c][at + count * 8 : at + count * 8 + full, :].astype(
                        jnp.float32
                    )
                    for n in range(count):
                        to = offsets[c] + n
                        pool[to, :LANES, :LANES] = recvs[c][n * LANES : (n + 1) * LANES, :]
                        below = remf[c, n * 8 : (n + 1) * 8, :]
                        below = jnp.concatenate([below, jnp.zeros_like(below)], axis=0)
                        pool[to, LANES:full, :LANES] = below.astype(pool.dtype)
                        pool[to, :, LANES:width] = farf[
                            c, :, n * rest : (n + 1) * rest
                        ].astype(pool.dtype)

        pack_faces(list(range(nch)))
        pl.semaphore_wait(barrier, expected)
        send_faces([0, 1])
        send_faces(list(range(2, nch)))

        @pl.loop(0, elems // 4)
        def _(group):
            for u in range(4):
                e = group * 4 + u
                pt[e] = block(e).T[:tall].astype(pt.dtype)

        def lay_out(i):
            k = block_at(i)
            j_copy(i).wait()
            own = (k == 0).astype(jnp.float32)
            spread(
                lambda c: jraw[i % AHEAD, pl.ds(c * step_rows, step_rows)],
                res_ref[...].astype(jnp.float32) * own,
            )

            @pl.when(i + AHEAD < sides)
            def _():
                j_copy(i + AHEAD).start()

            @pl.loop(0, elems // 4)
            def _(group):
                for u in range(4):
                    e = group * 4 + u
                    jm[k, e] = block(e).astype(jm.dtype)

        my_group = me_z // stride_z

        def target_of(r):
            return partner_bits(my_group, r // per_owner) * stride_z

        def slot_of(z, r):
            return z * per_owner + r % per_owner

        def row_copy(r, piece):
            at = pl.ds(pl.multiple_of(piece * LANES, LANES), LANES)
            slot = slot_of(me_z, r)
            return pltpu.make_async_remote_copy(
                src_ref=msg.at[r, at],
                dst_ref=rows_ref.at[slot, at],
                send_sem=r_send.at[r, piece],
                recv_sem=r_recv.at[slot, piece],
                device_id={"gz": target_of(r)},
                device_id_type=MESH,
            )

        def self_copy(r, piece):
            at = pl.ds(pl.multiple_of(piece * LANES, LANES), LANES)
            return pltpu.make_async_copy(
                msg.at[r, at],
                rows_ref.at[slot_of(me_z, r), at],
                self_sem.at[r % per_owner, piece],
            )

        def send_row(r, piece):
            sent = present(piece, me_z)

            @pl.when((target_of(r) != me_z) & sent)
            def _():
                row_copy(r, piece).start()

            @pl.when((target_of(r) == me_z) & sent)
            def _():
                self_copy(r, piece).start()

        def emit(r, s, value):
            msg[r, s * LANES : (s + 1) * LANES, :] = value[:LANES, :LANES].astype(msg.dtype)
            msg_rem[r, s * 8 : (s + 1) * 8, :] = value[LANES:tall, :LANES]
            msg_far[r, :, s * rest : (s + 1) * rest] = value[:, LANES:width]

        def present(piece, z):
            if piece == 5:
                return z > 0
            if piece == 6:
                return z < size_z - 1
            return True

        def side_sum(r, d):
            total = None
            for m in range(on_face):
                code = table_ref[nch + 1 + d, r * on_face + m]
                e, n = code % elems, jnp.clip(code // elems, 0, zero_block)
                product = mul(jm[1 + d, e], pool[n]).astype(jnp.bfloat16)
                triple = mul(pt[e], product)
                total = triple if total is None else total + triple
            return total

        def own_slot(r):
            acc[...] = jnp.zeros_like(acc)
            racc[...] = jnp.zeros_like(racc)

            @pl.loop(0, members // 4)
            def _(pair):
                total = None
                for u in range(4):
                    code = table_ref[nch, r * members + pair * 4 + u]
                    e, code = code % elems, code // elems
                    product = mul(jm[0, e], pool[e])
                    for axis in range(3):
                        x, code = code % (2 * elems), code // (2 * elems)
                        k = 1 + 2 * axis + x // elems
                        product = product + mul(jm[k, e], pool[x % elems])
                    racc[...] += product[LANES:tall]
                    triple = mul(pt[e], product.astype(jnp.bfloat16))
                    total = triple if total is None else total + triple
                acc[...] += total

            below = racc[...]
            spare = lax.broadcasted_iota(jnp.int32, below.shape, 0) == width - LANES
            acc[LANES:tall, :] += jnp.where(spare, below, 0.0)
            emit(r, 0, acc[...])
            send_row(r, 0)

        def pack_row_tail(r):
            msg_rem[r, sides * 8 : (sides + 1) * 8, :] = msg_far[r, LANES:tall, :]
            msg[r, tail : tail + half, :] = msg_rem[r].astype(msg.dtype)
            right = pltpu.roll(msg_far[r, half:LANES, :], half, 1)
            left = msg_far[r, :half, :]
            folded = jnp.where(lane_ids(left.shape) < half, left, right)
            msg[r, tail + half : msg_rows, :] = folded.astype(msg.dtype)

        def side_slots(r, axis):
            pair = (2 * axis, 2 * axis + 1)
            for d, total in [(d, side_sum(r, d)) for d in pair]:
                emit(r, 1 + d, total)
            if axis == 2:
                pack_row_tail(r)
            for d in pair:
                send_row(r, 1 + d)
            if axis == 2:
                send_row(r, sides)

        axis_faces = [list(range(4, nch)), [2, 3], [0, 1]]

        for step in range(size_z - 2):
            for way, ahead in enumerate((1, -1)):
                told = (me_z - ahead, me_z + ahead * (1 + step), me_z + ahead * (2 + step))
                inside = [(z >= 0) & (z < size_z) for z in told]

                @pl.when(inside[0] & inside[1])
                def _(way=way, step=step, ahead=ahead):
                    pl.semaphore_signal(
                        relay_sem.at[way, step],
                        inc=1,
                        device_id={"gz": me_z - ahead},
                        device_id_type=MESH,
                    )

                @pl.when(inside[2])
                def _(way=way, step=step):
                    pl.semaphore_wait(relay_sem.at[way, step], 1)

        @pl.loop(0, 2)
        def _(part):
            first, last = part * early, part * early + early

            @pl.when(part == 0)
            def _():
                pl.loop(0, 2)(lay_out)
                take_faces(axis_faces[0])

            pl.loop(first, last)(lambda r: side_slots(r, 0))

            @pl.when(part == 0)
            def _():
                pl.loop(2, sides)(lay_out)

            pl.loop(first, last)(own_slot)
            for axis in (1, 2):

                @pl.when(part == 0)
                def _(axis=axis):
                    take_faces(axis_faces[axis])

                pl.loop(first, last)(lambda r, axis=axis: side_slots(r, axis))

        owner = me_z % stride_z == 0

        def row_arrival(slot, piece):
            at = pl.ds(piece * LANES, LANES)
            return pltpu.make_async_remote_copy(
                src_ref=msg.at[0, at],
                dst_ref=rows_ref.at[slot, at],
                send_sem=r_send.at[0, piece],
                recv_sem=r_recv.at[slot, piece],
                device_id={"gz": me_z},
                device_id_type=MESH,
            )

        def arrive(piece):
            for slot in range(out_slots):
                sent = present(piece, slot // per_owner)
                if sent is False:
                    continue
                mine = slot // per_owner == me_z

                @pl.when(mine)
                def _(slot=slot):
                    self_copy(aggs_here - per_owner + slot % per_owner, piece).wait()

                @pl.when(jnp.logical_not(mine))
                def _(slot=slot):
                    row_arrival(slot, piece).wait_recv()

        def scatter(ref, slot, start, value):
            count = value.shape[0]
            ref[pl.ds(start * out_slots + slot, count, stride=out_slots), :] = value

        def gathered(ref, count):
            value = ref[: count * out_slots, :].astype(jnp.bfloat16)
            return value.reshape(count, out_slots, LANES)

        def unpack():
            for s in [1, 2, 0, *range(3, sides)]:
                arrive(s)
                for slot in range(out_slots):
                    block_of = rows_ref[slot, s * LANES : (s + 1) * LANES, :]
                    scatter(mixed, slot, 0, block_of.astype(jnp.float32))
                out_ref[s, :LANES, :, :LANES] = gathered(mixed, LANES)

            arrive(sides)
            for slot in range(out_slots):
                below = rows_ref[slot, tail : tail + half, :].astype(jnp.float32)
                folded = rows_ref[slot, tail + half : msg_rows, :].astype(jnp.float32)
                scatter(mixed, slot, 0, folded)
                scatter(mixed, slot, half, pltpu.roll(folded, half, 1))
                scatter(mixed, slot, LANES, below[sides * 8 :])
                for s in range(sides):
                    scatter(mixed_rem.at[s], slot, 0, below[s * 8 : (s + 1) * 8])
                mixed_rest[slot : slot + 1, :LANES] = below[rest : rest + 1]
                at = sides * 8 + rest
                mixed_rest[slot : slot + 1, LANES:] = below[at : at + 1, :rest]
            rest_ref[...] = mixed_rest[:out_slots].astype(rest_ref.dtype)
            for s in range(sides):
                low = gathered(mixed_rem.at[s], 8)
                out_ref[s, LANES:, :, :LANES] = low[:rest]
                right = mixed[...]
                if s > 0:
                    right = pltpu.roll(right, LANES - s * rest, 1)
                right = right.astype(jnp.bfloat16).reshape(tall, out_slots, LANES)
                out_ref[s, :, :, LANES:] = right[:width, :, :rest]

        if stride_z == 1:
            unpack()
        else:
            pl.when(owner)(unpack)

            @pl.when(jnp.logical_not(owner))
            def _():
                out_ref[...] = jnp.zeros_like(out_ref)
                rest_ref[...] = jnp.zeros_like(rest_ref)

        for c in range(nch):

            @when_sent(c)
            def _(c=c):
                for part in range(len(face_parts(c))):
                    face_copy(c, part).wait_send()

        @pl.loop(0, aggs_here)
        def _(r):
            @pl.when(target_of(r) != me_z)
            def _():
                for piece in range(pieces):

                    @pl.when(present(piece, me_z))
                    def _(piece=piece):
                        row_copy(r, piece).wait_send()

    bf16, f32 = jnp.bfloat16, jnp.float32
    spread_rows = (width + 1) * pitch
    faces = [pltpu.VMEM((face_rows(count, full), LANES), bf16) for _, _, count, _ in channels]
    parts = most // CHUNK + 1
    table_rows = pl.cdiv(nch + sides, 8) * 8
    scratch = [
        pltpu.VMEM((table_rows, LANES), jnp.int32),
        pltpu.SMEM((table_rows, LANES), jnp.int32),
        pltpu.VMEM((width, elems, width), bf16),
        pltpu.VMEM((AHEAD, width, elems, width), bf16),
        pltpu.VMEM((spread_rows, LANES), f32),
        pltpu.VMEM((spread_rows, LANES), f32),
        pltpu.VMEM((zero_block + 1, full, width), bf16),
        pltpu.VMEM((elems, tall, full), bf16),
        pltpu.VMEM((sides, elems, full, full), bf16),
        *faces,
        *faces,
        pltpu.VMEM((nch, most * 8, LANES), f32),
        pltpu.VMEM((nch, full, LANES), f32),
        pltpu.VMEM((aggs_here, msg_rows, LANES), bf16),
        pltpu.VMEM((aggs_here, (sides + 1) * 8, LANES), f32),
        pltpu.VMEM((aggs_here, tall, LANES), f32),
        pltpu.VMEM((8, width), f32),
        pltpu.VMEM((tall, width), f32),
        pltpu.VMEM((out_slots, msg_rows, LANES), bf16),
        pltpu.VMEM((tall * out_slots, LANES), f32),
        pltpu.VMEM((sides, 8 * out_slots, LANES), f32),
        pltpu.VMEM((pl.cdiv(out_slots, 8) * 8, width), f32),
        pltpu.SemaphoreType.DMA,
        pltpu.SemaphoreType.DMA,
        pltpu.SemaphoreType.DMA((AHEAD,)),
        pltpu.SemaphoreType.DMA((nch, parts)),
        pltpu.SemaphoreType.DMA((nch, parts)),
        pltpu.SemaphoreType.DMA((aggs_here, pieces)),
        pltpu.SemaphoreType.DMA((out_slots, pieces)),
        pltpu.SemaphoreType.DMA((per_owner, pieces)),
        pltpu.SemaphoreType.REGULAR((2, size_z - 2)),
    ]
    return pl.pallas_call(
        kernel,
        in_specs=[pl.BlockSpec(memory_space=pltpu.VMEM)] * 3
        + [pl.BlockSpec(memory_space=pl.ANY)] * 2
        + [pl.BlockSpec(memory_space=pltpu.VMEM)],
        out_specs=[pl.BlockSpec(memory_space=pltpu.VMEM)] * 2,
        out_shape=[
            pltpu.VMEM((sides, width, out_slots, width), bf16),
            pltpu.VMEM((out_slots, width), bf16),
        ],
        scratch_shapes=scratch,
        compiler_params=pltpu.CompilerParams(
            collective_id=0, has_side_effects=True, vmem_limit_bytes=54 << 20
        ),
    )(neighbours, agg_map, owners, prolong, jac, residual)


def stored(coarse, restricted):
    pieces = coarse.shape[0]

    def kernel(coarse_ref, small_ref, out_hbm, small_hbm, sems):
        copies = [
            pltpu.make_async_copy(coarse_ref.at[k], out_hbm.at[k], sems.at[k])
            for k in range(pieces)
        ]
        copies.append(pltpu.make_async_copy(small_ref, small_hbm, sems.at[pieces]))
        for copy in copies:
            copy.start()
        for copy in copies:
            copy.wait()

    return pl.pallas_call(
        kernel,
        in_specs=[pl.BlockSpec(memory_space=pltpu.VMEM)] * 2,
        out_specs=[pl.BlockSpec(memory_space=pl.ANY)] * 2,
        out_shape=[jax.ShapeDtypeStruct(a.shape, a.dtype) for a in (coarse, restricted)],
        scratch_shapes=[pltpu.SemaphoreType.DMA((pieces + 1,))],
        compiler_params=pltpu.CompilerParams(vmem_limit_bytes=1 << 20),
    )(coarse, restricted)


def write_table(tab, nbr, agg, owners, base, mine, x, sizes):
    size_x, _, size_z = sizes
    elems, aggs_here = nbr.shape[1], owners.shape[1]
    per_owner = aggs_here // GROUPS
    stride_z = size_z // GROUPS
    members = elems // aggs_here
    on_face = members // 2
    channels = channels_of(size_x)
    offsets, zero_block = channel_offsets(channels, elems)
    nch = len(channels)
    square = (elems, elems)
    down = lax.broadcasted_iota(jnp.int32, square, 0)
    along = lax.broadcasted_iota(jnp.int32, square, 1)
    ids = down[:, :1]

    def flag(mask):
        return jnp.where(mask, 1, 0)

    eye = flag(down == along)
    before = flag(along < down)

    def by_row(value):
        return jnp.sum(value, axis=1, keepdims=True)

    def by_column(value):
        return jnp.sum(value, axis=0, keepdims=True)

    def column(row):
        return by_row(eye * row)

    def row(col):
        return by_column(eye * col)

    def listed(place, value):
        return by_column(flag(place == along) * value)

    def put(at, value):
        tab[at : at + 1, :elems] = value

    a_down = lax.broadcasted_iota(jnp.int32, (aggs_here, aggs_here), 0)
    a_along = lax.broadcasted_iota(jnp.int32, (aggs_here, aggs_here), 1)
    to = owners // stride_z
    crosses = jnp.abs(to // 2 - mine // 2)
    flips = jnp.abs(to % 2 - mine % 2)
    turn = 2 * (1 - crosses) + (1 + flips + crosses * ((mine // 2 + mine % 2) % 2)) % 2
    turn = jnp.broadcast_to(turn, a_down.shape)
    turn = by_row(jnp.where(a_down == a_along, turn, 0))
    if per_owner > 1:
        turn_row = by_column(jnp.where(a_down == a_along, turn, 0))
        equal = flag(turn_row == turn) * flag(a_along < a_down)
        turn = turn * per_owner + by_row(equal)
    a_ids = lax.broadcasted_iota(jnp.int32, (aggs_here, elems), 0)
    order_row = by_column(flag(agg == a_ids) * turn)
    order = column(order_row)
    agg_col = column(agg)
    together = before * flag(order_row == order)
    m_place = order * members + by_row(together)

    if size_x == 2:
        listing = [(5, 0), (4, 1), (3, 2), (2, 3)]
        sources = [4, 4, 2, 3, 0, 1]
    else:
        listing = [(5, 0), (4, 1), (3, 2), (2, 3), (1, 4), (0, 5)]
        sources = [4, 5, 2, 3, 0, 1]
    sides_of, local_of, same_of = [], [], []
    for d in range(6):
        nbr_row = nbr[d : d + 1]
        nbr_col = column(nbr_row)
        local_row, local = nbr_row - base, nbr_col - base
        away_row = 1 - flag(local_row >= 0) * flag(local_row < elems)
        here = flag(local >= 0) * flag(local < elems)
        rank = by_row(before * away_row)
        place = jnp.where(here > 0, -1, rank)
        sides_of.append(listed(place, ids))
        crossing = away_row * flag(nbr_row >= 0)
        position = by_row(crossing * flag(nbr_row < nbr_col))
        index = jnp.where(here > 0, local, position + offsets[sources[d]])
        index = jnp.where(nbr_col >= 0, index, zero_block)
        near_agg = by_row(flag(local == along) * agg)
        same = here * flag(near_agg == agg_col)
        local_of.append(local)
        same_of.append(same)
        s_rank = by_row(together * (1 - row(same)))
        s_place = jnp.where(same > 0, -1, order * on_face + s_rank)
        put(nch + 1 + d, listed(s_place, ids + elems * index))
    for d, c in listing:
        put(c, sides_of[d])
    if size_x == 2:
        put(4, jnp.where(x == 0, sides_of[1], sides_of[0]))
    code = jnp.zeros_like(ids)
    for axis in (2, 1, 0):
        after = same_of[2 * axis + 1] > 0
        inner = jnp.where(after, local_of[2 * axis + 1] + elems, local_of[2 * axis])
        code = code * (2 * elems) + inner
    put(nch, listed(m_place, code * elems + ids))


def body(jacobian, prolong, residual, neighbours, agg_map, owners):
    sizes = tuple(lax.axis_size(a) for a in ("gx", "gy", "gz"))
    coarse, restricted = fused_kernel(
        neighbours.T,
        agg_map[None],
        owners[None],
        jnp.transpose(prolong, (1, 0, 2)),
        jnp.transpose(jacobian, (1, 2, 0, 3)),
        residual,
        sizes,
    )
    coarse, restricted = stored(coarse, restricted)
    return jnp.transpose(coarse, (2, 0, 1, 3)), restricted


def solution(mesh):
    spec = P(("gx", "gy", "gz"))
    return jax.shard_map(
        body,
        mesh=mesh,
        in_specs=(spec,) * 6,
        out_specs=(spec, spec),
        check_vma=False,
    )
```

```python
import jax
import jax.numpy as jnp
from jax import lax
from jax.experimental import pallas as pl
from jax.experimental.pallas import tpu as pltpu
from jax.sharding import PartitionSpec as P

LX = 4
LY = 4
LZ = 2
GROUPS = 4
LANES = 128
CHUNK = 4
AHEAD = 4
MESH = pl.DeviceIdType.MESH


def mul(a, b):
    return jnp.dot(a, b, preferred_element_type=jnp.float32)


def lane_ids(shape):
    return lax.broadcasted_iota(jnp.int32, shape, 1)


def channels_of(size_x):
    z = [("gz", 1, LX * LY, 5), ("gz", -1, LX * LY, 4)]
    y = [("gy", 1, LX * LZ, 3), ("gy", -1, LX * LZ, 2)]
    if size_x == 2:
        x = [("gx", 0, LY * LZ, None)]
    else:
        x = [("gx", 1, LY * LZ, 1), ("gx", -1, LY * LZ, 0)]
    return z + y + x


def channel_offsets(channels, elems):
    offsets, at = [], elems
    for _, _, count, _ in channels:
        offsets.append(at)
        at += count
    return offsets, at


def face_rows(count, tall):
    return count * LANES + count * 8 + tall


def partner_bits(me, r):
    high, low = me // 2, me % 2
    inner = (high + low) % 2
    cross = 1 - r // 2
    turn = (1 + r + inner * cross) % 2
    high = high + cross * (1 - 2 * high)
    low = low + turn * (1 - 2 * low)
    return high * 2 + low


def fused_kernel(neighbours, agg_map, owners, prolong, jac, residual, sizes):
    width, elems, _ = prolong.shape
    sides = jac.shape[0]
    aggs_here = owners.shape[1]
    size_x, size_y, size_z = sizes
    rest = width - LANES
    tall = pl.cdiv(width + 1, 8) * 8
    full = pl.cdiv(width + 1, 16) * 16
    pitch = elems + 1
    per_owner = aggs_here // GROUPS
    stride_z = size_z // GROUPS
    out_slots = size_z * per_owner
    members = elems // aggs_here
    on_face = members // 2
    channels = channels_of(size_x)
    offsets, zero_block = channel_offsets(channels, elems)
    nch = len(channels)
    tail = sides * LANES
    msg_rows = tail + LANES
    half = LANES // 2
    most = max(count for _, _, count, _ in channels)
    pieces = sides + 1
    early = aggs_here // 2
    step_rows = 5 if width % 5 == 0 else 1

    def kernel(nbr_ref, agg_ref, own_ref, p_hbm, j_hbm, res_ref, out_ref, rest_ref, *refs):
        tab, table_ref, praw, jraw, near, far, pool, pt, jm = refs[:9]
        sends, recvs = refs[9 : 9 + nch], refs[9 + nch : 9 + 2 * nch]
        refs = refs[9 + 2 * nch :]
        remf, farf, msg, msg_rem, msg_far, racc, acc = refs[:7]
        rows_ref, mixed, mixed_rem, mixed_rest = refs[7:11]
        t_sem, p_sem, j_sem, f_send, f_recv, r_send, r_recv, self_sem, relay_sem = refs[11:]
        me = {"gx": lax.axis_index("gx"), "gy": lax.axis_index("gy"), "gz": lax.axis_index("gz")}
        size = {"gx": size_x, "gy": size_y, "gz": size_z}
        me_z = me["gz"]

        p_copy = pltpu.make_async_copy(p_hbm, praw, p_sem)
        p_copy.start()

        def block_at(i):
            return (i + 1) * (i < 2) + i * (i > 2)

        def j_copy(i):
            slot = i % AHEAD
            return pltpu.make_async_copy(
                j_hbm.at[block_at(i)], jraw.at[slot], j_sem.at[slot]
            )

        barrier = pltpu.get_barrier_semaphore()
        expected = 0
        if size_x == 2:
            pl.semaphore_signal(
                barrier, inc=1, device_id={"gx": 1 - me["gx"]}, device_id_type=MESH
            )
            expected = expected + 1
        for axis in ["gz", "gy"] + (["gx"] if size_x > 2 else []):
            for step in (1, -1):
                there = me[axis] + step
                exists = (there >= 0) & (there < size[axis])

                @pl.when(exists)
                def _(axis=axis, there=there):
                    pl.semaphore_signal(
                        barrier, inc=1, device_id={axis: there}, device_id_type=MESH
                    )

                expected = expected + exists.astype(jnp.int32)

        msg_far[...] = jnp.zeros_like(msg_far)
        for sub in range(per_owner):
            for piece, slot in ((5, sub), (6, out_slots - per_owner + sub)):
                rows_ref[slot, piece * LANES : (piece + 1) * LANES, :] = jnp.zeros(
                    (LANES, LANES), rows_ref.dtype
                )
        pool[zero_block] = jnp.zeros(pool.shape[1:], pool.dtype)

        def spread(load, last):
            @pl.loop(0, width // step_rows)
            def _(c):
                part = load(c).astype(jnp.float32)
                for i in range(step_rows):
                    rows = pl.ds((c * step_rows + i) * pitch, elems)
                    near[rows, :] = part[i, :, :LANES]
                    far[rows, :rest] = part[i, :, LANES:]

            near[pl.ds(width * pitch, elems), :] = last[:, :LANES]
            far[pl.ds(width * pitch, elems), :rest] = last[:, LANES:]

        def block(e):
            rows = pl.ds(e, width + 1, stride=pitch)
            right = far[rows, :]
            right = jnp.where(lane_ids(right.shape) < rest, right, 0.0)
            both = jnp.concatenate([near[rows, :], right], axis=1)[:, :full]
            below = jnp.zeros((full - width - 1, full), jnp.float32)
            return jnp.concatenate([both, below], axis=0)

        device = (me["gx"] * size_y + me["gy"]) * size_z + me_z
        write_table(
            tab,
            nbr_ref[...],
            agg_ref[...] - device * aggs_here,
            own_ref[...],
            device * elems,
            me_z // stride_z,
            me["gx"],
            sizes,
        )
        t_copy = pltpu.make_async_copy(tab, table_ref, t_sem)
        t_copy.start()
        p_copy.wait()
        for k in range(AHEAD):
            j_copy(k).start()
        spread(
            lambda c: praw[pl.ds(c * step_rows, step_rows)],
            jnp.zeros((elems, width), jnp.float32),
        )

        @pl.loop(0, elems // 4)
        def _(group):
            for u in range(4):
                e = group * 4 + u
                pool[e] = block(e)[:, :width].astype(pool.dtype)

        t_copy.wait()

        def face_target(c):
            axis, step, _, _ = channels[c]
            return {axis: 1 - me[axis] if step == 0 else me[axis] + step}

        def when_sent(c):
            axis, step, _, _ = channels[c]
            if step == 0:
                return lambda f: f()
            there = me[axis] + step
            return pl.when((there >= 0) & (there < size[axis]))

        def when_received(c):
            axis, step, _, _ = channels[c]
            if step == 0:
                return lambda f: f()
            there = me[axis] - step
            return pl.when((there >= 0) & (there < size[axis]))

        def face_parts(c):
            count = channels[c][2]
            parts = [(n * LANES, CHUNK * LANES) for n in range(0, count, CHUNK)]
            return parts + [(count * LANES, count * 8 + full)]

        def face_copy(c, part):
            start, rows = face_parts(c)[part]
            return pltpu.make_async_remote_copy(
                src_ref=sends[c].at[pl.ds(start, rows)],
                dst_ref=recvs[c].at[pl.ds(start, rows)],
                send_sem=f_send.at[c, part],
                recv_sem=f_recv.at[c, part],
                device_id=face_target(c),
                device_id_type=MESH,
            )

        def pack(c, n):
            whole = pool[table_ref[c, n] % elems]
            sends[c][n * LANES : (n + 1) * LANES, :] = whole[:LANES, :LANES]
            remf[c, n * 8 : (n + 1) * 8, :] = whole[LANES:tall, :LANES].astype(jnp.float32)
            farf[c, :, n * rest : (n + 1) * rest] = whole[:, LANES:width].astype(jnp.float32)

        def pack_tail(c):
            count = channels[c][2]
            at = count * LANES
            sends[c][at : at + count * 8, :] = remf[c, : count * 8, :].astype(jnp.bfloat16)
            sends[c][at + count * 8 : at + count * 8 + full, :] = farf[c].astype(jnp.bfloat16)

        def send_faces(group):
            for part in range(max(len(face_parts(c)) for c in group)):
                for c in group:
                    if part < len(face_parts(c)) - 1:
                        for n in range(part * CHUNK, (part + 1) * CHUNK):
                            pack(c, n)
                    elif part < len(face_parts(c)):
                        pack_tail(c)
                    if part < len(face_parts(c)):

                        @when_sent(c)
                        def _(c=c, part=part):
                            face_copy(c, part).start()

        def take_faces(group):
            for c in group:

                @when_received(c)
                def _(c=c):
                    for part in range(len(face_parts(c))):
                        face_copy(c, part).wait_recv()
                    count = channels[c][2]
                    at = count * LANES
                    remf[c, : count * 8, :] = recvs[c][at : at + count * 8, :].astype(jnp.float32)
                    farf[c] = recvs[c][at + count * 8 : at + count * 8 + full, :].astype(
                        jnp.float32
                    )
                    for n in range(count):
                        to = offsets[c] + n
                        pool[to, :LANES, :LANES] = recvs[c][n * LANES : (n + 1) * LANES, :]
                        below = remf[c, n * 8 : (n + 1) * 8, :]
                        below = jnp.concatenate([below, jnp.zeros_like(below)], axis=0)
                        pool[to, LANES:full, :LANES] = below.astype(pool.dtype)
                        pool[to, :, LANES:width] = farf[
                            c, :, n * rest : (n + 1) * rest
                        ].astype(pool.dtype)

        pl.semaphore_wait(barrier, expected)
        send_faces([0, 1])
        send_faces(list(range(2, nch)))

        @pl.loop(0, elems // 4)
        def _(group):
            for u in range(4):
                e = group * 4 + u
                pt[e] = block(e).T[:tall].astype(pt.dtype)

        def lay_out(i):
            k = block_at(i)
            j_copy(i).wait()
            own = (k == 0).astype(jnp.float32)
            spread(
                lambda c: jraw[i % AHEAD, pl.ds(c * step_rows, step_rows)],
                res_ref[...].astype(jnp.float32) * own,
            )

            @pl.when(i + AHEAD < sides)
            def _():
                j_copy(i + AHEAD).start()

            @pl.loop(0, elems // 4)
            def _(group):
                for u in range(4):
                    e = group * 4 + u
                    jm[k, e] = block(e).astype(jm.dtype)

        my_group = me_z // stride_z

        def target_of(r):
            return partner_bits(my_group, r // per_owner) * stride_z

        def slot_of(z, r):
            return z * per_owner + r % per_owner

        def row_copy(r, piece):
            at = pl.ds(pl.multiple_of(piece * LANES, LANES), LANES)
            slot = slot_of(me_z, r)
            return pltpu.make_async_remote_copy(
                src_ref=msg.at[r, at],
                dst_ref=rows_ref.at[slot, at],
                send_sem=r_send.at[r, piece],
                recv_sem=r_recv.at[slot, piece],
                device_id={"gz": target_of(r)},
                device_id_type=MESH,
            )

        def self_copy(r, piece):
            at = pl.ds(pl.multiple_of(piece * LANES, LANES), LANES)
            return pltpu.make_async_copy(
                msg.at[r, at],
                rows_ref.at[slot_of(me_z, r), at],
                self_sem.at[r % per_owner, piece],
            )

        def send_row(r, piece):
            sent = present(piece, me_z)

            @pl.when((target_of(r) != me_z) & sent)
            def _():
                row_copy(r, piece).start()

            @pl.when((target_of(r) == me_z) & sent)
            def _():
                self_copy(r, piece).start()

        def emit(r, s, value):
            msg[r, s * LANES : (s + 1) * LANES, :] = value[:LANES, :LANES].astype(msg.dtype)
            msg_rem[r, s * 8 : (s + 1) * 8, :] = value[LANES:tall, :LANES]
            msg_far[r, :, s * rest : (s + 1) * rest] = value[:, LANES:width]

        def present(piece, z):
            if piece == 5:
                return z > 0
            if piece == 6:
                return z < size_z - 1
            return True

        def side_sum(r, d):
            total = None
            for m in range(on_face):
                code = table_ref[nch + 1 + d, r * on_face + m]
                e, n = code % elems, jnp.clip(code // elems, 0, zero_block)
                product = mul(jm[1 + d, e], pool[n]).astype(jnp.bfloat16)
                triple = mul(pt[e], product)
                total = triple if total is None else total + triple
            return total

        def own_slot(r):
            acc[...] = jnp.zeros_like(acc)
            racc[...] = jnp.zeros_like(racc)

            @pl.loop(0, members // 4)
            def _(pair):
                total = None
                for u in range(4):
                    code = table_ref[nch, r * members + pair * 4 + u]
                    e, code = code % elems, code // elems
                    product = mul(jm[0, e], pool[e])
                    for axis in range(3):
                        x, code = code % (2 * elems), code // (2 * elems)
                        k = 1 + 2 * axis + x // elems
                        product = product + mul(jm[k, e], pool[x % elems])
                    racc[...] += product[LANES:tall]
                    triple = mul(pt[e], product.astype(jnp.bfloat16))
                    total = triple if total is None else total + triple
                acc[...] += total

            below = racc[...]
            spare = lax.broadcasted_iota(jnp.int32, below.shape, 0) == width - LANES
            acc[LANES:tall, :] += jnp.where(spare, below, 0.0)
            emit(r, 0, acc[...])
            send_row(r, 0)

        def pack_row_tail(r):
            msg_rem[r, sides * 8 : (sides + 1) * 8, :] = msg_far[r, LANES:tall, :]
            msg[r, tail : tail + half, :] = msg_rem[r].astype(msg.dtype)
            right = pltpu.roll(msg_far[r, half:LANES, :], half, 1)
            left = msg_far[r, :half, :]
            folded = jnp.where(lane_ids(left.shape) < half, left, right)
            msg[r, tail + half : msg_rows, :] = folded.astype(msg.dtype)

        def side_slots(r, axis):
            pair = (2 * axis, 2 * axis + 1)
            for d, total in [(d, side_sum(r, d)) for d in pair]:
                emit(r, 1 + d, total)
            if axis == 2:
                pack_row_tail(r)
            for d in pair:
                send_row(r, 1 + d)
            if axis == 2:
                send_row(r, sides)

        axis_faces = [list(range(4, nch)), [2, 3], [0, 1]]

        for step in range(size_z - 2):
            for way, ahead in enumerate((1, -1)):
                told = (me_z - ahead, me_z + ahead * (1 + step), me_z + ahead * (2 + step))
                inside = [(z >= 0) & (z < size_z) for z in told]

                @pl.when(inside[0] & inside[1])
                def _(way=way, step=step, ahead=ahead):
                    pl.semaphore_signal(
                        relay_sem.at[way, step],
                        inc=1,
                        device_id={"gz": me_z - ahead},
                        device_id_type=MESH,
                    )

                @pl.when(inside[2])
                def _(way=way, step=step):
                    pl.semaphore_wait(relay_sem.at[way, step], 1)

        @pl.loop(0, 2)
        def _(part):
            first, last = part * early, part * early + early

            @pl.when(part == 0)
            def _():
                pl.loop(0, 2)(lay_out)
                take_faces(axis_faces[0])

            pl.loop(first, last)(lambda r: side_slots(r, 0))

            @pl.when(part == 0)
            def _():
                pl.loop(2, sides)(lay_out)

            pl.loop(first, last)(own_slot)
            for axis in (1, 2):

                @pl.when(part == 0)
                def _(axis=axis):
                    take_faces(axis_faces[axis])

                pl.loop(first, last)(lambda r, axis=axis: side_slots(r, axis))

        owner = me_z % stride_z == 0

        def row_arrival(slot, piece):
            at = pl.ds(piece * LANES, LANES)
            return pltpu.make_async_remote_copy(
                src_ref=msg.at[0, at],
                dst_ref=rows_ref.at[slot, at],
                send_sem=r_send.at[0, piece],
                recv_sem=r_recv.at[slot, piece],
                device_id={"gz": me_z},
                device_id_type=MESH,
            )

        def arrive(piece):
            for slot in range(out_slots):
                sent = present(piece, slot // per_owner)
                if sent is False:
                    continue
                mine = slot // per_owner == me_z

                @pl.when(mine)
                def _(slot=slot):
                    self_copy(aggs_here - per_owner + slot % per_owner, piece).wait()

                @pl.when(jnp.logical_not(mine))
                def _(slot=slot):
                    row_arrival(slot, piece).wait_recv()

        def scatter(ref, slot, start, value):
            count = value.shape[0]
            ref[pl.ds(start * out_slots + slot, count, stride=out_slots), :] = value

        def gathered(ref, count):
            value = ref[: count * out_slots, :].astype(jnp.bfloat16)
            return value.reshape(count, out_slots, LANES)

        def unpack():
            for s in [1, 2, 0, *range(3, sides)]:
                arrive(s)
                for slot in range(out_slots):
                    block_of = rows_ref[slot, s * LANES : (s + 1) * LANES, :]
                    scatter(mixed, slot, 0, block_of.astype(jnp.float32))
                out_ref[s, :LANES, :, :LANES] = gathered(mixed, LANES)

            arrive(sides)
            for slot in range(out_slots):
                below = rows_ref[slot, tail : tail + half, :].astype(jnp.float32)
                folded = rows_ref[slot, tail + half : msg_rows, :].astype(jnp.float32)
                scatter(mixed, slot, 0, folded)
                scatter(mixed, slot, half, pltpu.roll(folded, half, 1))
                scatter(mixed, slot, LANES, below[sides * 8 :])
                for s in range(sides):
                    scatter(mixed_rem.at[s], slot, 0, below[s * 8 : (s + 1) * 8])
                mixed_rest[slot : slot + 1, :LANES] = below[rest : rest + 1]
                at = sides * 8 + rest
                mixed_rest[slot : slot + 1, LANES:] = below[at : at + 1, :rest]
            rest_ref[...] = mixed_rest[:out_slots].astype(rest_ref.dtype)
            for s in range(sides):
                low = gathered(mixed_rem.at[s], 8)
                out_ref[s, LANES:, :, :LANES] = low[:rest]
                right = mixed[...]
                if s > 0:
                    right = pltpu.roll(right, LANES - s * rest, 1)
                right = right.astype(jnp.bfloat16).reshape(tall, out_slots, LANES)
                out_ref[s, :, :, LANES:] = right[:width, :, :rest]

        if stride_z == 1:
            unpack()
        else:
            pl.when(owner)(unpack)

            @pl.when(jnp.logical_not(owner))
            def _():
                out_ref[...] = jnp.zeros_like(out_ref)
                rest_ref[...] = jnp.zeros_like(rest_ref)

        for c in range(nch):

            @when_sent(c)
            def _(c=c):
                for part in range(len(face_parts(c))):
                    face_copy(c, part).wait_send()

        @pl.loop(0, aggs_here)
        def _(r):
            @pl.when(target_of(r) != me_z)
            def _():
                for piece in range(pieces):

                    @pl.when(present(piece, me_z))
                    def _(piece=piece):
                        row_copy(r, piece).wait_send()

    bf16, f32 = jnp.bfloat16, jnp.float32
    spread_rows = (width + 1) * pitch
    faces = [pltpu.VMEM((face_rows(count, full), LANES), bf16) for _, _, count, _ in channels]
    parts = most // CHUNK + 1
    table_rows = pl.cdiv(nch + sides, 8) * 8
    scratch = [
        pltpu.VMEM((table_rows, LANES), jnp.int32),
        pltpu.SMEM((table_rows, LANES), jnp.int32),
        pltpu.VMEM((width, elems, width), bf16),
        pltpu.VMEM((AHEAD, width, elems, width), bf16),
        pltpu.VMEM((spread_rows, LANES), f32),
        pltpu.VMEM((spread_rows, LANES), f32),
        pltpu.VMEM((zero_block + 1, full, width), bf16),
        pltpu.VMEM((elems, tall, full), bf16),
        pltpu.VMEM((sides, elems, full, full), bf16),
        *faces,
        *faces,
        pltpu.VMEM((nch, most * 8, LANES), f32),
        pltpu.VMEM((nch, full, LANES), f32),
        pltpu.VMEM((aggs_here, msg_rows, LANES), bf16),
        pltpu.VMEM((aggs_here, (sides + 1) * 8, LANES), f32),
        pltpu.VMEM((aggs_here, tall, LANES), f32),
        pltpu.VMEM((8, width), f32),
        pltpu.VMEM((tall, width), f32),
        pltpu.VMEM((out_slots, msg_rows, LANES), bf16),
        pltpu.VMEM((tall * out_slots, LANES), f32),
        pltpu.VMEM((sides, 8 * out_slots, LANES), f32),
        pltpu.VMEM((pl.cdiv(out_slots, 8) * 8, width), f32),
        pltpu.SemaphoreType.DMA,
        pltpu.SemaphoreType.DMA,
        pltpu.SemaphoreType.DMA((AHEAD,)),
        pltpu.SemaphoreType.DMA((nch, parts)),
        pltpu.SemaphoreType.DMA((nch, parts)),
        pltpu.SemaphoreType.DMA((aggs_here, pieces)),
        pltpu.SemaphoreType.DMA((out_slots, pieces)),
        pltpu.SemaphoreType.DMA((per_owner, pieces)),
        pltpu.SemaphoreType.REGULAR((2, size_z - 2)),
    ]
    return pl.pallas_call(
        kernel,
        in_specs=[pl.BlockSpec(memory_space=pltpu.VMEM)] * 3
        + [pl.BlockSpec(memory_space=pl.ANY)] * 2
        + [pl.BlockSpec(memory_space=pltpu.VMEM)],
        out_specs=[pl.BlockSpec(memory_space=pltpu.VMEM)] * 2,
        out_shape=[
            pltpu.VMEM((sides, width, out_slots, width), bf16),
            pltpu.VMEM((out_slots, width), bf16),
        ],
        scratch_shapes=scratch,
        compiler_params=pltpu.CompilerParams(
            collective_id=0, has_side_effects=True, vmem_limit_bytes=54 << 20
        ),
    )(neighbours, agg_map, owners, prolong, jac, residual)


def stored(coarse, restricted):
    pieces = coarse.shape[0]

    def kernel(coarse_ref, small_ref, out_hbm, small_hbm, sems):
        copies = [
            pltpu.make_async_copy(coarse_ref.at[k], out_hbm.at[k], sems.at[k])
            for k in range(pieces)
        ]
        copies.append(pltpu.make_async_copy(small_ref, small_hbm, sems.at[pieces]))
        for copy in copies:
            copy.start()
        for copy in copies:
            copy.wait()

    return pl.pallas_call(
        kernel,
        in_specs=[pl.BlockSpec(memory_space=pltpu.VMEM)] * 2,
        out_specs=[pl.BlockSpec(memory_space=pl.ANY)] * 2,
        out_shape=[jax.ShapeDtypeStruct(a.shape, a.dtype) for a in (coarse, restricted)],
        scratch_shapes=[pltpu.SemaphoreType.DMA((pieces + 1,))],
        compiler_params=pltpu.CompilerParams(vmem_limit_bytes=1 << 20),
    )(coarse, restricted)


def write_table(tab, nbr, agg, owners, base, mine, x, sizes):
    size_x, _, size_z = sizes
    elems, aggs_here = nbr.shape[1], owners.shape[1]
    per_owner = aggs_here // GROUPS
    stride_z = size_z // GROUPS
    members = elems // aggs_here
    on_face = members // 2
    channels = channels_of(size_x)
    offsets, zero_block = channel_offsets(channels, elems)
    nch = len(channels)
    square = (elems, elems)
    down = lax.broadcasted_iota(jnp.int32, square, 0)
    along = lax.broadcasted_iota(jnp.int32, square, 1)
    ids = down[:, :1]

    def flag(mask):
        return jnp.where(mask, 1, 0)

    eye = flag(down == along)
    before = flag(along < down)

    def by_row(value):
        return jnp.sum(value, axis=1, keepdims=True)

    def by_column(value):
        return jnp.sum(value, axis=0, keepdims=True)

    def column(row):
        return by_row(eye * row)

    def row(col):
        return by_column(eye * col)

    def listed(place, value):
        return by_column(flag(place == along) * value)

    def put(at, value):
        tab[at : at + 1, :elems] = value

    a_down = lax.broadcasted_iota(jnp.int32, (aggs_here, aggs_here), 0)
    a_along = lax.broadcasted_iota(jnp.int32, (aggs_here, aggs_here), 1)
    to = owners // stride_z
    crosses = jnp.abs(to // 2 - mine // 2)
    flips = jnp.abs(to % 2 - mine % 2)
    turn = 2 * (1 - crosses) + (1 + flips + crosses * ((mine // 2 + mine % 2) % 2)) % 2
    turn = jnp.broadcast_to(turn, a_down.shape)
    turn = by_row(jnp.where(a_down == a_along, turn, 0))
    if per_owner > 1:
        turn_row = by_column(jnp.where(a_down == a_along, turn, 0))
        equal = flag(turn_row == turn) * flag(a_along < a_down)
        turn = turn * per_owner + by_row(equal)
    a_ids = lax.broadcasted_iota(jnp.int32, (aggs_here, elems), 0)
    order_row = by_column(flag(agg == a_ids) * turn)
    order = column(order_row)
    agg_col = column(agg)
    together = before * flag(order_row == order)
    m_place = order * members + by_row(together)

    if size_x == 2:
        listing = [(5, 0), (4, 1), (3, 2), (2, 3)]
        sources = [4, 4, 2, 3, 0, 1]
    else:
        listing = [(5, 0), (4, 1), (3, 2), (2, 3), (1, 4), (0, 5)]
        sources = [4, 5, 2, 3, 0, 1]
    sides_of, local_of, same_of = [], [], []
    for d in range(6):
        nbr_row = nbr[d : d + 1]
        nbr_col = column(nbr_row)
        local_row, local = nbr_row - base, nbr_col - base
        away_row = 1 - flag(local_row >= 0) * flag(local_row < elems)
        here = flag(local >= 0) * flag(local < elems)
        rank = by_row(before * away_row)
        place = jnp.where(here > 0, -1, rank)
        sides_of.append(listed(place, ids))
        crossing = away_row * flag(nbr_row >= 0)
        position = by_row(crossing * flag(nbr_row < nbr_col))
        index = jnp.where(here > 0, local, position + offsets[sources[d]])
        index = jnp.where(nbr_col >= 0, index, zero_block)
        near_agg = by_row(flag(local == along) * agg)
        same = here * flag(near_agg == agg_col)
        local_of.append(local)
        same_of.append(same)
        s_rank = by_row(together * (1 - row(same)))
        s_place = jnp.where(same > 0, -1, order * on_face + s_rank)
        put(nch + 1 + d, listed(s_place, ids + elems * index))
    for d, c in listing:
        put(c, sides_of[d])
    if size_x == 2:
        put(4, jnp.where(x == 0, sides_of[1], sides_of[0]))
    code = jnp.zeros_like(ids)
    for axis in (2, 1, 0):
        after = same_of[2 * axis + 1] > 0
        inner = jnp.where(after, local_of[2 * axis + 1] + elems, local_of[2 * axis])
        code = code * (2 * elems) + inner
    put(nch, listed(m_place, code * elems + ids))


def body(jacobian, prolong, residual, neighbours, agg_map, owners):
    sizes = tuple(lax.axis_size(a) for a in ("gx", "gy", "gz"))
    coarse, restricted = fused_kernel(
        neighbours.T,
        agg_map[None],
        owners[None],
        jnp.transpose(prolong, (1, 0, 2)),
        jnp.transpose(jacobian, (1, 2, 0, 3)),
        residual,
        sizes,
    )
    coarse, restricted = stored(coarse, restricted)
    return jnp.transpose(coarse, (2, 0, 1, 3)), restricted


def solution(mesh):
    spec = P(("gx", "gy", "gz"))
    return jax.shard_map(
        body,
        mesh=mesh,
        in_specs=(spec,) * 6,
        out_specs=(spec, spec),
        check_vma=False,
    )
```

```python
import jax
import jax.numpy as jnp
from jax import lax
from jax.experimental import pallas as pl
from jax.experimental.pallas import tpu as pltpu
from jax.sharding import PartitionSpec as P

LX = 4
LY = 4
LZ = 2
GROUPS = 4
LANES = 128
CHUNK = 4
AHEAD = 4
MESH = pl.DeviceIdType.MESH


def mul(a, b):
    return jnp.dot(a, b, preferred_element_type=jnp.float32)


def lane_ids(shape):
    return lax.broadcasted_iota(jnp.int32, shape, 1)


def channels_of(size_x):
    z = [("gz", 1, LX * LY, 5), ("gz", -1, LX * LY, 4)]
    y = [("gy", 1, LX * LZ, 3), ("gy", -1, LX * LZ, 2)]
    if size_x == 2:
        x = [("gx", 0, LY * LZ, None)]
    else:
        x = [("gx", 1, LY * LZ, 1), ("gx", -1, LY * LZ, 0)]
    return z + y + x


def channel_offsets(channels, elems):
    offsets, at = [], elems
    for _, _, count, _ in channels:
        offsets.append(at)
        at += count
    return offsets, at


def face_rows(count, tall):
    return count * LANES + count * 8 + tall


def partner_bits(me, r):
    high, low = me // 2, me % 2
    inner = (high + low) % 2
    cross = 1 - r // 2
    turn = (1 + r + inner * cross) % 2
    high = high + cross * (1 - 2 * high)
    low = low + turn * (1 - 2 * low)
    return high * 2 + low


def fused_kernel(neighbours, agg_map, owners, prolong, jac, residual, sizes):
    width, elems, _ = prolong.shape
    sides = jac.shape[0]
    aggs_here = owners.shape[1]
    size_x, size_y, size_z = sizes
    rest = width - LANES
    tall = pl.cdiv(width + 1, 8) * 8
    full = pl.cdiv(width + 1, 16) * 16
    pitch = elems + 1
    per_owner = aggs_here // GROUPS
    stride_z = size_z // GROUPS
    out_slots = size_z * per_owner
    members = elems // aggs_here
    on_face = members // 2
    channels = channels_of(size_x)
    offsets, zero_block = channel_offsets(channels, elems)
    nch = len(channels)
    tail = sides * LANES
    msg_rows = tail + LANES
    half = LANES // 2
    most = max(count for _, _, count, _ in channels)
    pieces = sides + 1
    early = aggs_here // 2
    step_rows = 5 if width % 5 == 0 else 1

    def kernel(nbr_in, agg_in, own_in, p_hbm, j_hbm, res_in, out_ref, tail_ref, *refs):
        nbr_ref, agg_ref, own_ref, res_ref, picks, picks_ref = refs[:6]
        refs = refs[6:]
        tab, table_ref, praw, jraw, near, far, pool, pt, jm = refs[:9]
        sends, recvs = refs[9 : 9 + nch], refs[9 + nch : 9 + 2 * nch]
        refs = refs[9 + 2 * nch :]
        remf, farf, msg, msg_rem, msg_far, racc, acc = refs[:7]
        rows_ref, mixed = refs[7:9]
        in_sem, k_sem, t_sem, p_sem, j_sem, f_send, f_recv, r_send, r_recv, self_sem, relay_sem = refs[9:]
        me = {"gx": lax.axis_index("gx"), "gy": lax.axis_index("gy"), "gz": lax.axis_index("gz")}
        size = {"gx": size_x, "gy": size_y, "gz": size_z}
        me_z = me["gz"]

        p_copy = pltpu.make_async_copy(p_hbm, praw, p_sem)
        p_copy.start()
        small = [
            pltpu.make_async_copy(source, ref, in_sem.at[i])
            for i, (source, ref) in enumerate(
                zip((nbr_in, agg_in, own_in, res_in), (nbr_ref, agg_ref, own_ref, res_ref))
            )
        ]
        for copy in small:
            copy.start()

        def block_at(i):
            return (i + 1) * (i < 2) + i * (i > 2)

        def j_copy(i):
            slot = i % AHEAD
            return pltpu.make_async_copy(
                j_hbm.at[block_at(i)], jraw.at[slot], j_sem.at[slot]
            )

        barrier = pltpu.get_barrier_semaphore()
        expected = 0
        if size_x == 2:
            pl.semaphore_signal(
                barrier, inc=1, device_id={"gx": 1 - me["gx"]}, device_id_type=MESH
            )
            expected = expected + 1
        for axis in ["gz", "gy"] + (["gx"] if size_x > 2 else []):
            for step in (1, -1):
                there = me[axis] + step
                exists = (there >= 0) & (there < size[axis])

                @pl.when(exists)
                def _(axis=axis, there=there):
                    pl.semaphore_signal(
                        barrier, inc=1, device_id={axis: there}, device_id_type=MESH
                    )

                expected = expected + exists.astype(jnp.int32)

        def spread(load, last):
            @pl.loop(0, width // step_rows)
            def _(c):
                part = load(c).astype(jnp.float32)
                for i in range(step_rows):
                    rows = pl.ds((c * step_rows + i) * pitch, elems)
                    near[rows, :] = part[i, :, :LANES]
                    far[rows, :rest] = part[i, :, LANES:]

            near[pl.ds(width * pitch, elems), :] = last[:, :LANES]
            far[pl.ds(width * pitch, elems), :rest] = last[:, LANES:]

        def block(e):
            rows = pl.ds(e, width + 1, stride=pitch)
            right = far[rows, :]
            right = jnp.where(lane_ids(right.shape) < rest, right, 0.0)
            both = jnp.concatenate([near[rows, :], right], axis=1)[:, :full]
            below = jnp.zeros((full - width - 1, full), jnp.float32)
            return jnp.concatenate([both, below], axis=0)

        device = (me["gx"] * size_y + me["gy"]) * size_z + me_z
        for copy in small:
            copy.wait()
        lists = Lists(nbr_ref[...], device * elems)
        for c in range(2):
            picks[c : c + 1, :elems] = lists.side(channels[c][3])
        k_copy = pltpu.make_async_copy(picks, picks_ref, k_sem)
        k_copy.start()
        for c in range(2):
            farf[c, tall:, :] = jnp.zeros((full - tall, LANES), jnp.float32)
        p_copy.wait()
        for k in range(AHEAD):
            j_copy(k).start()
        spread(
            lambda c: praw[pl.ds(c * step_rows, step_rows)],
            jnp.zeros((elems, width), jnp.float32),
        )

        def face_target(c):
            axis, step, _, _ = channels[c]
            return {axis: 1 - me[axis] if step == 0 else me[axis] + step}

        def when_sent(c):
            axis, step, _, _ = channels[c]
            if step == 0:
                return lambda f: f()
            there = me[axis] + step
            return pl.when((there >= 0) & (there < size[axis]))

        def when_received(c):
            axis, step, _, _ = channels[c]
            if step == 0:
                return lambda f: f()
            there = me[axis] - step
            return pl.when((there >= 0) & (there < size[axis]))

        def face_parts(c):
            count = channels[c][2]
            parts = [(n * LANES, CHUNK * LANES) for n in range(0, count, CHUNK)]
            return parts + [(count * LANES, count * 8 + full)]

        def face_copy(c, part):
            start, rows = face_parts(c)[part]
            return pltpu.make_async_remote_copy(
                src_ref=sends[c].at[pl.ds(start, rows)],
                dst_ref=recvs[c].at[pl.ds(start, rows)],
                send_sem=f_send.at[c],
                recv_sem=f_recv.at[c],
                device_id=face_target(c),
                device_id_type=MESH,
            )

        def whole_face(c):
            return pltpu.make_async_remote_copy(
                src_ref=sends[c],
                dst_ref=recvs[c],
                send_sem=f_send.at[c],
                recv_sem=f_recv.at[c],
                device_id=face_target(c),
                device_id_type=MESH,
            )

        def pack(c, n):
            if c < 2:
                rows = pl.ds(picks_ref[c, n] % elems, width + 1, stride=pitch)
                left, right = near[rows, :], far[rows, :]
                sends[c][n * LANES : (n + 1) * LANES, :] = left[:LANES].astype(jnp.bfloat16)
                remf[c, n * 8 : (n + 1) * 8, :] = left[LANES:tall]
                farf[c, :tall, n * rest : (n + 1) * rest] = right[:, :rest]
                return
            whole = pool[table_ref[c, n] % elems]
            sends[c][n * LANES : (n + 1) * LANES, :] = whole[:LANES, :LANES]
            remf[c, n * 8 : (n + 1) * 8, :] = whole[LANES:tall, :LANES].astype(jnp.float32)
            farf[c, :, n * rest : (n + 1) * rest] = whole[:, LANES:width].astype(jnp.float32)

        def pack_tail(c):
            count = channels[c][2]
            at = count * LANES
            sends[c][at : at + count * 8, :] = remf[c, : count * 8, :].astype(jnp.bfloat16)
            sends[c][at + count * 8 : at + count * 8 + full, :] = farf[c].astype(jnp.bfloat16)

        def send_faces(group):
            for part in range(max(len(face_parts(c)) for c in group)):
                for c in group:
                    if part < len(face_parts(c)) - 1:
                        for n in range(part * CHUNK, (part + 1) * CHUNK):
                            pack(c, n)
                    elif part < len(face_parts(c)):
                        pack_tail(c)
                    if part < len(face_parts(c)):

                        @when_sent(c)
                        def _(c=c, part=part):
                            face_copy(c, part).start()

        def take_faces(group):
            for c in group:

                @when_received(c)
                def _(c=c):
                    whole_face(c).wait_recv()
                    count = channels[c][2]
                    at = count * LANES
                    remf[c, : count * 8, :] = recvs[c][at : at + count * 8, :].astype(jnp.float32)
                    farf[c] = recvs[c][at + count * 8 : at + count * 8 + full, :].astype(
                        jnp.float32
                    )
                    for n in range(count):
                        to = offsets[c] + n
                        pool[to, :LANES, :LANES] = recvs[c][n * LANES : (n + 1) * LANES, :]
                        below = remf[c, n * 8 : (n + 1) * 8, :]
                        below = jnp.concatenate([below, jnp.zeros_like(below)], axis=0)
                        pool[to, LANES:full, :LANES] = below.astype(pool.dtype)
                        pool[to, :, LANES:width] = farf[
                            c, :, n * rest : (n + 1) * rest
                        ].astype(pool.dtype)

        pl.semaphore_wait(barrier, expected)
        k_copy.wait()
        send_faces([0, 1])

        lists.table(
            tab, agg_ref[...] - device * aggs_here, own_ref[...], me_z // stride_z, me["gx"], sizes
        )
        t_copy = pltpu.make_async_copy(tab, table_ref, t_sem)
        t_copy.start()
        msg_far[...] = jnp.zeros_like(msg_far)
        for sub in range(per_owner):
            for piece, slot in ((5, sub), (6, out_slots - per_owner + sub)):
                rows_ref[slot, piece * LANES : (piece + 1) * LANES, :] = jnp.zeros(
                    (LANES, LANES), rows_ref.dtype
                )
        pool[zero_block] = jnp.zeros(pool.shape[1:], pool.dtype)

        @pl.loop(0, elems // 4)
        def _(group):
            for u in range(4):
                e = group * 4 + u
                pool[e] = block(e)[:, :width].astype(pool.dtype)

        t_copy.wait()
        send_faces([*range(4, nch), 2, 3])

        @pl.loop(0, elems // 4)
        def _(group):
            for u in range(4):
                e = group * 4 + u
                pt[e] = block(e).T[:tall].astype(pt.dtype)

        def lay_out(i):
            k = block_at(i)
            j_copy(i).wait()
            own = (k == 0).astype(jnp.float32)
            spread(
                lambda c: jraw[i % AHEAD, pl.ds(c * step_rows, step_rows)],
                res_ref[...].astype(jnp.float32) * own,
            )

            @pl.when(i + AHEAD < sides)
            def _():
                j_copy(i + AHEAD).start()

            @pl.loop(0, elems // 4)
            def _(group):
                for u in range(4):
                    e = group * 4 + u
                    jm[k, e] = block(e).astype(jm.dtype)

        my_group = me_z // stride_z

        def target_of(r):
            return partner_bits(my_group, r // per_owner) * stride_z

        def slot_of(z, r):
            return z * per_owner + r % per_owner

        def late(piece):
            return int(piece > 4)

        def row_copy(r, piece):
            at = pl.ds(pl.multiple_of(piece * LANES, LANES), LANES)
            slot = slot_of(me_z, r)
            last = piece == sides
            return pltpu.make_async_remote_copy(
                src_ref=msg.at[r, at],
                dst_ref=tail_ref.at[slot] if last else rows_ref.at[slot, at],
                send_sem=r_send.at[r],
                recv_sem=r_recv.at[slot, late(piece)],
                device_id={"gz": target_of(r)},
                device_id_type=MESH,
            )

        def self_copy(r, piece):
            at = pl.ds(pl.multiple_of(piece * LANES, LANES), LANES)
            slot = slot_of(me_z, r)
            return pltpu.make_async_copy(
                msg.at[r, at],
                tail_ref.at[slot] if piece == sides else rows_ref.at[slot, at],
                self_sem.at[r % per_owner, late(piece)],
            )

        def send_row(r, piece):
            sent = present(piece, me_z)

            @pl.when((target_of(r) != me_z) & sent)
            def _():
                row_copy(r, piece).start()

            @pl.when((target_of(r) == me_z) & sent)
            def _():
                self_copy(r, piece).start()

        def emit(r, s, value):
            msg[r, s * LANES : (s + 1) * LANES, :] = value[:LANES, :LANES].astype(msg.dtype)
            msg_rem[r, s * 8 : (s + 1) * 8, :] = value[LANES:tall, :LANES]
            msg_far[r, :, s * rest : (s + 1) * rest] = value[:, LANES:width]

        def present(piece, z):
            if piece == 5:
                return z > 0
            if piece == 6:
                return z < size_z - 1
            return True

        def side_sum(r, d):
            total = None
            for m in range(on_face):
                code = table_ref[nch + 1 + d, r * on_face + m]
                e, n = code % elems, jnp.clip(code // elems, 0, zero_block)
                product = mul(jm[1 + d, e], pool[n]).astype(jnp.bfloat16)
                triple = mul(pt[e], product)
                total = triple if total is None else total + triple
            return total

        def own_slot(r):
            acc[...] = jnp.zeros_like(acc)
            racc[...] = jnp.zeros_like(racc)

            @pl.loop(0, members // 4)
            def _(pair):
                total = None
                for u in range(4):
                    code = table_ref[nch, r * members + pair * 4 + u]
                    e, code = code % elems, code // elems
                    product = mul(jm[0, e], pool[e])
                    for axis in range(3):
                        x, code = code % (2 * elems), code // (2 * elems)
                        k = 1 + 2 * axis + x // elems
                        product = product + mul(jm[k, e], pool[x % elems])
                    racc[...] += product[LANES:tall]
                    triple = mul(pt[e], product.astype(jnp.bfloat16))
                    total = triple if total is None else total + triple
                acc[...] += total

            below = racc[...]
            spare = lax.broadcasted_iota(jnp.int32, below.shape, 0) == width - LANES
            acc[LANES:tall, :] += jnp.where(spare, below, 0.0)
            emit(r, 0, acc[...])
            send_row(r, 0)

        def pack_row_tail(r):
            msg_rem[r, sides * 8 : (sides + 1) * 8, :] = msg_far[r, LANES:tall, :]
            msg[r, tail : tail + half, :] = msg_rem[r].astype(msg.dtype)
            right = pltpu.roll(msg_far[r, half:LANES, :], half, 1)
            left = msg_far[r, :half, :]
            folded = jnp.where(lane_ids(left.shape) < half, left, right)
            msg[r, tail + half : msg_rows, :] = folded.astype(msg.dtype)

        def side_slots(r, axis):
            pair = (2 * axis, 2 * axis + 1)
            for d, total in [(d, side_sum(r, d)) for d in pair]:
                emit(r, 1 + d, total)
            if axis == 2:
                pack_row_tail(r)
            for d in pair:
                send_row(r, 1 + d)
            if axis == 2:
                send_row(r, sides)

        axis_faces = [list(range(4, nch)), [2, 3], [0, 1]]

        for step in range(size_z - 2):
            for way, ahead in enumerate((1, -1)):
                told = (me_z - ahead, me_z + ahead * (1 + step), me_z + ahead * (2 + step))
                inside = [(z >= 0) & (z < size_z) for z in told]

                @pl.when(inside[0] & inside[1])
                def _(way=way, step=step, ahead=ahead):
                    pl.semaphore_signal(
                        relay_sem.at[way, step],
                        inc=1,
                        device_id={"gz": me_z - ahead},
                        device_id_type=MESH,
                    )

                @pl.when(inside[2])
                def _(way=way, step=step):
                    pl.semaphore_wait(relay_sem.at[way, step], 1)

        @pl.loop(0, 2)
        def _(part):
            first, last = part * early, part * early + early

            @pl.when(part == 0)
            def _():
                pl.loop(0, 2)(lay_out)
                take_faces(axis_faces[0])

            pl.loop(first, last)(lambda r: side_slots(r, 0))

            @pl.when(part == 0)
            def _():
                pl.loop(2, sides)(lay_out)

            pl.loop(first, last)(own_slot)
            for axis in (1, 2):

                @pl.when(part == 0)
                def _(axis=axis):
                    take_faces(axis_faces[axis])

                pl.loop(first, last)(lambda r, axis=axis: side_slots(r, axis))

        owner = me_z % stride_z == 0

        def span(group, z):
            start, count = (0, 5) if group == 0 else (5, pieces - 5)
            if group == 1 and z in (0, size_z - 1):
                count -= 1
            return pl.ds(start * LANES, count * LANES)

        def arrive(group):
            for slot in range(out_slots):
                at = span(group, slot // per_owner)
                mine = slot // per_owner == me_z

                @pl.when(mine)
                def _(slot=slot, at=at):
                    pltpu.make_async_copy(
                        msg.at[0, at], msg.at[1, at], self_sem.at[slot % per_owner, group]
                    ).wait()

                @pl.when(jnp.logical_not(mine))
                def _(slot=slot, at=at):
                    pltpu.make_async_remote_copy(
                        src_ref=msg.at[0, at],
                        dst_ref=msg.at[0, at],
                        send_sem=r_send.at[0],
                        recv_sem=r_recv.at[slot, group],
                        device_id={"gz": me_z},
                        device_id_type=MESH,
                    ).wait_recv()

        def unpack():
            for s in range(sides):
                if s in (0, 5):
                    arrive(late(s))
                for slot in range(out_slots):
                    block_of = rows_ref[slot, s * LANES : (s + 1) * LANES, :]
                    scatter(mixed, out_slots, slot, 0, block_of.astype(jnp.float32))
                out_ref[s, :LANES, :, :LANES] = gathered(mixed[...], LANES, out_slots)

        if stride_z == 1:
            unpack()
        else:
            pl.when(owner)(unpack)

            @pl.when(jnp.logical_not(owner))
            def _():
                out_ref[...] = jnp.zeros_like(out_ref)
                tail_ref[...] = jnp.zeros_like(tail_ref)

        for c in range(nch):

            @when_sent(c)
            def _(c=c):
                whole_face(c).wait_send()

        @pl.loop(0, aggs_here)
        def _(r):
            @pl.when(target_of(r) != me_z)
            def _():
                inside = (me_z > 0) & (me_z < size_z - 1)
                for count, at_end in ((pieces, False), (pieces - 1, True)):

                    @pl.when(inside != at_end)
                    def _(count=count):
                        at = pl.ds(0, count * LANES)
                        pltpu.make_async_remote_copy(
                            src_ref=msg.at[r, at],
                            dst_ref=msg.at[r, at],
                            send_sem=r_send.at[r],
                            recv_sem=r_recv.at[0, 0],
                            device_id={"gz": target_of(r)},
                            device_id_type=MESH,
                        ).wait_send()

    bf16, f32 = jnp.bfloat16, jnp.float32
    spread_rows = (width + 1) * pitch
    faces = [pltpu.VMEM((face_rows(count, full), LANES), bf16) for _, _, count, _ in channels]
    table_rows = pl.cdiv(nch + sides, 8) * 8
    scratch = [
        *[pltpu.VMEM(a.shape, a.dtype) for a in (neighbours, agg_map, owners, residual)],
        pltpu.VMEM((8, LANES), jnp.int32),
        pltpu.SMEM((8, LANES), jnp.int32),
        pltpu.VMEM((table_rows, LANES), jnp.int32),
        pltpu.SMEM((table_rows, LANES), jnp.int32),
        pltpu.VMEM((width, elems, width), bf16),
        pltpu.VMEM((AHEAD, width, elems, width), bf16),
        pltpu.VMEM((spread_rows, LANES), f32),
        pltpu.VMEM((spread_rows, LANES), f32),
        pltpu.VMEM((zero_block + 1, full, width), bf16),
        pltpu.VMEM((elems, tall, full), bf16),
        pltpu.VMEM((sides, elems, full, full), bf16),
        *faces,
        *faces,
        pltpu.VMEM((nch, most * 8, LANES), f32),
        pltpu.VMEM((nch, full, LANES), f32),
        pltpu.VMEM((aggs_here, msg_rows, LANES), bf16),
        pltpu.VMEM((aggs_here, (sides + 1) * 8, LANES), f32),
        pltpu.VMEM((aggs_here, tall, LANES), f32),
        pltpu.VMEM((8, width), f32),
        pltpu.VMEM((tall, width), f32),
        pltpu.VMEM((out_slots, tail, LANES), bf16),
        pltpu.VMEM((LANES * out_slots, LANES), f32),
        pltpu.SemaphoreType.DMA((4,)),
        pltpu.SemaphoreType.DMA,
        pltpu.SemaphoreType.DMA,
        pltpu.SemaphoreType.DMA,
        pltpu.SemaphoreType.DMA((AHEAD,)),
        pltpu.SemaphoreType.DMA((nch,)),
        pltpu.SemaphoreType.DMA((nch,)),
        pltpu.SemaphoreType.DMA((aggs_here,)),
        pltpu.SemaphoreType.DMA((out_slots, 2)),
        pltpu.SemaphoreType.DMA((per_owner, 2)),
        pltpu.SemaphoreType.REGULAR((2, size_z - 2)),
    ]
    return pl.pallas_call(
        kernel,
        in_specs=[pl.BlockSpec(memory_space=pl.ANY)] * 6,
        out_specs=[pl.BlockSpec(memory_space=pltpu.VMEM)] * 2,
        out_shape=[
            pltpu.VMEM((sides, width, out_slots, width), bf16),
            pltpu.VMEM((out_slots, LANES, LANES), bf16),
        ],
        scratch_shapes=scratch,
        compiler_params=pltpu.CompilerParams(
            collective_id=0, has_side_effects=True, vmem_limit_bytes=54 << 20
        ),
    )(neighbours, agg_map, owners, prolong, jac, residual)


def scatter(ref, out_slots, slot, start, value):
    count = value.shape[0]
    ref[pl.ds(start * out_slots + slot, count, stride=out_slots), :] = value


def gathered(value, count, out_slots):
    return value.astype(jnp.bfloat16).reshape(count, out_slots, LANES)


def stored(coarse, tails):
    sides, width, out_slots, _ = coarse.shape
    rest = width - LANES
    half = LANES // 2
    tall = pl.cdiv(width + 1, 8) * 8

    def kernel(_, tail_ref, kept, out_hbm, small_hbm, mixed, mixed_rem, restr, small, sems):
        for slot in range(out_slots):
            below = tail_ref[slot, :half].astype(jnp.float32)
            folded = tail_ref[slot, half:].astype(jnp.float32)
            scatter(mixed, out_slots, slot, 0, folded)
            scatter(mixed, out_slots, slot, half, pltpu.roll(folded, half, 1))
            scatter(mixed, out_slots, slot, LANES, below[sides * 8 :])
            for s in range(sides):
                scatter(mixed_rem.at[s], out_slots, slot, 0, below[s * 8 : (s + 1) * 8])
            restr[slot : slot + 1, :LANES] = below[rest : rest + 1]
            at = sides * 8 + rest
            restr[slot : slot + 1, LANES:] = below[at : at + 1, :rest]
        small[...] = restr[:out_slots].astype(small.dtype)
        copies = [pltpu.make_async_copy(small, small_hbm, sems.at[sides])]
        copies[0].start()
        for s in range(sides):
            low = gathered(mixed_rem[s], 8, out_slots)
            kept[s, LANES:, :, :LANES] = low[:rest]
            right = mixed[...]
            if s > 0:
                right = pltpu.roll(right, LANES - s * rest, 1)
            kept[s, :, :, LANES:] = gathered(right, tall, out_slots)[:width, :, :rest]
            copies.append(pltpu.make_async_copy(kept.at[s], out_hbm.at[s], sems.at[s]))
            copies[-1].start()
        for copy in copies:
            copy.wait()

    f32 = jnp.float32
    _, out, small = pl.pallas_call(
        kernel,
        in_specs=[pl.BlockSpec(memory_space=pltpu.VMEM)] * 2,
        out_specs=[pl.BlockSpec(memory_space=pltpu.VMEM)]
        + [pl.BlockSpec(memory_space=pl.ANY)] * 2,
        out_shape=[
            pltpu.VMEM(coarse.shape, coarse.dtype),
            jax.ShapeDtypeStruct(coarse.shape, coarse.dtype),
            jax.ShapeDtypeStruct((out_slots, width), coarse.dtype),
        ],
        input_output_aliases={0: 0},
        scratch_shapes=[
            pltpu.VMEM((tall * out_slots, LANES), f32),
            pltpu.VMEM((sides, 8 * out_slots, LANES), f32),
            pltpu.VMEM((pl.cdiv(out_slots, 8) * 8, width), f32),
            pltpu.VMEM((out_slots, width), coarse.dtype),
            pltpu.SemaphoreType.DMA((sides + 1,)),
        ],
        compiler_params=pltpu.CompilerParams(vmem_limit_bytes=4 << 20),
    )(coarse, tails)
    return out, small


class Lists:
    def __init__(self, nbr, base):
        self.nbr, self.base = nbr, base
        square = (nbr.shape[1],) * 2
        self.down = lax.broadcasted_iota(jnp.int32, square, 0)
        self.along = lax.broadcasted_iota(jnp.int32, square, 1)
        self.eye = flag(self.down == self.along)
        self.before = flag(self.along < self.down)

    def column(self, row):
        return by_row(self.eye * row)

    def row(self, col):
        return by_column(self.eye * col)

    def listed(self, place, value):
        return by_column(flag(place == self.along) * value)

    def side(self, d):
        elems = self.nbr.shape[1]
        local = self.nbr[d : d + 1] - self.base
        away_row = 1 - flag(local >= 0) * flag(local < elems)
        rank = by_row(self.before * away_row)
        place = jnp.where(self.column(away_row) > 0, rank, -1)
        return self.listed(place, self.down[:, :1])

    def table(self, tab, agg, owners, mine, x, sizes):
        write_table(self, tab, agg, owners, mine, x, sizes)


def flag(mask):
    return jnp.where(mask, 1, 0)


def by_row(value):
    return jnp.sum(value, axis=1, keepdims=True)


def by_column(value):
    return jnp.sum(value, axis=0, keepdims=True)


def write_table(lists, tab, agg, owners, mine, x, sizes):
    nbr, base = lists.nbr, lists.base
    column, row, listed = lists.column, lists.row, lists.listed
    size_x, _, size_z = sizes
    elems, aggs_here = nbr.shape[1], owners.shape[1]
    per_owner = aggs_here // GROUPS
    stride_z = size_z // GROUPS
    members = elems // aggs_here
    on_face = members // 2
    channels = channels_of(size_x)
    offsets, zero_block = channel_offsets(channels, elems)
    nch = len(channels)
    along, before = lists.along, lists.before
    ids = lists.down[:, :1]

    def put(at, value):
        tab[at : at + 1, :elems] = value

    a_down = lax.broadcasted_iota(jnp.int32, (aggs_here, aggs_here), 0)
    a_along = lax.broadcasted_iota(jnp.int32, (aggs_here, aggs_here), 1)
    to = owners // stride_z
    crosses = jnp.abs(to // 2 - mine // 2)
    flips = jnp.abs(to % 2 - mine % 2)
    turn = 2 * (1 - crosses) + (1 + flips + crosses * ((mine // 2 + mine % 2) % 2)) % 2
    turn = jnp.broadcast_to(turn, a_down.shape)
    turn = by_row(jnp.where(a_down == a_along, turn, 0))
    if per_owner > 1:
        turn_row = by_column(jnp.where(a_down == a_along, turn, 0))
        equal = flag(turn_row == turn) * flag(a_along < a_down)
        turn = turn * per_owner + by_row(equal)
    a_ids = lax.broadcasted_iota(jnp.int32, (aggs_here, elems), 0)
    order_row = by_column(flag(agg == a_ids) * turn)
    order = column(order_row)
    agg_col = column(agg)
    together = before * flag(order_row == order)
    m_place = order * members + by_row(together)

    if size_x == 2:
        listing = [(3, 2), (2, 3)]
        sources = [4, 4, 2, 3, 0, 1]
    else:
        listing = [(3, 2), (2, 3), (1, 4), (0, 5)]
        sources = [4, 5, 2, 3, 0, 1]
    local_of, same_of = [], []
    for d in range(6):
        nbr_row = nbr[d : d + 1]
        nbr_col = column(nbr_row)
        local_row, local = nbr_row - base, nbr_col - base
        away_row = 1 - flag(local_row >= 0) * flag(local_row < elems)
        here = flag(local >= 0) * flag(local < elems)
        crossing = away_row * flag(nbr_row >= 0)
        position = by_row(crossing * flag(nbr_row < nbr_col))
        index = jnp.where(here > 0, local, position + offsets[sources[d]])
        index = jnp.where(nbr_col >= 0, index, zero_block)
        near_agg = by_row(flag(local == along) * agg)
        same = here * flag(near_agg == agg_col)
        local_of.append(local)
        same_of.append(same)
        s_rank = by_row(together * (1 - row(same)))
        s_place = jnp.where(same > 0, -1, order * on_face + s_rank)
        put(nch + 1 + d, listed(s_place, ids + elems * index))
    for d, c in listing:
        put(c, lists.side(d))
    if size_x == 2:
        put(4, jnp.where(x == 0, lists.side(1), lists.side(0)))
    code = jnp.zeros_like(ids)
    for axis in (2, 1, 0):
        after = same_of[2 * axis + 1] > 0
        inner = jnp.where(after, local_of[2 * axis + 1] + elems, local_of[2 * axis])
        code = code * (2 * elems) + inner
    put(nch, listed(m_place, code * elems + ids))


def body(jacobian, prolong, residual, neighbours, agg_map, owners):
    sizes = tuple(lax.axis_size(a) for a in ("gx", "gy", "gz"))
    coarse, tails = fused_kernel(
        neighbours.T,
        agg_map[None],
        owners[None],
        jnp.transpose(prolong, (1, 0, 2)),
        jnp.transpose(jacobian, (1, 2, 0, 3)),
        residual,
        sizes,
    )
    coarse, restricted = stored(coarse, tails)
    return jnp.transpose(coarse, (2, 0, 1, 3)), restricted


def solution(mesh):
    spec = P(("gx", "gy", "gz"))
    return jax.shard_map(
        body,
        mesh=mesh,
        in_specs=(spec,) * 6,
        out_specs=(spec, spec),
        check_vma=False,
    )
```

```python
import jax
import jax.numpy as jnp
from jax import lax
from jax.experimental import pallas as pl
from jax.experimental.pallas import tpu as pltpu
from jax.sharding import PartitionSpec as P

LX = 4
LY = 4
LZ = 2
GROUPS = 4
LANES = 128
CHUNK = 4
AHEAD = 4
MESH = pl.DeviceIdType.MESH


def mul(a, b):
    return jnp.dot(a, b, preferred_element_type=jnp.float32)


def lane_ids(shape):
    return lax.broadcasted_iota(jnp.int32, shape, 1)


def channels_of(size_x):
    z = [("gz", 1, LX * LY, 5), ("gz", -1, LX * LY, 4)]
    y = [("gy", 1, LX * LZ, 3), ("gy", -1, LX * LZ, 2)]
    if size_x == 2:
        x = [("gx", 0, LY * LZ, None)]
    else:
        x = [("gx", 1, LY * LZ, 1), ("gx", -1, LY * LZ, 0)]
    return z + y + x


def channel_offsets(channels, elems):
    offsets, at = [], elems
    for _, _, count, _ in channels:
        offsets.append(at)
        at += count
    return offsets, at


def face_rows(count, tall):
    return count * LANES + count * 8 + tall


def partner_bits(me, r):
    high, low = me // 2, me % 2
    inner = (high + low) % 2
    cross = 1 - r // 2
    turn = (1 + r + inner * cross) % 2
    high = high + cross * (1 - 2 * high)
    low = low + turn * (1 - 2 * low)
    return high * 2 + low


def fused_kernel(neighbours, agg_map, owners, prolong, jac, residual, sizes):
    width, elems, _ = prolong.shape
    sides = jac.shape[0]
    aggs_here = owners.shape[1]
    size_x, size_y, size_z = sizes
    rest = width - LANES
    tall = pl.cdiv(width + 1, 8) * 8
    full = pl.cdiv(width + 1, 16) * 16
    pitch = elems + 1
    per_owner = aggs_here // GROUPS
    stride_z = size_z // GROUPS
    out_slots = size_z * per_owner
    members = elems // aggs_here
    on_face = members // 2
    channels = channels_of(size_x)
    offsets, zero_block = channel_offsets(channels, elems)
    nch = len(channels)
    tail = sides * LANES
    msg_rows = tail + LANES
    half = LANES // 2
    most = max(count for _, _, count, _ in channels)
    pieces = sides + 1
    early = aggs_here // 2
    step_rows = 5 if width % 5 == 0 else 1

    def kernel(nbr_in, agg_in, own_in, p_hbm, j_hbm, res_in, out_ref, tail_ref, *refs):
        nbr_ref, agg_ref, own_ref, res_ref, picks, picks_ref = refs[:6]
        refs = refs[6:]
        tab, table_ref, praw, jraw, near, far, pool, pt, jm = refs[:9]
        sends, recvs = refs[9 : 9 + nch], refs[9 + nch : 9 + 2 * nch]
        refs = refs[9 + 2 * nch :]
        remf, farf, msg, msg_rem, msg_far = refs[:5]
        rows_ref, mixed = refs[5:7]
        in_sem, k_sem, t_sem, p_sem, j_sem, f_send, f_recv, r_send, r_recv, self_sem, relay_sem = refs[7:]
        me = {"gx": lax.axis_index("gx"), "gy": lax.axis_index("gy"), "gz": lax.axis_index("gz")}
        size = {"gx": size_x, "gy": size_y, "gz": size_z}
        me_z = me["gz"]

        p_copy = pltpu.make_async_copy(p_hbm, praw, p_sem)
        p_copy.start()
        small = [
            pltpu.make_async_copy(source, ref, in_sem.at[i])
            for i, (source, ref) in enumerate(
                zip((nbr_in, agg_in, own_in, res_in), (nbr_ref, agg_ref, own_ref, res_ref))
            )
        ]
        for copy in small:
            copy.start()

        def block_at(i):
            return (i + 1) * (i < 2) + i * (i > 2)

        def j_copy(i):
            slot = i % AHEAD
            return pltpu.make_async_copy(
                j_hbm.at[block_at(i)], jraw.at[slot], j_sem.at[slot]
            )

        barrier = pltpu.get_barrier_semaphore()
        expected = 0
        if size_x == 2:
            pl.semaphore_signal(
                barrier, inc=1, device_id={"gx": 1 - me["gx"]}, device_id_type=MESH
            )
            expected = expected + 1
        for axis in ["gz", "gy"] + (["gx"] if size_x > 2 else []):
            for step in (1, -1):
                there = me[axis] + step
                exists = (there >= 0) & (there < size[axis])

                @pl.when(exists)
                def _(axis=axis, there=there):
                    pl.semaphore_signal(
                        barrier, inc=1, device_id={axis: there}, device_id_type=MESH
                    )

                expected = expected + exists.astype(jnp.int32)

        def spread(load, last):
            @pl.loop(0, width // step_rows)
            def _(c):
                part = load(c).astype(jnp.float32)
                for i in range(step_rows):
                    rows = pl.ds((c * step_rows + i) * pitch, elems)
                    near[rows, :] = part[i, :, :LANES]
                    far[rows, :rest] = part[i, :, LANES:]

            near[pl.ds(width * pitch, elems), :] = last[:, :LANES]
            far[pl.ds(width * pitch, elems), :rest] = last[:, LANES:]

        def block(e):
            rows = pl.ds(e, width + 1, stride=pitch)
            right = far[rows, :]
            right = jnp.where(lane_ids(right.shape) < rest, right, 0.0)
            both = jnp.concatenate([near[rows, :], right], axis=1)[:, :full]
            below = jnp.zeros((full - width - 1, full), jnp.float32)
            return jnp.concatenate([both, below], axis=0)

        device = (me["gx"] * size_y + me["gy"]) * size_z + me_z
        for copy in small:
            copy.wait()
        lists = Lists(nbr_ref[...], device * elems)
        for c in range(2):
            picks[c : c + 1, :elems] = lists.side(channels[c][3])
        k_copy = pltpu.make_async_copy(picks, picks_ref, k_sem)
        k_copy.start()
        for c in range(2):
            farf[c, tall:, :] = jnp.zeros((full - tall, LANES), jnp.float32)
        p_copy.wait()
        for k in range(AHEAD):
            j_copy(k).start()
        spread(
            lambda c: praw[pl.ds(c * step_rows, step_rows)],
            jnp.zeros((elems, width), jnp.float32),
        )

        def face_target(c):
            axis, step, _, _ = channels[c]
            return {axis: 1 - me[axis] if step == 0 else me[axis] + step}

        def when_sent(c):
            axis, step, _, _ = channels[c]
            if step == 0:
                return lambda f: f()
            there = me[axis] + step
            return pl.when((there >= 0) & (there < size[axis]))

        def when_received(c):
            axis, step, _, _ = channels[c]
            if step == 0:
                return lambda f: f()
            there = me[axis] - step
            return pl.when((there >= 0) & (there < size[axis]))

        def face_parts(c):
            count = channels[c][2]
            parts = [(n * LANES, CHUNK * LANES) for n in range(0, count, CHUNK)]
            return parts + [(count * LANES, count * 8 + full)]

        def face_copy(c, part):
            start, rows = face_parts(c)[part]
            return pltpu.make_async_remote_copy(
                src_ref=sends[c].at[pl.ds(start, rows)],
                dst_ref=recvs[c].at[pl.ds(start, rows)],
                send_sem=f_send.at[c],
                recv_sem=f_recv.at[c],
                device_id=face_target(c),
                device_id_type=MESH,
            )

        def whole_face(c):
            return pltpu.make_async_remote_copy(
                src_ref=sends[c],
                dst_ref=recvs[c],
                send_sem=f_send.at[c],
                recv_sem=f_recv.at[c],
                device_id=face_target(c),
                device_id_type=MESH,
            )

        def pack(c, n):
            if c < 2:
                rows = pl.ds(picks_ref[c, n] % elems, width + 1, stride=pitch)
                left, right = near[rows, :], far[rows, :]
                sends[c][n * LANES : (n + 1) * LANES, :] = left[:LANES].astype(jnp.bfloat16)
                remf[c, n * 8 : (n + 1) * 8, :] = left[LANES:tall]
                farf[c, :tall, n * rest : (n + 1) * rest] = right[:, :rest]
                return
            whole = pool[table_ref[c, n] % elems]
            sends[c][n * LANES : (n + 1) * LANES, :] = whole[:LANES, :LANES]
            remf[c, n * 8 : (n + 1) * 8, :] = whole[LANES:tall, :LANES].astype(jnp.float32)
            farf[c, :, n * rest : (n + 1) * rest] = whole[:, LANES:width].astype(jnp.float32)

        def pack_tail(c):
            count = channels[c][2]
            at = count * LANES
            sends[c][at : at + count * 8, :] = remf[c, : count * 8, :].astype(jnp.bfloat16)
            sends[c][at + count * 8 : at + count * 8 + full, :] = farf[c].astype(jnp.bfloat16)

        def send_faces(group):
            for part in range(max(len(face_parts(c)) for c in group)):
                for c in group:
                    if part < len(face_parts(c)) - 1:
                        for n in range(part * CHUNK, (part + 1) * CHUNK):
                            pack(c, n)
                    elif part < len(face_parts(c)):
                        pack_tail(c)
                    if part < len(face_parts(c)):

                        @when_sent(c)
                        def _(c=c, part=part):
                            face_copy(c, part).start()

        def take_faces(group):
            for c in group:

                @when_received(c)
                def _(c=c):
                    whole_face(c).wait_recv()
                    count = channels[c][2]
                    at = count * LANES
                    remf[c, : count * 8, :] = recvs[c][at : at + count * 8, :].astype(jnp.float32)
                    farf[c] = recvs[c][at + count * 8 : at + count * 8 + full, :].astype(
                        jnp.float32
                    )
                    for n in range(count):
                        to = offsets[c] + n
                        pool[to, :LANES, :LANES] = recvs[c][n * LANES : (n + 1) * LANES, :]
                        below = remf[c, n * 8 : (n + 1) * 8, :]
                        below = jnp.concatenate([below, jnp.zeros_like(below)], axis=0)
                        pool[to, LANES:full, :LANES] = below.astype(pool.dtype)
                        pool[to, :, LANES:width] = farf[
                            c, :, n * rest : (n + 1) * rest
                        ].astype(pool.dtype)

        pl.semaphore_wait(barrier, expected)
        k_copy.wait()
        send_faces([0, 1])

        lists.table(
            tab, agg_ref[...] - device * aggs_here, own_ref[...], me_z // stride_z, me["gx"], sizes
        )
        t_copy = pltpu.make_async_copy(tab, table_ref, t_sem)
        t_copy.start()
        msg_far[...] = jnp.zeros_like(msg_far)
        for sub in range(per_owner):
            for piece, slot in ((5, sub), (6, out_slots - per_owner + sub)):
                rows_ref[slot, piece * LANES : (piece + 1) * LANES, :] = jnp.zeros(
                    (LANES, LANES), rows_ref.dtype
                )
        pool[zero_block] = jnp.zeros(pool.shape[1:], pool.dtype)

        @pl.loop(0, elems // 4)
        def _(group):
            for u in range(4):
                e = group * 4 + u
                pool[e] = block(e)[:, :width].astype(pool.dtype)

        t_copy.wait()
        send_faces([*range(4, nch), 2, 3])

        @pl.loop(0, elems // 8)
        def _(group):
            for u in range(8):
                e = group * 8 + u
                pt[e] = block(e).T[:tall].astype(pt.dtype)

        def lay_out(i):
            k = block_at(i)
            j_copy(i).wait()
            own = (k == 0).astype(jnp.float32)
            spread(
                lambda c: jraw[i % AHEAD, pl.ds(c * step_rows, step_rows)],
                res_ref[...].astype(jnp.float32) * own,
            )

            @pl.when(i + AHEAD < sides)
            def _():
                j_copy(i + AHEAD).start()

            @pl.loop(0, elems // 4)
            def _(group):
                for u in range(4):
                    e = group * 4 + u
                    jm[k, e] = block(e).astype(jm.dtype)

        my_group = me_z // stride_z

        def target_of(r):
            return partner_bits(my_group, r // per_owner) * stride_z

        def slot_of(z, r):
            return z * per_owner + r % per_owner

        def late(piece):
            return int(piece > 4)

        def row_copy(r, piece):
            at = pl.ds(pl.multiple_of(piece * LANES, LANES), LANES)
            slot = slot_of(me_z, r)
            last = piece == sides
            return pltpu.make_async_remote_copy(
                src_ref=msg.at[r, at],
                dst_ref=tail_ref.at[slot] if last else rows_ref.at[slot, at],
                send_sem=r_send.at[r],
                recv_sem=r_recv.at[slot, late(piece)],
                device_id={"gz": target_of(r)},
                device_id_type=MESH,
            )

        def self_copy(r, piece):
            at = pl.ds(pl.multiple_of(piece * LANES, LANES), LANES)
            slot = slot_of(me_z, r)
            return pltpu.make_async_copy(
                msg.at[r, at],
                tail_ref.at[slot] if piece == sides else rows_ref.at[slot, at],
                self_sem.at[r % per_owner, late(piece)],
            )

        def send_row(r, piece):
            sent = present(piece, me_z)

            @pl.when((target_of(r) != me_z) & sent)
            def _():
                row_copy(r, piece).start()

            @pl.when((target_of(r) == me_z) & sent)
            def _():
                self_copy(r, piece).start()

        def emit(r, s, value, more=0.0):
            msg[r, s * LANES : (s + 1) * LANES, :] = value[:LANES, :LANES].astype(msg.dtype)
            last = value[LANES:tall] + more
            msg_rem[r, s * 8 : (s + 1) * 8, :] = last[:, :LANES]
            lanes = slice(s * rest, (s + 1) * rest)
            msg_far[r, :LANES, lanes] = value[:LANES, LANES:width]
            msg_far[r, LANES:, lanes] = last[:, LANES:width]

        def present(piece, z):
            if piece == 5:
                return z > 0
            if piece == 6:
                return z < size_z - 1
            return True

        def side_sum(r, d):
            total = None
            for m in range(on_face):
                code = table_ref[nch + 1 + d, r * on_face + m]
                e, n = code % elems, jnp.clip(code // elems, 0, zero_block)
                product = mul(jm[1 + d, e], pool[n]).astype(jnp.bfloat16)
                triple = mul(pt[e], product)
                total = triple if total is None else total + triple
            return total

        def own_slot(r):
            total, below = None, None
            for m in range(members):
                code = table_ref[nch, r * members + m]
                e, code = code % elems, code // elems
                product = mul(jm[0, e], pool[e])
                for axis in range(3):
                    x, code = code % (2 * elems), code // (2 * elems)
                    k = 1 + 2 * axis + x // elems
                    product = product + mul(jm[k, e], pool[x % elems])
                last = product[LANES:tall]
                below = last if below is None else below + last
                triple = mul(pt[e], product.astype(jnp.bfloat16))
                total = triple if total is None else total + triple
            spare = lax.broadcasted_iota(jnp.int32, below.shape, 0) == width - LANES
            emit(r, 0, total, jnp.where(spare, below, 0.0))
            send_row(r, 0)

        def pack_row_tail(r):
            msg_rem[r, sides * 8 : (sides + 1) * 8, :] = msg_far[r, LANES:tall, :]
            msg[r, tail : tail + half, :] = msg_rem[r].astype(msg.dtype)
            right = pltpu.roll(msg_far[r, half:LANES, :], half, 1)
            left = msg_far[r, :half, :]
            folded = jnp.where(lane_ids(left.shape) < half, left, right)
            msg[r, tail + half : msg_rows, :] = folded.astype(msg.dtype)

        def side_slots(first, axis):
            todo = [(first + i, d) for i in range(early) for d in (2 * axis, 2 * axis + 1)]
            for (r, d), total in [(at, side_sum(*at)) for at in todo]:
                emit(r, 1 + d, total)
            if axis == 2:
                for i in range(early):
                    pack_row_tail(first + i)
            for r, d in todo:
                send_row(r, 1 + d)
            if axis == 2:
                for i in range(early):
                    send_row(first + i, sides)

        axis_faces = [list(range(4, nch)), [2, 3], [0, 1]]

        for step in range(size_z - 2):
            for way, ahead in enumerate((1, -1)):
                told = (me_z - ahead, me_z + ahead * (1 + step), me_z + ahead * (2 + step))
                inside = [(z >= 0) & (z < size_z) for z in told]

                @pl.when(inside[0] & inside[1])
                def _(way=way, step=step, ahead=ahead):
                    pl.semaphore_signal(
                        relay_sem.at[way, step],
                        inc=1,
                        device_id={"gz": me_z - ahead},
                        device_id_type=MESH,
                    )

                @pl.when(inside[2])
                def _(way=way, step=step):
                    pl.semaphore_wait(relay_sem.at[way, step], 1)

        @pl.loop(0, 2)
        def _(part):
            first, last = part * early, part * early + early

            @pl.when(part == 0)
            def _():
                pl.loop(0, 2)(lay_out)
                take_faces(axis_faces[0])

            side_slots(first, 0)

            @pl.when(part == 0)
            def _():
                pl.loop(2, sides)(lay_out)

            pl.loop(first, last)(own_slot)
            for axis in (1, 2):

                @pl.when(part == 0)
                def _(axis=axis):
                    take_faces(axis_faces[axis])

                side_slots(first, axis)

        owner = me_z % stride_z == 0

        def span(group, z):
            start, count = (0, 5) if group == 0 else (5, pieces - 5)
            if group == 1 and z in (0, size_z - 1):
                count -= 1
            return pl.ds(start * LANES, count * LANES)

        def arrive(group):
            for slot in range(out_slots):
                at = span(group, slot // per_owner)
                mine = slot // per_owner == me_z

                @pl.when(mine)
                def _(slot=slot, at=at):
                    pltpu.make_async_copy(
                        msg.at[0, at], msg.at[1, at], self_sem.at[slot % per_owner, group]
                    ).wait()

                @pl.when(jnp.logical_not(mine))
                def _(slot=slot, at=at):
                    pltpu.make_async_remote_copy(
                        src_ref=msg.at[0, at],
                        dst_ref=msg.at[0, at],
                        send_sem=r_send.at[0],
                        recv_sem=r_recv.at[slot, group],
                        device_id={"gz": me_z},
                        device_id_type=MESH,
                    ).wait_recv()

        def unpack():
            for s in range(sides):
                if s in (0, 5):
                    arrive(late(s))
                for slot in range(out_slots):
                    block_of = rows_ref[slot, s * LANES : (s + 1) * LANES, :]
                    scatter(mixed, out_slots, slot, 0, block_of.astype(jnp.float32))
                out_ref[s, :LANES, :, :LANES] = gathered(mixed[...], LANES, out_slots)

        if stride_z == 1:
            unpack()
        else:
            pl.when(owner)(unpack)

            @pl.when(jnp.logical_not(owner))
            def _():
                out_ref[...] = jnp.zeros_like(out_ref)
                tail_ref[...] = jnp.zeros_like(tail_ref)

        for c in range(nch):

            @when_sent(c)
            def _(c=c):
                whole_face(c).wait_send()

        @pl.loop(0, aggs_here)
        def _(r):
            @pl.when(target_of(r) != me_z)
            def _():
                inside = (me_z > 0) & (me_z < size_z - 1)
                for count, at_end in ((pieces, False), (pieces - 1, True)):

                    @pl.when(inside != at_end)
                    def _(count=count):
                        at = pl.ds(0, count * LANES)
                        pltpu.make_async_remote_copy(
                            src_ref=msg.at[r, at],
                            dst_ref=msg.at[r, at],
                            send_sem=r_send.at[r],
                            recv_sem=r_recv.at[0, 0],
                            device_id={"gz": target_of(r)},
                            device_id_type=MESH,
                        ).wait_send()

    bf16, f32 = jnp.bfloat16, jnp.float32
    spread_rows = (width + 1) * pitch
    faces = [pltpu.VMEM((face_rows(count, full), LANES), bf16) for _, _, count, _ in channels]
    table_rows = pl.cdiv(nch + sides, 8) * 8
    scratch = [
        *[pltpu.VMEM(a.shape, a.dtype) for a in (neighbours, agg_map, owners, residual)],
        pltpu.VMEM((8, LANES), jnp.int32),
        pltpu.SMEM((8, LANES), jnp.int32),
        pltpu.VMEM((table_rows, LANES), jnp.int32),
        pltpu.SMEM((table_rows, LANES), jnp.int32),
        pltpu.VMEM((width, elems, width), bf16),
        pltpu.VMEM((AHEAD, width, elems, width), bf16),
        pltpu.VMEM((spread_rows, LANES), f32),
        pltpu.VMEM((spread_rows, LANES), f32),
        pltpu.VMEM((zero_block + 1, full, width), bf16),
        pltpu.VMEM((elems, tall, full), bf16),
        pltpu.VMEM((sides, elems, full, full), bf16),
        *faces,
        *faces,
        pltpu.VMEM((nch, most * 8, LANES), f32),
        pltpu.VMEM((nch, full, LANES), f32),
        pltpu.VMEM((aggs_here, msg_rows, LANES), bf16),
        pltpu.VMEM((aggs_here, (sides + 1) * 8, LANES), f32),
        pltpu.VMEM((aggs_here, tall, LANES), f32),
        pltpu.VMEM((out_slots, tail, LANES), bf16),
        pltpu.VMEM((LANES * out_slots, LANES), f32),
        pltpu.SemaphoreType.DMA((4,)),
        pltpu.SemaphoreType.DMA,
        pltpu.SemaphoreType.DMA,
        pltpu.SemaphoreType.DMA,
        pltpu.SemaphoreType.DMA((AHEAD,)),
        pltpu.SemaphoreType.DMA((nch,)),
        pltpu.SemaphoreType.DMA((nch,)),
        pltpu.SemaphoreType.DMA((aggs_here,)),
        pltpu.SemaphoreType.DMA((out_slots, 2)),
        pltpu.SemaphoreType.DMA((per_owner, 2)),
        pltpu.SemaphoreType.REGULAR((2, size_z - 2)),
    ]
    return pl.pallas_call(
        kernel,
        in_specs=[pl.BlockSpec(memory_space=pl.ANY)] * 6,
        out_specs=[pl.BlockSpec(memory_space=pltpu.VMEM)] * 2,
        out_shape=[
            pltpu.VMEM((sides, width, out_slots, width), bf16),
            pltpu.VMEM((out_slots, LANES, LANES), bf16),
        ],
        scratch_shapes=scratch,
        compiler_params=pltpu.CompilerParams(
            collective_id=0, has_side_effects=True, vmem_limit_bytes=54 << 20
        ),
    )(neighbours, agg_map, owners, prolong, jac, residual)


def scatter(ref, out_slots, slot, start, value):
    count = value.shape[0]
    ref[pl.ds(start * out_slots + slot, count, stride=out_slots), :] = value


def gathered(value, count, out_slots):
    return value.astype(jnp.bfloat16).reshape(count, out_slots, LANES)


def stored(coarse, tails):
    sides, width, out_slots, _ = coarse.shape
    rest = width - LANES
    half = LANES // 2
    tall = pl.cdiv(width + 1, 8) * 8

    def kernel(_, tail_ref, kept, out_hbm, small_hbm, mixed, mixed_rem, restr, small, sems):
        for slot in range(out_slots):
            below = tail_ref[slot, :half].astype(jnp.float32)
            folded = tail_ref[slot, half:].astype(jnp.float32)
            scatter(mixed, out_slots, slot, 0, folded)
            scatter(mixed, out_slots, slot, half, pltpu.roll(folded, half, 1))
            scatter(mixed, out_slots, slot, LANES, below[sides * 8 :])
            for s in range(sides):
                scatter(mixed_rem.at[s], out_slots, slot, 0, below[s * 8 : (s + 1) * 8])
            restr[slot : slot + 1, :LANES] = below[rest : rest + 1]
            at = sides * 8 + rest
            restr[slot : slot + 1, LANES:] = below[at : at + 1, :rest]
        small[...] = restr[:out_slots].astype(small.dtype)
        copies = [pltpu.make_async_copy(small, small_hbm, sems.at[sides])]
        copies[0].start()
        for s in range(sides):
            low = gathered(mixed_rem[s], 8, out_slots)
            kept[s, LANES:, :, :LANES] = low[:rest]
            right = mixed[...]
            if s > 0:
                right = pltpu.roll(right, LANES - s * rest, 1)
            kept[s, :, :, LANES:] = gathered(right, tall, out_slots)[:width, :, :rest]
            copies.append(pltpu.make_async_copy(kept.at[s], out_hbm.at[s], sems.at[s]))
            copies[-1].start()
        for copy in copies:
            copy.wait()

    f32 = jnp.float32
    _, out, small = pl.pallas_call(
        kernel,
        in_specs=[pl.BlockSpec(memory_space=pltpu.VMEM)] * 2,
        out_specs=[pl.BlockSpec(memory_space=pltpu.VMEM)]
        + [pl.BlockSpec(memory_space=pl.ANY)] * 2,
        out_shape=[
            pltpu.VMEM(coarse.shape, coarse.dtype),
            jax.ShapeDtypeStruct(coarse.shape, coarse.dtype),
            jax.ShapeDtypeStruct((out_slots, width), coarse.dtype),
        ],
        input_output_aliases={0: 0},
        scratch_shapes=[
            pltpu.VMEM((tall * out_slots, LANES), f32),
            pltpu.VMEM((sides, 8 * out_slots, LANES), f32),
            pltpu.VMEM((pl.cdiv(out_slots, 8) * 8, width), f32),
            pltpu.VMEM((out_slots, width), coarse.dtype),
            pltpu.SemaphoreType.DMA((sides + 1,)),
        ],
        compiler_params=pltpu.CompilerParams(vmem_limit_bytes=4 << 20),
    )(coarse, tails)
    return out, small


class Lists:
    def __init__(self, nbr, base):
        self.nbr, self.base = nbr, base
        square = (nbr.shape[1],) * 2
        self.down = lax.broadcasted_iota(jnp.int32, square, 0)
        self.along = lax.broadcasted_iota(jnp.int32, square, 1)
        self.eye = flag(self.down == self.along)
        self.before = flag(self.along < self.down)

    def column(self, row):
        return by_row(self.eye * row)

    def row(self, col):
        return by_column(self.eye * col)

    def listed(self, place, value):
        return by_column(flag(place == self.along) * value)

    def side(self, d):
        elems = self.nbr.shape[1]
        local = self.nbr[d : d + 1] - self.base
        away_row = 1 - flag(local >= 0) * flag(local < elems)
        rank = by_row(self.before * away_row)
        place = jnp.where(self.column(away_row) > 0, rank, -1)
        return self.listed(place, self.down[:, :1])

    def table(self, tab, agg, owners, mine, x, sizes):
        write_table(self, tab, agg, owners, mine, x, sizes)


def flag(mask):
    return jnp.where(mask, 1, 0)


def by_row(value):
    return jnp.sum(value, axis=1, keepdims=True)


def by_column(value):
    return jnp.sum(value, axis=0, keepdims=True)


def write_table(lists, tab, agg, owners, mine, x, sizes):
    nbr, base = lists.nbr, lists.base
    column, row, listed = lists.column, lists.row, lists.listed
    size_x, _, size_z = sizes
    elems, aggs_here = nbr.shape[1], owners.shape[1]
    per_owner = aggs_here // GROUPS
    stride_z = size_z // GROUPS
    members = elems // aggs_here
    on_face = members // 2
    channels = channels_of(size_x)
    offsets, zero_block = channel_offsets(channels, elems)
    nch = len(channels)
    along, before = lists.along, lists.before
    ids = lists.down[:, :1]

    def put(at, value):
        tab[at : at + 1, :elems] = value

    a_down = lax.broadcasted_iota(jnp.int32, (aggs_here, aggs_here), 0)
    a_along = lax.broadcasted_iota(jnp.int32, (aggs_here, aggs_here), 1)
    to = owners // stride_z
    crosses = jnp.abs(to // 2 - mine // 2)
    flips = jnp.abs(to % 2 - mine % 2)
    turn = 2 * (1 - crosses) + (1 + flips + crosses * ((mine // 2 + mine % 2) % 2)) % 2
    turn = jnp.broadcast_to(turn, a_down.shape)
    turn = by_row(jnp.where(a_down == a_along, turn, 0))
    if per_owner > 1:
        turn_row = by_column(jnp.where(a_down == a_along, turn, 0))
        equal = flag(turn_row == turn) * flag(a_along < a_down)
        turn = turn * per_owner + by_row(equal)
    a_ids = lax.broadcasted_iota(jnp.int32, (aggs_here, elems), 0)
    order_row = by_column(flag(agg == a_ids) * turn)
    order = column(order_row)
    agg_col = column(agg)
    together = before * flag(order_row == order)
    m_place = order * members + by_row(together)

    if size_x == 2:
        listing = [(3, 2), (2, 3)]
        sources = [4, 4, 2, 3, 0, 1]
    else:
        listing = [(3, 2), (2, 3), (1, 4), (0, 5)]
        sources = [4, 5, 2, 3, 0, 1]
    local_of, same_of = [], []
    for d in range(6):
        nbr_row = nbr[d : d + 1]
        nbr_col = column(nbr_row)
        local_row, local = nbr_row - base, nbr_col - base
        away_row = 1 - flag(local_row >= 0) * flag(local_row < elems)
        here = flag(local >= 0) * flag(local < elems)
        crossing = away_row * flag(nbr_row >= 0)
        position = by_row(crossing * flag(nbr_row < nbr_col))
        index = jnp.where(here > 0, local, position + offsets[sources[d]])
        index = jnp.where(nbr_col >= 0, index, zero_block)
        near_agg = by_row(flag(local == along) * agg)
        same = here * flag(near_agg == agg_col)
        local_of.append(local)
        same_of.append(same)
        s_rank = by_row(together * (1 - row(same)))
        s_place = jnp.where(same > 0, -1, order * on_face + s_rank)
        put(nch + 1 + d, listed(s_place, ids + elems * index))
    for d, c in listing:
        put(c, lists.side(d))
    if size_x == 2:
        put(4, jnp.where(x == 0, lists.side(1), lists.side(0)))
    code = jnp.zeros_like(ids)
    for axis in (2, 1, 0):
        after = same_of[2 * axis + 1] > 0
        inner = jnp.where(after, local_of[2 * axis + 1] + elems, local_of[2 * axis])
        code = code * (2 * elems) + inner
    put(nch, listed(m_place, code * elems + ids))


def body(jacobian, prolong, residual, neighbours, agg_map, owners):
    sizes = tuple(lax.axis_size(a) for a in ("gx", "gy", "gz"))
    coarse, tails = fused_kernel(
        neighbours.T,
        agg_map[None],
        owners[None],
        jnp.transpose(prolong, (1, 0, 2)),
        jnp.transpose(jacobian, (1, 2, 0, 3)),
        residual,
        sizes,
    )
    coarse, restricted = stored(coarse, tails)
    return jnp.transpose(coarse, (2, 0, 1, 3)), restricted


def solution(mesh):
    spec = P(("gx", "gy", "gz"))
    return jax.shard_map(
        body,
        mesh=mesh,
        in_specs=(spec,) * 6,
        out_specs=(spec, spec),
        check_vma=False,
    )
```

```python
import jax
import jax.numpy as jnp
from jax import lax
from jax.experimental import pallas as pl
from jax.experimental.pallas import tpu as pltpu
from jax.sharding import PartitionSpec as P

LX = 4
LY = 4
LZ = 2
GROUPS = 4
LANES = 128
CHUNK = 4
AHEAD = 4
MESH = pl.DeviceIdType.MESH


def mul(a, b):
    return jnp.dot(a, b, preferred_element_type=jnp.float32)


def lane_ids(shape):
    return lax.broadcasted_iota(jnp.int32, shape, 1)


def channels_of(size_x):
    z = [("gz", 1, LX * LY, 5), ("gz", -1, LX * LY, 4)]
    y = [("gy", 1, LX * LZ, 3), ("gy", -1, LX * LZ, 2)]
    if size_x == 2:
        x = [("gx", 0, LY * LZ, None)]
    else:
        x = [("gx", 1, LY * LZ, 1), ("gx", -1, LY * LZ, 0)]
    return z + y + x


def channel_offsets(channels, elems):
    offsets, at = [], elems
    for _, _, count, _ in channels:
        offsets.append(at)
        at += count
    return offsets, at


def face_rows(count, tall):
    return count * LANES + count * 8 + tall


def partner_bits(me, r):
    high, low = me // 2, me % 2
    inner = (high + low) % 2
    cross = 1 - r // 2
    turn = (1 + r + inner * cross) % 2
    high = high + cross * (1 - 2 * high)
    low = low + turn * (1 - 2 * low)
    return high * 2 + low


def fused_kernel(neighbours, agg_map, owners, prolong, jac, residual, sizes):
    width, elems, _ = prolong.shape
    sides = jac.shape[0]
    aggs_here = owners.shape[1]
    size_x, size_y, size_z = sizes
    rest = width - LANES
    tall = pl.cdiv(width + 1, 8) * 8
    full = pl.cdiv(width + 1, 16) * 16
    pitch = elems + 1
    per_owner = aggs_here // GROUPS
    stride_z = size_z // GROUPS
    out_slots = size_z * per_owner
    members = elems // aggs_here
    on_face = members // 2
    channels = channels_of(size_x)
    offsets, zero_block = channel_offsets(channels, elems)
    nch = len(channels)
    tail = sides * LANES
    msg_rows = tail + LANES
    half = LANES // 2
    most = max(count for _, _, count, _ in channels)
    pieces = sides + 1
    early = aggs_here // 2
    step_rows = 5 if width % 5 == 0 else 1

    def kernel(nbr_in, agg_in, own_in, p_hbm, j_hbm, res_in, out_ref, tail_ref, *refs):
        nbr_ref, agg_ref, own_ref, res_ref, picks, picks_ref = refs[:6]
        refs = refs[6:]
        tab, table_ref, praw, jraw, near, far, pool, pt, jm = refs[:9]
        sends, recvs = refs[9 : 9 + nch], refs[9 + nch : 9 + 2 * nch]
        refs = refs[9 + 2 * nch :]
        remf, farf, msg, msg_rem, msg_far = refs[:5]
        rows_ref, mixed = refs[5:7]
        in_sem, k_sem, t_sem, p_sem, j_sem, f_send, f_recv, r_send, r_recv, self_sem, relay_sem = refs[7:]
        me = {"gx": lax.axis_index("gx"), "gy": lax.axis_index("gy"), "gz": lax.axis_index("gz")}
        size = {"gx": size_x, "gy": size_y, "gz": size_z}
        me_z = me["gz"]

        p_copy = pltpu.make_async_copy(p_hbm, praw, p_sem)
        p_copy.start()
        small = [
            pltpu.make_async_copy(source, ref, in_sem.at[i])
            for i, (source, ref) in enumerate(
                zip((nbr_in, agg_in, own_in, res_in), (nbr_ref, agg_ref, own_ref, res_ref))
            )
        ]
        for copy in small:
            copy.start()

        def block_at(i):
            return (i + 1) * (i < 2) + i * (i > 2)

        def j_copy(i):
            slot = i % AHEAD
            return pltpu.make_async_copy(
                j_hbm.at[block_at(i)], jraw.at[slot], j_sem.at[slot]
            )

        barrier = pltpu.get_barrier_semaphore()
        expected = 0
        if size_x == 2:
            pl.semaphore_signal(
                barrier, inc=1, device_id={"gx": 1 - me["gx"]}, device_id_type=MESH
            )
            expected = expected + 1
        for axis in ["gz", "gy"] + (["gx"] if size_x > 2 else []):
            for step in (1, -1):
                there = me[axis] + step
                exists = (there >= 0) & (there < size[axis])

                @pl.when(exists)
                def _(axis=axis, there=there):
                    pl.semaphore_signal(
                        barrier, inc=1, device_id={axis: there}, device_id_type=MESH
                    )

                expected = expected + exists.astype(jnp.int32)

        def spread(load, last):
            @pl.loop(0, width // step_rows)
            def _(c):
                part = load(c).astype(jnp.float32)
                for i in range(step_rows):
                    rows = pl.ds((c * step_rows + i) * pitch, elems)
                    near[rows, :] = part[i, :, :LANES]
                    far[rows, :rest] = part[i, :, LANES:]

            near[pl.ds(width * pitch, elems), :] = last[:, :LANES]
            far[pl.ds(width * pitch, elems), :rest] = last[:, LANES:]

        def block(e):
            rows = pl.ds(e, width + 1, stride=pitch)
            right = far[rows, :]
            right = jnp.where(lane_ids(right.shape) < rest, right, 0.0)
            both = jnp.concatenate([near[rows, :], right], axis=1)[:, :full]
            below = jnp.zeros((full - width - 1, full), jnp.float32)
            return jnp.concatenate([both, below], axis=0)

        device = (me["gx"] * size_y + me["gy"]) * size_z + me_z
        for copy in small:
            copy.wait()
        lists = Lists(nbr_ref[...], device * elems)
        for c in range(2):
            picks[c : c + 1, :elems] = lists.side(channels[c][3])
        k_copy = pltpu.make_async_copy(picks, picks_ref, k_sem)
        k_copy.start()
        for c in range(2):
            farf[c, tall:, :] = jnp.zeros((full - tall, LANES), jnp.float32)
        p_copy.wait()
        for k in range(AHEAD):
            j_copy(k).start()
        spread(
            lambda c: praw[pl.ds(c * step_rows, step_rows)],
            jnp.zeros((elems, width), jnp.float32),
        )

        def face_target(c):
            axis, step, _, _ = channels[c]
            return {axis: 1 - me[axis] if step == 0 else me[axis] + step}

        def when_sent(c):
            axis, step, _, _ = channels[c]
            if step == 0:
                return lambda f: f()
            there = me[axis] + step
            return pl.when((there >= 0) & (there < size[axis]))

        def when_received(c):
            axis, step, _, _ = channels[c]
            if step == 0:
                return lambda f: f()
            there = me[axis] - step
            return pl.when((there >= 0) & (there < size[axis]))

        def face_parts(c):
            count = channels[c][2]
            parts = [(n * LANES, CHUNK * LANES) for n in range(0, count, CHUNK)]
            return parts + [(count * LANES, count * 8 + full)]

        def face_copy(c, part):
            start, rows = face_parts(c)[part]
            return pltpu.make_async_remote_copy(
                src_ref=sends[c].at[pl.ds(start, rows)],
                dst_ref=recvs[c].at[pl.ds(start, rows)],
                send_sem=f_send.at[c],
                recv_sem=f_recv.at[c],
                device_id=face_target(c),
                device_id_type=MESH,
            )

        def whole_face(c):
            return pltpu.make_async_remote_copy(
                src_ref=sends[c],
                dst_ref=recvs[c],
                send_sem=f_send.at[c],
                recv_sem=f_recv.at[c],
                device_id=face_target(c),
                device_id_type=MESH,
            )

        def pack(c, n):
            if c < 2:
                rows = pl.ds(picks_ref[c, n] % elems, width + 1, stride=pitch)
                left, right = near[rows, :], far[rows, :]
                sends[c][n * LANES : (n + 1) * LANES, :] = left[:LANES].astype(jnp.bfloat16)
                remf[c, n * 8 : (n + 1) * 8, :] = left[LANES:tall]
                farf[c, :tall, n * rest : (n + 1) * rest] = right[:, :rest]
                return
            whole = pool[table_ref[c, n] % elems]
            sends[c][n * LANES : (n + 1) * LANES, :] = whole[:LANES, :LANES]
            remf[c, n * 8 : (n + 1) * 8, :] = whole[LANES:tall, :LANES].astype(jnp.float32)
            farf[c, :, n * rest : (n + 1) * rest] = whole[:, LANES:width].astype(jnp.float32)

        def pack_tail(c):
            count = channels[c][2]
            at = count * LANES
            sends[c][at : at + count * 8, :] = remf[c, : count * 8, :].astype(jnp.bfloat16)
            sends[c][at + count * 8 : at + count * 8 + full, :] = farf[c].astype(jnp.bfloat16)

        def send_faces(group):
            for part in range(max(len(face_parts(c)) for c in group)):
                for c in group:
                    if part < len(face_parts(c)) - 1:
                        for n in range(part * CHUNK, (part + 1) * CHUNK):
                            pack(c, n)
                    elif part < len(face_parts(c)):
                        pack_tail(c)
                    if part < len(face_parts(c)):

                        @when_sent(c)
                        def _(c=c, part=part):
                            face_copy(c, part).start()

        def take_faces(group):
            for c in group:

                @when_received(c)
                def _(c=c):
                    whole_face(c).wait_recv()
                    count = channels[c][2]
                    at = count * LANES
                    remf[c, : count * 8, :] = recvs[c][at : at + count * 8, :].astype(jnp.float32)
                    farf[c] = recvs[c][at + count * 8 : at + count * 8 + full, :].astype(
                        jnp.float32
                    )
                    for n in range(count):
                        to = offsets[c] + n
                        pool[to, :LANES, :LANES] = recvs[c][n * LANES : (n + 1) * LANES, :]
                        below = remf[c, n * 8 : (n + 1) * 8, :]
                        below = jnp.concatenate([below, jnp.zeros_like(below)], axis=0)
                        pool[to, LANES:full, :LANES] = below.astype(pool.dtype)
                        pool[to, :, LANES:width] = farf[
                            c, :, n * rest : (n + 1) * rest
                        ].astype(pool.dtype)

        pl.semaphore_wait(barrier, expected)
        k_copy.wait()
        send_faces([0, 1])

        lists.table(
            tab, agg_ref[...] - device * aggs_here, own_ref[...], me_z // stride_z, me["gx"], sizes
        )
        t_copy = pltpu.make_async_copy(tab, table_ref, t_sem)
        t_copy.start()
        msg_far[...] = jnp.zeros_like(msg_far)
        for sub in range(per_owner):
            for piece, slot in ((5, sub), (6, out_slots - per_owner + sub)):
                rows_ref[slot, piece * LANES : (piece + 1) * LANES, :] = jnp.zeros(
                    (LANES, LANES), rows_ref.dtype
                )
        pool[zero_block] = jnp.zeros(pool.shape[1:], pool.dtype)

        @pl.loop(0, elems // 4)
        def _(group):
            for u in range(4):
                e = group * 4 + u
                pool[e] = block(e)[:, :width].astype(pool.dtype)

        t_copy.wait()
        send_faces([*range(4, nch), 2, 3])

        @pl.loop(0, elems // 8)
        def _(group):
            for u in range(8):
                e = group * 8 + u
                pt[e] = block(e).T[:tall].astype(pt.dtype)

        def lay_out(i):
            k = block_at(i)
            j_copy(i).wait()
            own = (k == 0).astype(jnp.float32)
            spread(
                lambda c: jraw[i % AHEAD, pl.ds(c * step_rows, step_rows)],
                res_ref[...].astype(jnp.float32) * own,
            )

            @pl.when(i + AHEAD < sides)
            def _():
                j_copy(i + AHEAD).start()

            @pl.loop(0, elems // 4)
            def _(group):
                for u in range(4):
                    e = group * 4 + u
                    jm[k, e] = block(e).astype(jm.dtype)

        my_group = me_z // stride_z

        def target_of(r):
            return partner_bits(my_group, r // per_owner) * stride_z

        def slot_of(z, r):
            return z * per_owner + r % per_owner

        def late(piece):
            return int(piece > 4)

        def row_copy(r, piece, count):
            at = pl.ds(piece * LANES, count * LANES)
            slot = slot_of(me_z, r)
            last = piece == sides
            return pltpu.make_async_remote_copy(
                src_ref=msg.at[r, at],
                dst_ref=tail_ref.at[slot] if last else rows_ref.at[slot, at],
                send_sem=r_send.at[r],
                recv_sem=r_recv.at[slot, late(piece)],
                device_id={"gz": target_of(r)},
                device_id_type=MESH,
            )

        def self_copy(r, piece, count):
            at = pl.ds(piece * LANES, count * LANES)
            slot = slot_of(me_z, r)
            return pltpu.make_async_copy(
                msg.at[r, at],
                tail_ref.at[slot] if piece == sides else rows_ref.at[slot, at],
                self_sem.at[r % per_owner, late(piece)],
            )

        def send_row(r, piece, count=1):
            sent = present(piece, me_z)

            @pl.when((target_of(r) != me_z) & sent)
            def _():
                row_copy(r, piece, count).start()

            @pl.when((target_of(r) == me_z) & sent)
            def _():
                self_copy(r, piece, count).start()

        def emit(r, s, value, more=0.0):
            msg[r, s * LANES : (s + 1) * LANES, :] = value[:LANES, :LANES].astype(msg.dtype)
            last = value[LANES:tall] + more
            msg_rem[r, s * 8 : (s + 1) * 8, :] = last[:, :LANES]
            lanes = slice(s * rest, (s + 1) * rest)
            msg_far[r, :LANES, lanes] = value[:LANES, LANES:width]
            msg_far[r, LANES:, lanes] = last[:, LANES:width]

        def present(piece, z):
            if piece == 5:
                return z > 0
            if piece == 6:
                return z < size_z - 1
            return True

        def side_sum(r, d):
            total = None
            for m in range(on_face):
                code = table_ref[nch + 1 + d, r * on_face + m]
                e, n = code % elems, jnp.clip(code // elems, 0, zero_block)
                product = mul(jm[1 + d, e], pool[n]).astype(jnp.bfloat16)
                triple = mul(pt[e], product)
                total = triple if total is None else total + triple
            return total

        def own_slot(r):
            total, below = None, None
            for m in range(members):
                code = table_ref[nch, r * members + m]
                e, code = code % elems, code // elems
                product = mul(jm[0, e], pool[e])
                for axis in range(3):
                    x, code = code % (2 * elems), code // (2 * elems)
                    k = 1 + 2 * axis + x // elems
                    product = product + mul(jm[k, e], pool[x % elems])
                last = product[LANES:tall]
                below = last if below is None else below + last
                triple = mul(pt[e], product.astype(jnp.bfloat16))
                total = triple if total is None else total + triple
            spare = lax.broadcasted_iota(jnp.int32, below.shape, 0) == width - LANES
            emit(r, 0, total, jnp.where(spare, below, 0.0))
            send_row(r, 0)

        def pack_row_tail(r):
            msg_rem[r, sides * 8 : (sides + 1) * 8, :] = msg_far[r, LANES:tall, :]
            msg[r, tail : tail + half, :] = msg_rem[r].astype(msg.dtype)
            right = pltpu.roll(msg_far[r, half:LANES, :], half, 1)
            left = msg_far[r, :half, :]
            folded = jnp.where(lane_ids(left.shape) < half, left, right)
            msg[r, tail + half : msg_rows, :] = folded.astype(msg.dtype)

        def side_slots(rows, wanted):
            todo = [(r, d) for r in rows for d in wanted]
            for (r, d), total in [(at, side_sum(*at)) for at in todo]:
                emit(r, 1 + d, total)
            complete = sides - 2 in wanted
            if complete:
                for r in rows:
                    pack_row_tail(r)
            for r in rows:
                if not complete:
                    send_row(r, 1 + wanted[0], len(wanted))
                    continue
                for piece in (*(1 + d for d in wanted), sides):
                    send_row(r, piece)

        axis_faces = [list(range(4, nch)), [2, 3], [0, 1]]

        for step in range(size_z - 2):
            for way, ahead in enumerate((1, -1)):
                told = (me_z - ahead, me_z + ahead * (1 + step), me_z + ahead * (2 + step))
                inside = [(z >= 0) & (z < size_z) for z in told]

                @pl.when(inside[0] & inside[1])
                def _(way=way, step=step, ahead=ahead):
                    pl.semaphore_signal(
                        relay_sem.at[way, step],
                        inc=1,
                        device_id={"gz": me_z - ahead},
                        device_id_type=MESH,
                    )

                @pl.when(inside[2])
                def _(way=way, step=step):
                    pl.semaphore_wait(relay_sem.at[way, step], 1)

        far_rows = list(range(early))
        pl.loop(0, 2)(lay_out)
        take_faces(axis_faces[0])
        side_slots(far_rows, (0, 1))
        pl.loop(2, sides)(lay_out)
        pl.loop(0, early)(own_slot)
        for axis in (1, 2):
            take_faces(axis_faces[axis])
            side_slots(far_rows, (2 * axis, 2 * axis + 1))

        @pl.loop(early, aggs_here)
        def _(r):
            own_slot(r)
            side_slots([r], (0, 1, 2, 3))
            side_slots([r], (4, 5))

        owner = me_z % stride_z == 0

        def span(group, z):
            start, count = (0, 5) if group == 0 else (5, pieces - 5)
            if group == 1 and z in (0, size_z - 1):
                count -= 1
            return pl.ds(start * LANES, count * LANES)

        def arrive(group):
            for slot in range(out_slots):
                at = span(group, slot // per_owner)
                mine = slot // per_owner == me_z

                @pl.when(mine)
                def _(slot=slot, at=at):
                    pltpu.make_async_copy(
                        msg.at[0, at], msg.at[1, at], self_sem.at[slot % per_owner, group]
                    ).wait()

                @pl.when(jnp.logical_not(mine))
                def _(slot=slot, at=at):
                    pltpu.make_async_remote_copy(
                        src_ref=msg.at[0, at],
                        dst_ref=msg.at[0, at],
                        send_sem=r_send.at[0],
                        recv_sem=r_recv.at[slot, group],
                        device_id={"gz": me_z},
                        device_id_type=MESH,
                    ).wait_recv()

        def unpack():
            for s in range(sides):
                if s in (0, 5):
                    arrive(late(s))
                for slot in range(out_slots):
                    block_of = rows_ref[slot, s * LANES : (s + 1) * LANES, :]
                    scatter(mixed, out_slots, slot, 0, block_of.astype(jnp.float32))
                out_ref[s, :LANES, :, :LANES] = gathered(mixed[...], LANES, out_slots)

        if stride_z == 1:
            unpack()
        else:
            pl.when(owner)(unpack)

            @pl.when(jnp.logical_not(owner))
            def _():
                out_ref[...] = jnp.zeros_like(out_ref)
                tail_ref[...] = jnp.zeros_like(tail_ref)

        for c in range(nch):

            @when_sent(c)
            def _(c=c):
                whole_face(c).wait_send()

        @pl.loop(0, aggs_here)
        def _(r):
            @pl.when(target_of(r) != me_z)
            def _():
                inside = (me_z > 0) & (me_z < size_z - 1)
                for count, at_end in ((pieces, False), (pieces - 1, True)):

                    @pl.when(inside != at_end)
                    def _(count=count):
                        at = pl.ds(0, count * LANES)
                        pltpu.make_async_remote_copy(
                            src_ref=msg.at[r, at],
                            dst_ref=msg.at[r, at],
                            send_sem=r_send.at[r],
                            recv_sem=r_recv.at[0, 0],
                            device_id={"gz": target_of(r)},
                            device_id_type=MESH,
                        ).wait_send()

    bf16, f32 = jnp.bfloat16, jnp.float32
    spread_rows = (width + 1) * pitch
    faces = [pltpu.VMEM((face_rows(count, full), LANES), bf16) for _, _, count, _ in channels]
    table_rows = pl.cdiv(nch + sides, 8) * 8
    scratch = [
        *[pltpu.VMEM(a.shape, a.dtype) for a in (neighbours, agg_map, owners, residual)],
        pltpu.VMEM((8, LANES), jnp.int32),
        pltpu.SMEM((8, LANES), jnp.int32),
        pltpu.VMEM((table_rows, LANES), jnp.int32),
        pltpu.SMEM((table_rows, LANES), jnp.int32),
        pltpu.VMEM((width, elems, width), bf16),
        pltpu.VMEM((AHEAD, width, elems, width), bf16),
        pltpu.VMEM((spread_rows, LANES), f32),
        pltpu.VMEM((spread_rows, LANES), f32),
        pltpu.VMEM((zero_block + 1, full, width), bf16),
        pltpu.VMEM((elems, tall, full), bf16),
        pltpu.VMEM((sides, elems, full, full), bf16),
        *faces,
        *faces,
        pltpu.VMEM((nch, most * 8, LANES), f32),
        pltpu.VMEM((nch, full, LANES), f32),
        pltpu.VMEM((aggs_here, msg_rows, LANES), bf16),
        pltpu.VMEM((aggs_here, (sides + 1) * 8, LANES), f32),
        pltpu.VMEM((aggs_here, tall, LANES), f32),
        pltpu.VMEM((out_slots, tail, LANES), bf16),
        pltpu.VMEM((LANES * out_slots, LANES), f32),
        pltpu.SemaphoreType.DMA((4,)),
        pltpu.SemaphoreType.DMA,
        pltpu.SemaphoreType.DMA,
        pltpu.SemaphoreType.DMA,
        pltpu.SemaphoreType.DMA((AHEAD,)),
        pltpu.SemaphoreType.DMA((nch,)),
        pltpu.SemaphoreType.DMA((nch,)),
        pltpu.SemaphoreType.DMA((aggs_here,)),
        pltpu.SemaphoreType.DMA((out_slots, 2)),
        pltpu.SemaphoreType.DMA((per_owner, 2)),
        pltpu.SemaphoreType.REGULAR((2, size_z - 2)),
    ]
    return pl.pallas_call(
        kernel,
        in_specs=[pl.BlockSpec(memory_space=pl.ANY)] * 6,
        out_specs=[pl.BlockSpec(memory_space=pltpu.VMEM)] * 2,
        out_shape=[
            pltpu.VMEM((sides, width, out_slots, width), bf16),
            pltpu.VMEM((out_slots, LANES, LANES), bf16),
        ],
        scratch_shapes=scratch,
        compiler_params=pltpu.CompilerParams(
            collective_id=0, has_side_effects=True, vmem_limit_bytes=54 << 20
        ),
    )(neighbours, agg_map, owners, prolong, jac, residual)


def scatter(ref, out_slots, slot, start, value):
    count = value.shape[0]
    ref[pl.ds(start * out_slots + slot, count, stride=out_slots), :] = value


def gathered(value, count, out_slots):
    return value.astype(jnp.bfloat16).reshape(count, out_slots, LANES)


def stored(coarse, tails):
    sides, width, out_slots, _ = coarse.shape
    rest = width - LANES
    half = LANES // 2
    tall = pl.cdiv(width + 1, 8) * 8

    def kernel(_, tail_ref, kept, out_hbm, small_hbm, mixed, mixed_rem, restr, small, sems):
        for slot in range(out_slots):
            below = tail_ref[slot, :half].astype(jnp.float32)
            folded = tail_ref[slot, half:].astype(jnp.float32)
            scatter(mixed, out_slots, slot, 0, folded)
            scatter(mixed, out_slots, slot, half, pltpu.roll(folded, half, 1))
            scatter(mixed, out_slots, slot, LANES, below[sides * 8 :])
            for s in range(sides):
                scatter(mixed_rem.at[s], out_slots, slot, 0, below[s * 8 : (s + 1) * 8])
            restr[slot : slot + 1, :LANES] = below[rest : rest + 1]
            at = sides * 8 + rest
            restr[slot : slot + 1, LANES:] = below[at : at + 1, :rest]
        small[...] = restr[:out_slots].astype(small.dtype)
        copies = [pltpu.make_async_copy(small, small_hbm, sems.at[sides])]
        copies[0].start()
        for s in range(sides):
            low = gathered(mixed_rem[s], 8, out_slots)
            kept[s, LANES:, :, :LANES] = low[:rest]
            right = mixed[...]
            if s > 0:
                right = pltpu.roll(right, LANES - s * rest, 1)
            kept[s, :, :, LANES:] = gathered(right, tall, out_slots)[:width, :, :rest]
            copies.append(pltpu.make_async_copy(kept.at[s], out_hbm.at[s], sems.at[s]))
            copies[-1].start()
        for copy in copies:
            copy.wait()

    f32 = jnp.float32
    _, out, small = pl.pallas_call(
        kernel,
        in_specs=[pl.BlockSpec(memory_space=pltpu.VMEM)] * 2,
        out_specs=[pl.BlockSpec(memory_space=pltpu.VMEM)]
        + [pl.BlockSpec(memory_space=pl.ANY)] * 2,
        out_shape=[
            pltpu.VMEM(coarse.shape, coarse.dtype),
            jax.ShapeDtypeStruct(coarse.shape, coarse.dtype),
            jax.ShapeDtypeStruct((out_slots, width), coarse.dtype),
        ],
        input_output_aliases={0: 0},
        scratch_shapes=[
            pltpu.VMEM((tall * out_slots, LANES), f32),
            pltpu.VMEM((sides, 8 * out_slots, LANES), f32),
            pltpu.VMEM((pl.cdiv(out_slots, 8) * 8, width), f32),
            pltpu.VMEM((out_slots, width), coarse.dtype),
            pltpu.SemaphoreType.DMA((sides + 1,)),
        ],
        compiler_params=pltpu.CompilerParams(vmem_limit_bytes=4 << 20),
    )(coarse, tails)
    return out, small


class Lists:
    def __init__(self, nbr, base):
        self.nbr, self.base = nbr, base
        square = (nbr.shape[1],) * 2
        self.down = lax.broadcasted_iota(jnp.int32, square, 0)
        self.along = lax.broadcasted_iota(jnp.int32, square, 1)
        self.eye = flag(self.down == self.along)
        self.before = flag(self.along < self.down)

    def column(self, row):
        return by_row(self.eye * row)

    def row(self, col):
        return by_column(self.eye * col)

    def listed(self, place, value):
        return by_column(flag(place == self.along) * value)

    def side(self, d):
        elems = self.nbr.shape[1]
        local = self.nbr[d : d + 1] - self.base
        away_row = 1 - flag(local >= 0) * flag(local < elems)
        rank = by_row(self.before * away_row)
        place = jnp.where(self.column(away_row) > 0, rank, -1)
        return self.listed(place, self.down[:, :1])

    def table(self, tab, agg, owners, mine, x, sizes):
        write_table(self, tab, agg, owners, mine, x, sizes)


def flag(mask):
    return jnp.where(mask, 1, 0)


def by_row(value):
    return jnp.sum(value, axis=1, keepdims=True)


def by_column(value):
    return jnp.sum(value, axis=0, keepdims=True)


def write_table(lists, tab, agg, owners, mine, x, sizes):
    nbr, base = lists.nbr, lists.base
    column, row, listed = lists.column, lists.row, lists.listed
    size_x, _, size_z = sizes
    elems, aggs_here = nbr.shape[1], owners.shape[1]
    per_owner = aggs_here // GROUPS
    stride_z = size_z // GROUPS
    members = elems // aggs_here
    on_face = members // 2
    channels = channels_of(size_x)
    offsets, zero_block = channel_offsets(channels, elems)
    nch = len(channels)
    along, before = lists.along, lists.before
    ids = lists.down[:, :1]

    def put(at, value):
        tab[at : at + 1, :elems] = value

    a_down = lax.broadcasted_iota(jnp.int32, (aggs_here, aggs_here), 0)
    a_along = lax.broadcasted_iota(jnp.int32, (aggs_here, aggs_here), 1)
    to = owners // stride_z
    crosses = jnp.abs(to // 2 - mine // 2)
    flips = jnp.abs(to % 2 - mine % 2)
    turn = 2 * (1 - crosses) + (1 + flips + crosses * ((mine // 2 + mine % 2) % 2)) % 2
    turn = jnp.broadcast_to(turn, a_down.shape)
    turn = by_row(jnp.where(a_down == a_along, turn, 0))
    if per_owner > 1:
        turn_row = by_column(jnp.where(a_down == a_along, turn, 0))
        equal = flag(turn_row == turn) * flag(a_along < a_down)
        turn = turn * per_owner + by_row(equal)
    a_ids = lax.broadcasted_iota(jnp.int32, (aggs_here, elems), 0)
    order_row = by_column(flag(agg == a_ids) * turn)
    order = column(order_row)
    agg_col = column(agg)
    together = before * flag(order_row == order)
    m_place = order * members + by_row(together)

    if size_x == 2:
        listing = [(3, 2), (2, 3)]
        sources = [4, 4, 2, 3, 0, 1]
    else:
        listing = [(3, 2), (2, 3), (1, 4), (0, 5)]
        sources = [4, 5, 2, 3, 0, 1]
    local_of, same_of = [], []
    for d in range(6):
        nbr_row = nbr[d : d + 1]
        nbr_col = column(nbr_row)
        local_row, local = nbr_row - base, nbr_col - base
        away_row = 1 - flag(local_row >= 0) * flag(local_row < elems)
        here = flag(local >= 0) * flag(local < elems)
        crossing = away_row * flag(nbr_row >= 0)
        position = by_row(crossing * flag(nbr_row < nbr_col))
        index = jnp.where(here > 0, local, position + offsets[sources[d]])
        index = jnp.where(nbr_col >= 0, index, zero_block)
        near_agg = by_row(flag(local == along) * agg)
        same = here * flag(near_agg == agg_col)
        local_of.append(local)
        same_of.append(same)
        s_rank = by_row(together * (1 - row(same)))
        s_place = jnp.where(same > 0, -1, order * on_face + s_rank)
        put(nch + 1 + d, listed(s_place, ids + elems * index))
    for d, c in listing:
        put(c, lists.side(d))
    if size_x == 2:
        put(4, jnp.where(x == 0, lists.side(1), lists.side(0)))
    code = jnp.zeros_like(ids)
    for axis in (2, 1, 0):
        after = same_of[2 * axis + 1] > 0
        inner = jnp.where(after, local_of[2 * axis + 1] + elems, local_of[2 * axis])
        code = code * (2 * elems) + inner
    put(nch, listed(m_place, code * elems + ids))


def body(jacobian, prolong, residual, neighbours, agg_map, owners):
    sizes = tuple(lax.axis_size(a) for a in ("gx", "gy", "gz"))
    coarse, tails = fused_kernel(
        neighbours.T,
        agg_map[None],
        owners[None],
        jnp.transpose(prolong, (1, 0, 2)),
        jnp.transpose(jacobian, (1, 2, 0, 3)),
        residual,
        sizes,
    )
    coarse, restricted = stored(coarse, tails)
    return jnp.transpose(coarse, (2, 0, 1, 3)), restricted


def solution(mesh):
    spec = P(("gx", "gy", "gz"))
    return jax.shard_map(
        body,
        mesh=mesh,
        in_specs=(spec,) * 6,
        out_specs=(spec, spec),
        check_vma=False,
    )
```

```python
import jax
import jax.numpy as jnp
from jax import lax
from jax.experimental import pallas as pl
from jax.experimental.pallas import tpu as pltpu
from jax.sharding import PartitionSpec as P

LX = 4
LY = 4
LZ = 2
GROUPS = 4
LANES = 128
CHUNK = 4
AHEAD = 4
MESH = pl.DeviceIdType.MESH


def mul(a, b):
    return jnp.dot(a, b, preferred_element_type=jnp.float32)


def lane_ids(shape):
    return lax.broadcasted_iota(jnp.int32, shape, 1)


def channels_of(size_x):
    z = [("gz", 1, LX * LY, 5), ("gz", -1, LX * LY, 4)]
    y = [("gy", 1, LX * LZ, 3), ("gy", -1, LX * LZ, 2)]
    if size_x == 2:
        x = [("gx", 0, LY * LZ, None)]
    else:
        x = [("gx", 1, LY * LZ, 1), ("gx", -1, LY * LZ, 0)]
    return z + y + x


def channel_offsets(channels, elems):
    offsets, at = [], elems
    for _, _, count, _ in channels:
        offsets.append(at)
        at += count
    return offsets, at


def face_rows(count, tall):
    return count * LANES + count * 8 + tall


def partner_bits(me, r):
    high, low = me // 2, me % 2
    inner = (high + low) % 2
    cross = 1 - r // 2
    turn = (1 + r + inner * cross) % 2
    high = high + cross * (1 - 2 * high)
    low = low + turn * (1 - 2 * low)
    return high * 2 + low


def fused_kernel(neighbours, agg_map, owners, prolong, jac, residual, sizes):
    width, elems, _ = prolong.shape
    sides = jac.shape[0]
    aggs_here = owners.shape[1]
    size_x, size_y, size_z = sizes
    rest = width - LANES
    tall = pl.cdiv(width + 1, 8) * 8
    full = pl.cdiv(width + 1, 16) * 16
    pitch = elems + 1
    per_owner = aggs_here // GROUPS
    stride_z = size_z // GROUPS
    out_slots = size_z * per_owner
    members = elems // aggs_here
    on_face = members // 2
    channels = channels_of(size_x)
    offsets, zero_block = channel_offsets(channels, elems)
    nch = len(channels)
    tail = sides * LANES
    msg_rows = tail + LANES
    half = LANES // 2
    most = max(count for _, _, count, _ in channels)
    pieces = sides + 1
    early = aggs_here // 2
    step_rows = 5 if width % 5 == 0 else 1

    def kernel(nbr_in, agg_in, own_in, p_hbm, j_hbm, res_in, out_ref, tail_ref, *refs):
        nbr_ref, agg_ref, own_ref, res_ref, picks, picks_ref = refs[:6]
        refs = refs[6:]
        tab, table_ref, praw, jraw, near, far, pool, pt, jm = refs[:9]
        sends, recvs = refs[9 : 9 + nch], refs[9 + nch : 9 + 2 * nch]
        refs = refs[9 + 2 * nch :]
        remf, farf, msg, msg_rem, msg_far = refs[:5]
        rows_ref, mixed = refs[5:7]
        in_sem, k_sem, t_sem, p_sem, j_sem, f_send, f_recv, r_send, r_recv, self_sem, relay_sem = refs[7:]
        me = {"gx": lax.axis_index("gx"), "gy": lax.axis_index("gy"), "gz": lax.axis_index("gz")}
        size = {"gx": size_x, "gy": size_y, "gz": size_z}
        me_z = me["gz"]

        p_copy = pltpu.make_async_copy(p_hbm, praw, p_sem)
        p_copy.start()
        small = [
            pltpu.make_async_copy(source, ref, in_sem.at[i])
            for i, (source, ref) in enumerate(
                zip((nbr_in, agg_in, own_in, res_in), (nbr_ref, agg_ref, own_ref, res_ref))
            )
        ]
        for copy in small:
            copy.start()

        def block_at(i):
            return (i + 1) * (i < 2) + i * (i > 2)

        def j_copy(i):
            slot = i % AHEAD
            return pltpu.make_async_copy(
                j_hbm.at[block_at(i)], jraw.at[slot], j_sem.at[slot]
            )

        barrier = pltpu.get_barrier_semaphore()
        expected = 0
        if size_x == 2:
            pl.semaphore_signal(
                barrier, inc=1, device_id={"gx": 1 - me["gx"]}, device_id_type=MESH
            )
            expected = expected + 1
        for axis in ["gz", "gy"] + (["gx"] if size_x > 2 else []):
            for step in (1, -1):
                there = me[axis] + step
                exists = (there >= 0) & (there < size[axis])

                @pl.when(exists)
                def _(axis=axis, there=there):
                    pl.semaphore_signal(
                        barrier, inc=1, device_id={axis: there}, device_id_type=MESH
                    )

                expected = expected + exists.astype(jnp.int32)

        def spread(load, last):
            @pl.loop(0, width // step_rows)
            def _(c):
                part = load(c).astype(jnp.float32)
                for i in range(step_rows):
                    rows = pl.ds((c * step_rows + i) * pitch, elems)
                    near[rows, :] = part[i, :, :LANES]
                    far[rows, :rest] = part[i, :, LANES:]

            near[pl.ds(width * pitch, elems), :] = last[:, :LANES]
            far[pl.ds(width * pitch, elems), :rest] = last[:, LANES:]

        def block(e):
            rows = pl.ds(e, width + 1, stride=pitch)
            right = far[rows, :]
            right = jnp.where(lane_ids(right.shape) < rest, right, 0.0)
            both = jnp.concatenate([near[rows, :], right], axis=1)[:, :full]
            below = jnp.zeros((full - width - 1, full), jnp.float32)
            return jnp.concatenate([both, below], axis=0)

        device = (me["gx"] * size_y + me["gy"]) * size_z + me_z
        for copy in small:
            copy.wait()
        lists = Lists(nbr_ref[...], device * elems)
        for c in range(2):
            picks[c : c + 1, :elems] = lists.side(channels[c][3])
        k_copy = pltpu.make_async_copy(picks, picks_ref, k_sem)
        k_copy.start()
        for c in range(2):
            farf[c, tall:, :] = jnp.zeros((full - tall, LANES), jnp.float32)
        p_copy.wait()
        for k in range(AHEAD):
            j_copy(k).start()
        spread(
            lambda c: praw[pl.ds(c * step_rows, step_rows)],
            jnp.zeros((elems, width), jnp.float32),
        )

        def face_target(c):
            axis, step, _, _ = channels[c]
            return {axis: 1 - me[axis] if step == 0 else me[axis] + step}

        def when_sent(c):
            axis, step, _, _ = channels[c]
            if step == 0:
                return lambda f: f()
            there = me[axis] + step
            return pl.when((there >= 0) & (there < size[axis]))

        def when_received(c):
            axis, step, _, _ = channels[c]
            if step == 0:
                return lambda f: f()
            there = me[axis] - step
            return pl.when((there >= 0) & (there < size[axis]))

        def chunk_of(c):
            return CHUNK if c < 2 else channels[c][2]

        def face_parts(c):
            count = channels[c][2]
            step = chunk_of(c)
            parts = [(n * LANES, step * LANES) for n in range(0, count, step)]
            return parts + [(count * LANES, count * 8 + full)]

        def face_copy(c, part):
            start, rows = face_parts(c)[part]
            return pltpu.make_async_remote_copy(
                src_ref=sends[c].at[pl.ds(start, rows)],
                dst_ref=recvs[c].at[pl.ds(start, rows)],
                send_sem=f_send.at[c],
                recv_sem=f_recv.at[c],
                device_id=face_target(c),
                device_id_type=MESH,
            )

        def whole_face(c):
            return pltpu.make_async_remote_copy(
                src_ref=sends[c],
                dst_ref=recvs[c],
                send_sem=f_send.at[c],
                recv_sem=f_recv.at[c],
                device_id=face_target(c),
                device_id_type=MESH,
            )

        def pack(c, n):
            if c < 2:
                rows = pl.ds(picks_ref[c, n] % elems, width + 1, stride=pitch)
                left, right = near[rows, :], far[rows, :]
                sends[c][n * LANES : (n + 1) * LANES, :] = left[:LANES].astype(jnp.bfloat16)
                remf[c, n * 8 : (n + 1) * 8, :] = left[LANES:tall]
                farf[c, :tall, n * rest : (n + 1) * rest] = right[:, :rest]
                return
            whole = pool[table_ref[c, n] % elems]
            sends[c][n * LANES : (n + 1) * LANES, :] = whole[:LANES, :LANES]
            remf[c, n * 8 : (n + 1) * 8, :] = whole[LANES:tall, :LANES].astype(jnp.float32)
            farf[c, :, n * rest : (n + 1) * rest] = whole[:, LANES:width].astype(jnp.float32)

        def pack_tail(c):
            count = channels[c][2]
            at = count * LANES
            sends[c][at : at + count * 8, :] = remf[c, : count * 8, :].astype(jnp.bfloat16)
            sends[c][at + count * 8 : at + count * 8 + full, :] = farf[c].astype(jnp.bfloat16)

        def send_faces(group):
            for part in range(max(len(face_parts(c)) for c in group)):
                for c in group:
                    if part < len(face_parts(c)) - 1:
                        for n in range(part * chunk_of(c), (part + 1) * chunk_of(c)):
                            pack(c, n)
                    elif part < len(face_parts(c)):
                        pack_tail(c)
                    if part < len(face_parts(c)):

                        @when_sent(c)
                        def _(c=c, part=part):
                            face_copy(c, part).start()

        def take_faces(group):
            for c in group:

                @when_received(c)
                def _(c=c):
                    whole_face(c).wait_recv()
                    count = channels[c][2]
                    at = count * LANES
                    remf[c, : count * 8, :] = recvs[c][at : at + count * 8, :].astype(jnp.float32)
                    farf[c] = recvs[c][at + count * 8 : at + count * 8 + full, :].astype(
                        jnp.float32
                    )
                    for n in range(count):
                        to = offsets[c] + n
                        pool[to, :LANES, :LANES] = recvs[c][n * LANES : (n + 1) * LANES, :]
                        below = remf[c, n * 8 : (n + 1) * 8, :]
                        below = jnp.concatenate([below, jnp.zeros_like(below)], axis=0)
                        pool[to, LANES:full, :LANES] = below.astype(pool.dtype)
                        pool[to, :, LANES:width] = farf[
                            c, :, n * rest : (n + 1) * rest
                        ].astype(pool.dtype)

        pl.semaphore_wait(barrier, expected)
        k_copy.wait()
        send_faces([0, 1])

        lists.table(
            tab, agg_ref[...] - device * aggs_here, own_ref[...], me_z // stride_z, me["gx"], sizes
        )
        t_copy = pltpu.make_async_copy(tab, table_ref, t_sem)
        t_copy.start()
        msg_far[...] = jnp.zeros_like(msg_far)
        for sub in range(per_owner):
            for piece, slot in ((5, sub), (6, out_slots - per_owner + sub)):
                rows_ref[slot, piece * LANES : (piece + 1) * LANES, :] = jnp.zeros(
                    (LANES, LANES), rows_ref.dtype
                )
        pool[zero_block] = jnp.zeros(pool.shape[1:], pool.dtype)

        @pl.loop(0, elems // 4)
        def _(group):
            for u in range(4):
                e = group * 4 + u
                pool[e] = block(e)[:, :width].astype(pool.dtype)

        t_copy.wait()
        send_faces([*range(4, nch), 2, 3])

        @pl.loop(0, elems // 8)
        def _(group):
            for u in range(8):
                e = group * 8 + u
                pt[e] = block(e).T[:tall].astype(pt.dtype)

        def lay_out(i):
            k = block_at(i)
            j_copy(i).wait()
            own = (k == 0).astype(jnp.float32)
            spread(
                lambda c: jraw[i % AHEAD, pl.ds(c * step_rows, step_rows)],
                res_ref[...].astype(jnp.float32) * own,
            )

            @pl.when(i + AHEAD < sides)
            def _():
                j_copy(i + AHEAD).start()

            @pl.loop(0, elems // 4)
            def _(group):
                for u in range(4):
                    e = group * 4 + u
                    jm[k, e] = block(e).astype(jm.dtype)

        my_group = me_z // stride_z

        def target_of(r):
            return partner_bits(my_group, r // per_owner) * stride_z

        def slot_of(z, r):
            return z * per_owner + r % per_owner

        def late(piece):
            return int(piece > 4)

        def row_copy(r, piece, count):
            at = pl.ds(piece * LANES, count * LANES)
            slot = slot_of(me_z, r)
            last = piece == sides
            return pltpu.make_async_remote_copy(
                src_ref=msg.at[r, at],
                dst_ref=tail_ref.at[slot] if last else rows_ref.at[slot, at],
                send_sem=r_send.at[r],
                recv_sem=r_recv.at[slot, late(piece)],
                device_id={"gz": target_of(r)},
                device_id_type=MESH,
            )

        def self_copy(r, piece, count):
            at = pl.ds(piece * LANES, count * LANES)
            slot = slot_of(me_z, r)
            return pltpu.make_async_copy(
                msg.at[r, at],
                tail_ref.at[slot] if piece == sides else rows_ref.at[slot, at],
                self_sem.at[r % per_owner, late(piece)],
            )

        def send_row(r, piece, count=1):
            sent = present(piece, me_z)

            @pl.when((target_of(r) != me_z) & sent)
            def _():
                row_copy(r, piece, count).start()

            @pl.when((target_of(r) == me_z) & sent)
            def _():
                self_copy(r, piece, count).start()

        def emit(r, s, value, more=0.0):
            msg[r, s * LANES : (s + 1) * LANES, :] = value[:LANES, :LANES].astype(msg.dtype)
            last = value[LANES:tall] + more
            msg_rem[r, s * 8 : (s + 1) * 8, :] = last[:, :LANES]
            lanes = slice(s * rest, (s + 1) * rest)
            msg_far[r, :LANES, lanes] = value[:LANES, LANES:width]
            msg_far[r, LANES:, lanes] = last[:, LANES:width]

        def present(piece, z):
            if piece == 5:
                return z > 0
            if piece == 6:
                return z < size_z - 1
            return True

        def side_sum(r, d):
            total = None
            for m in range(on_face):
                code = table_ref[nch + 1 + d, r * on_face + m]
                e, n = code % elems, jnp.clip(code // elems, 0, zero_block)
                product = mul(jm[1 + d, e], pool[n]).astype(jnp.bfloat16)
                triple = mul(pt[e], product)
                total = triple if total is None else total + triple
            return total

        def own_slot(r):
            total, below = None, None
            for m in range(members):
                code = table_ref[nch, r * members + m]
                e, code = code % elems, code // elems
                product = mul(jm[0, e], pool[e])
                for axis in range(3):
                    x, code = code % (2 * elems), code // (2 * elems)
                    k = 1 + 2 * axis + x // elems
                    product = product + mul(jm[k, e], pool[x % elems])
                last = product[LANES:tall]
                below = last if below is None else below + last
                triple = mul(pt[e], product.astype(jnp.bfloat16))
                total = triple if total is None else total + triple
            spare = lax.broadcasted_iota(jnp.int32, below.shape, 0) == width - LANES
            emit(r, 0, total, jnp.where(spare, below, 0.0))
            send_row(r, 0)

        def pack_row_tail(r):
            msg_rem[r, sides * 8 : (sides + 1) * 8, :] = msg_far[r, LANES:tall, :]
            msg[r, tail : tail + half, :] = msg_rem[r].astype(msg.dtype)
            right = pltpu.roll(msg_far[r, half:LANES, :], half, 1)
            left = msg_far[r, :half, :]
            folded = jnp.where(lane_ids(left.shape) < half, left, right)
            msg[r, tail + half : msg_rows, :] = folded.astype(msg.dtype)

        def side_slots(rows, wanted):
            todo = [(r, d) for r in rows for d in wanted]
            for (r, d), total in [(at, side_sum(*at)) for at in todo]:
                emit(r, 1 + d, total)
            complete = sides - 2 in wanted
            if complete:
                for r in rows:
                    pack_row_tail(r)
            for r in rows:
                if not complete:
                    send_row(r, 1 + wanted[0], len(wanted))
                    continue
                for piece in (*(1 + d for d in wanted), sides):
                    send_row(r, piece)

        axis_faces = [list(range(4, nch)), [2, 3], [0, 1]]

        for step in range(size_z - 2):
            for way, ahead in enumerate((1, -1)):
                told = (me_z - ahead, me_z + ahead * (1 + step), me_z + ahead * (2 + step))
                inside = [(z >= 0) & (z < size_z) for z in told]

                @pl.when(inside[0] & inside[1])
                def _(way=way, step=step, ahead=ahead):
                    pl.semaphore_signal(
                        relay_sem.at[way, step],
                        inc=1,
                        device_id={"gz": me_z - ahead},
                        device_id_type=MESH,
                    )

                @pl.when(inside[2])
                def _(way=way, step=step):
                    pl.semaphore_wait(relay_sem.at[way, step], 1)

        far_rows = list(range(early))
        pl.loop(0, 2)(lay_out)
        take_faces(axis_faces[0])
        side_slots(far_rows, (0, 1))
        pl.loop(2, sides)(lay_out)
        pl.loop(0, early)(own_slot)
        for axis in (1, 2):
            take_faces(axis_faces[axis])
            side_slots(far_rows, (2 * axis, 2 * axis + 1))

        @pl.loop(early, aggs_here)
        def _(r):
            own_slot(r)
            side_slots([r], (0, 1, 2, 3))
            side_slots([r], (4, 5))

        owner = me_z % stride_z == 0

        def span(group, z):
            start, count = (0, 5) if group == 0 else (5, pieces - 5)
            if group == 1 and z in (0, size_z - 1):
                count -= 1
            return pl.ds(start * LANES, count * LANES)

        def arrive(group):
            for slot in range(out_slots):
                at = span(group, slot // per_owner)
                mine = slot // per_owner == me_z

                @pl.when(mine)
                def _(slot=slot, at=at):
                    pltpu.make_async_copy(
                        msg.at[0, at], msg.at[1, at], self_sem.at[slot % per_owner, group]
                    ).wait()

                @pl.when(jnp.logical_not(mine))
                def _(slot=slot, at=at):
                    pltpu.make_async_remote_copy(
                        src_ref=msg.at[0, at],
                        dst_ref=msg.at[0, at],
                        send_sem=r_send.at[0],
                        recv_sem=r_recv.at[slot, group],
                        device_id={"gz": me_z},
                        device_id_type=MESH,
                    ).wait_recv()

        def unpack():
            for s in range(sides):
                if s in (0, 5):
                    arrive(late(s))
                for slot in range(out_slots):
                    block_of = rows_ref[slot, s * LANES : (s + 1) * LANES, :]
                    scatter(mixed, out_slots, slot, 0, block_of.astype(jnp.float32))
                out_ref[s, :LANES, :, :LANES] = gathered(mixed[...], LANES, out_slots)

        if stride_z == 1:
            unpack()
        else:
            pl.when(owner)(unpack)

            @pl.when(jnp.logical_not(owner))
            def _():
                out_ref[...] = jnp.zeros_like(out_ref)
                tail_ref[...] = jnp.zeros_like(tail_ref)

        for c in range(nch):

            @when_sent(c)
            def _(c=c):
                whole_face(c).wait_send()

        @pl.loop(0, aggs_here)
        def _(r):
            @pl.when(target_of(r) != me_z)
            def _():
                inside = (me_z > 0) & (me_z < size_z - 1)
                for count, at_end in ((pieces, False), (pieces - 1, True)):

                    @pl.when(inside != at_end)
                    def _(count=count):
                        at = pl.ds(0, count * LANES)
                        pltpu.make_async_remote_copy(
                            src_ref=msg.at[r, at],
                            dst_ref=msg.at[r, at],
                            send_sem=r_send.at[r],
                            recv_sem=r_recv.at[0, 0],
                            device_id={"gz": target_of(r)},
                            device_id_type=MESH,
                        ).wait_send()

    bf16, f32 = jnp.bfloat16, jnp.float32
    spread_rows = (width + 1) * pitch
    faces = [pltpu.VMEM((face_rows(count, full), LANES), bf16) for _, _, count, _ in channels]
    table_rows = pl.cdiv(nch + sides, 8) * 8
    scratch = [
        *[pltpu.VMEM(a.shape, a.dtype) for a in (neighbours, agg_map, owners, residual)],
        pltpu.VMEM((8, LANES), jnp.int32),
        pltpu.SMEM((8, LANES), jnp.int32),
        pltpu.VMEM((table_rows, LANES), jnp.int32),
        pltpu.SMEM((table_rows, LANES), jnp.int32),
        pltpu.VMEM((width, elems, width), bf16),
        pltpu.VMEM((AHEAD, width, elems, width), bf16),
        pltpu.VMEM((spread_rows, LANES), f32),
        pltpu.VMEM((spread_rows, LANES), f32),
        pltpu.VMEM((zero_block + 1, full, width), bf16),
        pltpu.VMEM((elems, tall, full), bf16),
        pltpu.VMEM((sides, elems, full, full), bf16),
        *faces,
        *faces,
        pltpu.VMEM((nch, most * 8, LANES), f32),
        pltpu.VMEM((nch, full, LANES), f32),
        pltpu.VMEM((aggs_here, msg_rows, LANES), bf16),
        pltpu.VMEM((aggs_here, (sides + 1) * 8, LANES), f32),
        pltpu.VMEM((aggs_here, tall, LANES), f32),
        pltpu.VMEM((out_slots, tail, LANES), bf16),
        pltpu.VMEM((LANES * out_slots, LANES), f32),
        pltpu.SemaphoreType.DMA((4,)),
        pltpu.SemaphoreType.DMA,
        pltpu.SemaphoreType.DMA,
        pltpu.SemaphoreType.DMA,
        pltpu.SemaphoreType.DMA((AHEAD,)),
        pltpu.SemaphoreType.DMA((nch,)),
        pltpu.SemaphoreType.DMA((nch,)),
        pltpu.SemaphoreType.DMA((aggs_here,)),
        pltpu.SemaphoreType.DMA((out_slots, 2)),
        pltpu.SemaphoreType.DMA((per_owner, 2)),
        pltpu.SemaphoreType.REGULAR((2, size_z - 2)),
    ]
    return pl.pallas_call(
        kernel,
        in_specs=[pl.BlockSpec(memory_space=pl.ANY)] * 6,
        out_specs=[pl.BlockSpec(memory_space=pltpu.VMEM)] * 2,
        out_shape=[
            pltpu.VMEM((sides, width, out_slots, width), bf16),
            pltpu.VMEM((out_slots, LANES, LANES), bf16),
        ],
        scratch_shapes=scratch,
        compiler_params=pltpu.CompilerParams(
            collective_id=0, has_side_effects=True, vmem_limit_bytes=54 << 20
        ),
    )(neighbours, agg_map, owners, prolong, jac, residual)


def scatter(ref, out_slots, slot, start, value):
    count = value.shape[0]
    ref[pl.ds(start * out_slots + slot, count, stride=out_slots), :] = value


def gathered(value, count, out_slots):
    return value.astype(jnp.bfloat16).reshape(count, out_slots, LANES)


def stored(coarse, tails):
    sides, width, out_slots, _ = coarse.shape
    rest = width - LANES
    half = LANES // 2
    tall = pl.cdiv(width + 1, 8) * 8

    def kernel(_, tail_ref, kept, out_hbm, small_hbm, mixed, mixed_rem, restr, small, sems):
        for slot in range(out_slots):
            below = tail_ref[slot, :half].astype(jnp.float32)
            folded = tail_ref[slot, half:].astype(jnp.float32)
            scatter(mixed, out_slots, slot, 0, folded)
            scatter(mixed, out_slots, slot, half, pltpu.roll(folded, half, 1))
            scatter(mixed, out_slots, slot, LANES, below[sides * 8 :])
            for s in range(sides):
                scatter(mixed_rem.at[s], out_slots, slot, 0, below[s * 8 : (s + 1) * 8])
            restr[slot : slot + 1, :LANES] = below[rest : rest + 1]
            at = sides * 8 + rest
            restr[slot : slot + 1, LANES:] = below[at : at + 1, :rest]
        small[...] = restr[:out_slots].astype(small.dtype)
        copies = [pltpu.make_async_copy(small, small_hbm, sems.at[sides])]
        copies[0].start()
        for s in range(sides):
            low = gathered(mixed_rem[s], 8, out_slots)
            kept[s, LANES:, :, :LANES] = low[:rest]
            right = mixed[...]
            if s > 0:
                right = pltpu.roll(right, LANES - s * rest, 1)
            kept[s, :, :, LANES:] = gathered(right, tall, out_slots)[:width, :, :rest]
            copies.append(pltpu.make_async_copy(kept.at[s], out_hbm.at[s], sems.at[s]))
            copies[-1].start()
        for copy in copies:
            copy.wait()

    f32 = jnp.float32
    _, out, small = pl.pallas_call(
        kernel,
        in_specs=[pl.BlockSpec(memory_space=pltpu.VMEM)] * 2,
        out_specs=[pl.BlockSpec(memory_space=pltpu.VMEM)]
        + [pl.BlockSpec(memory_space=pl.ANY)] * 2,
        out_shape=[
            pltpu.VMEM(coarse.shape, coarse.dtype),
            jax.ShapeDtypeStruct(coarse.shape, coarse.dtype),
            jax.ShapeDtypeStruct((out_slots, width), coarse.dtype),
        ],
        input_output_aliases={0: 0},
        scratch_shapes=[
            pltpu.VMEM((tall * out_slots, LANES), f32),
            pltpu.VMEM((sides, 8 * out_slots, LANES), f32),
            pltpu.VMEM((pl.cdiv(out_slots, 8) * 8, width), f32),
            pltpu.VMEM((out_slots, width), coarse.dtype),
            pltpu.SemaphoreType.DMA((sides + 1,)),
        ],
        compiler_params=pltpu.CompilerParams(vmem_limit_bytes=4 << 20),
    )(coarse, tails)
    return out, small


class Lists:
    def __init__(self, nbr, base):
        self.nbr, self.base = nbr, base
        square = (nbr.shape[1],) * 2
        self.down = lax.broadcasted_iota(jnp.int32, square, 0)
        self.along = lax.broadcasted_iota(jnp.int32, square, 1)
        self.eye = flag(self.down == self.along)
        self.before = flag(self.along < self.down)

    def column(self, row):
        return by_row(self.eye * row)

    def row(self, col):
        return by_column(self.eye * col)

    def listed(self, place, value):
        return by_column(flag(place == self.along) * value)

    def side(self, d):
        elems = self.nbr.shape[1]
        local = self.nbr[d : d + 1] - self.base
        away_row = 1 - flag(local >= 0) * flag(local < elems)
        rank = by_row(self.before * away_row)
        place = jnp.where(self.column(away_row) > 0, rank, -1)
        return self.listed(place, self.down[:, :1])

    def table(self, tab, agg, owners, mine, x, sizes):
        write_table(self, tab, agg, owners, mine, x, sizes)


def flag(mask):
    return jnp.where(mask, 1, 0)


def by_row(value):
    return jnp.sum(value, axis=1, keepdims=True)


def by_column(value):
    return jnp.sum(value, axis=0, keepdims=True)


def write_table(lists, tab, agg, owners, mine, x, sizes):
    nbr, base = lists.nbr, lists.base
    column, row, listed = lists.column, lists.row, lists.listed
    size_x, _, size_z = sizes
    elems, aggs_here = nbr.shape[1], owners.shape[1]
    per_owner = aggs_here // GROUPS
    stride_z = size_z // GROUPS
    members = elems // aggs_here
    on_face = members // 2
    channels = channels_of(size_x)
    offsets, zero_block = channel_offsets(channels, elems)
    nch = len(channels)
    along, before = lists.along, lists.before
    ids = lists.down[:, :1]

    def put(at, value):
        tab[at : at + 1, :elems] = value

    a_down = lax.broadcasted_iota(jnp.int32, (aggs_here, aggs_here), 0)
    a_along = lax.broadcasted_iota(jnp.int32, (aggs_here, aggs_here), 1)
    to = owners // stride_z
    crosses = jnp.abs(to // 2 - mine // 2)
    flips = jnp.abs(to % 2 - mine % 2)
    turn = 2 * (1 - crosses) + (1 + flips + crosses * ((mine // 2 + mine % 2) % 2)) % 2
    turn = jnp.broadcast_to(turn, a_down.shape)
    turn = by_row(jnp.where(a_down == a_along, turn, 0))
    if per_owner > 1:
        turn_row = by_column(jnp.where(a_down == a_along, turn, 0))
        equal = flag(turn_row == turn) * flag(a_along < a_down)
        turn = turn * per_owner + by_row(equal)
    a_ids = lax.broadcasted_iota(jnp.int32, (aggs_here, elems), 0)
    order_row = by_column(flag(agg == a_ids) * turn)
    order = column(order_row)
    agg_col = column(agg)
    together = before * flag(order_row == order)
    m_place = order * members + by_row(together)

    if size_x == 2:
        listing = [(3, 2), (2, 3)]
        sources = [4, 4, 2, 3, 0, 1]
    else:
        listing = [(3, 2), (2, 3), (1, 4), (0, 5)]
        sources = [4, 5, 2, 3, 0, 1]
    local_of, same_of = [], []
    for d in range(6):
        nbr_row = nbr[d : d + 1]
        nbr_col = column(nbr_row)
        local_row, local = nbr_row - base, nbr_col - base
        away_row = 1 - flag(local_row >= 0) * flag(local_row < elems)
        here = flag(local >= 0) * flag(local < elems)
        crossing = away_row * flag(nbr_row >= 0)
        position = by_row(crossing * flag(nbr_row < nbr_col))
        index = jnp.where(here > 0, local, position + offsets[sources[d]])
        index = jnp.where(nbr_col >= 0, index, zero_block)
        near_agg = by_row(flag(local == along) * agg)
        same = here * flag(near_agg == agg_col)
        local_of.append(local)
        same_of.append(same)
        s_rank = by_row(together * (1 - row(same)))
        s_place = jnp.where(same > 0, -1, order * on_face + s_rank)
        put(nch + 1 + d, listed(s_place, ids + elems * index))
    for d, c in listing:
        put(c, lists.side(d))
    if size_x == 2:
        put(4, jnp.where(x == 0, lists.side(1), lists.side(0)))
    code = jnp.zeros_like(ids)
    for axis in (2, 1, 0):
        after = same_of[2 * axis + 1] > 0
        inner = jnp.where(after, local_of[2 * axis + 1] + elems, local_of[2 * axis])
        code = code * (2 * elems) + inner
    put(nch, listed(m_place, code * elems + ids))


def body(jacobian, prolong, residual, neighbours, agg_map, owners):
    sizes = tuple(lax.axis_size(a) for a in ("gx", "gy", "gz"))
    coarse, tails = fused_kernel(
        neighbours.T,
        agg_map[None],
        owners[None],
        jnp.transpose(prolong, (1, 0, 2)),
        jnp.transpose(jacobian, (1, 2, 0, 3)),
        residual,
        sizes,
    )
    coarse, restricted = stored(coarse, tails)
    return jnp.transpose(coarse, (2, 0, 1, 3)), restricted


def solution(mesh):
    spec = P(("gx", "gy", "gz"))
    return jax.shard_map(
        body,
        mesh=mesh,
        in_specs=(spec,) * 6,
        out_specs=(spec, spec),
        check_vma=False,
    )
```
